32 devices in a mesh: section: 4 (over x, core), dp: 8 (over z, y).
Axes of the slice: x: 2, y: 2, z: 4, core: 2. Of those that a mesh axis runs over, the one named last changes fastest.
Arguments:
- images: bfloat16 [16, 256, 768], P('dp'), may hold values from -6 to 6
- cotangent: bfloat16 [16, 256, 768], P('dp'), may hold values from -6 to 6
- kept_count: int32 [16], P('dp'), may hold values from 1 to 256, as said below
- kept_index: int32 [16, 256], P('dp'), may hold values from 0 to 255, as said below
- gain_one: bfloat16 [4, 768], P('section', 'dp'), may hold values from 0.5 to 1.5
- shift_one: bfloat16 [4, 768], P('section', 'dp'), may hold values from -1.5 to 1.5
- qkv_matrix: bfloat16 [4, 768, 2304], P('section', 'dp'), may hold values from -0.21875 to 0.21875
- qkv_shift: bfloat16 [4, 2304], P('section', 'dp'), may hold values from -1.5 to 1.5
- proj_matrix: bfloat16 [4, 768, 768], P('section', 'dp'), may hold values from -0.625 to 0.625
- proj_shift: bfloat16 [4, 768], P('section', 'dp'), may hold values from -1.5 to 1.5
- gain_two: bfloat16 [4, 768], P('section', 'dp'), may hold values from 0.5 to 1.5
- shift_two: bfloat16 [4, 768], P('section', 'dp'), may hold values from -1.5 to 1.5
- up_matrix: bfloat16 [4, 768, 3072], P('section', 'dp'), may hold values from -0.21875 to 0.21875
- up_shift: bfloat16 [4, 3072], P('section', 'dp'), may hold values from -1.5 to 1.5
- down_matrix: bfloat16 [4, 3072, 768], P('section', 'dp'), may hold values from -0.109375 to 0.109375
- down_shift: bfloat16 [4, 768], P('section', 'dp'), may hold values from -1.5 to 1.5
- frequency: bfloat16 [4, 768], P('section', 'dp'), may hold values from 0.049804688 to 1
Outputs:
- section_outputs: float32 [4, 16, 256, 768], P('section', 'dp')
- section_input_grads: float32 [4, 16, 256, 768], P('section', 'dp')
- gain_one_grad: float32 [4, 768], P('section', 'dp')
- shift_one_grad: float32 [4, 768], P('section', 'dp')
- qkv_matrix_grad: float32 [4, 768, 2304], P('section', 'dp')
- qkv_shift_grad: float32 [4, 2304], P('section', 'dp')
- proj_matrix_grad: float32 [4, 768, 768], P('section', 'dp')
- proj_shift_grad: float32 [4, 768], P('section', 'dp')
- gain_two_grad: float32 [4, 768], P('section', 'dp')
- shift_two_grad: float32 [4, 768], P('section', 'dp')
- up_matrix_grad: float32 [4, 768, 3072], P('section', 'dp')
- up_shift_grad: float32 [4, 3072], P('section', 'dp')
- down_matrix_grad: float32 [4, 3072, 768], P('section', 'dp')
- down_shift_grad: float32 [4, 768], P('section', 'dp')
- frequency_grad: float32 [4, 768], P('section', 'dp')
The draws below stay inside these ranges and needn't reach their ends.
Inputs may be any that keep to these rules, and one draw needn't show every extreme that they name: `kept_count`: every image keeps at least one patch, and some image keeps all 256. `kept_index`: each row is a permutation of the 256 grid indices: slots below the image's kept_count hold its kept patches in rising order, the later slots the dropped ones in rising order.
All inputs are finite; a program needn't handle non-finite values.
Results may differ from the reference program's by a relative error of at most 0.025.
Values may be sent and summed in bfloat16 or wider, within the bound.
A program may use at most 256 MiB of HBM per device.

```python
import math
import jax
import jax.numpy as jnp
from jax import lax

D = 768
H = 12
HD = 64
FF = 3072
GRID = 16
P_SIZE = 256
IMAGES = 16
N_SECTION = 4
N_DP = 8


def kept_counts(key):
    base_key = jax.random.fold_in(key, 11)
    patches = GRID * GRID
    divisor = jax.random.randint(base_key, (IMAGES,), 1, 9)
    counts = patches // divisor
    full_image = jax.random.randint(jax.random.fold_in(base_key, 1), (), 0, IMAGES)
    return jnp.where(jnp.arange(IMAGES) == full_image, patches, counts).astype(jnp.int32)


def draw_kept_count(key, part):
    return kept_counts(key)


def draw_kept_index(key, part):
    counts = kept_counts(key)
    patches = GRID * GRID
    random_keys = jax.random.randint(jax.random.fold_in(key, 23), (IMAGES, patches), 0, 1 << 20)
    distinct = random_keys * patches + jnp.arange(patches)[None, :]
    order = jnp.argsort(distinct, axis=1)
    ranking = jnp.argsort(order, axis=1)
    chosen = ranking < counts[:, None]
    sort_keys = jnp.where(chosen, 0, patches) + jnp.arange(patches)[None, :]
    return jnp.argsort(sort_keys, axis=1).astype(jnp.int32)


def with_spikes(drawn, own_key, source, target, parts, factor):
    owner, partner = [(jnp.arange(drawn.shape[axis_at]) // (drawn.shape[axis_at] // parts)).reshape([-1 if axis == axis_at else 1 for axis in range(drawn.ndim)]) for axis_at in (source, target)]
    chosen = jax.random.permutation(own_key, parts)[partner]
    strong = (owner == chosen) | (owner == (partner + parts // 2) % parts)
    return jnp.where(strong, factor * drawn, drawn)


def block_levels(own_key, extent, pieces, low, top_value):
    gain, own = 1.0, jax.random.fold_in(own_key, 6)
    for position, blocks in pieces:
        steps = jnp.exp(jax.random.uniform(jax.random.fold_in(own, position), (blocks,), jnp.float32, low / len(pieces), top_value / len(pieces)))
        gain = gain * jnp.repeat(steps, extent[position] // blocks).reshape([-1 if axis == position else 1 for axis in range(len(extent))])
    return gain


def normal_values(own_key, dims, spread, most, cuts=(), dtype=jnp.bfloat16):
    values = jax.random.normal(own_key, dims, jnp.float32) * spread
    if len(cuts) > 0:
        values = block_levels(own_key, dims, cuts, -0.22, 0.18) * values
    return jnp.clip(values, min=-most, max=most).astype(dtype)


def heavy_noise(rng, dims, width, most, split, heavy, dtype=jnp.bfloat16):
    array = width * jax.random.normal(rng, dims, jnp.float32)
    if split:
        array = array * block_levels(rng, dims, split, -0.22, 0.18)
    return jnp.clip(with_spikes(array, jax.random.fold_in(rng, 3), *heavy), -most, most).astype(dtype)


def setup_inputs(seed: int = 0) -> dict:
    key_list = jax.random.split(jax.random.key(seed), 18)
    return {
        "images": normal_values(key_list[0], (IMAGES, P_SIZE, D), 1.0, 6.0, ((0, 8),)),
        "cotangent": heavy_noise(key_list[1], (IMAGES, P_SIZE, D), 1.0, 6.0, ((0, 8),), (0, 2, 8, 2.0)),
        "kept_count": draw_kept_count(jax.random.fold_in(key_list[17], 71), 0),
        "kept_index": draw_kept_index(jax.random.fold_in(key_list[17], 71), 0),
        "gain_one": jnp.clip(1.0 + 0.1 * jax.random.normal(key_list[4], (N_SECTION, D), jnp.float32), 0.5, 1.5).astype(jnp.bfloat16),
        "shift_one": normal_values(key_list[5], (N_SECTION, D), 0.3, 1.5, ((0, 4), (1, 8))),
        "qkv_matrix": normal_values(key_list[6], (N_SECTION, D, 3 * D), D ** -0.5, 0.21875, ((0, 4), (1, 8))),
        "qkv_shift": normal_values(key_list[7], (N_SECTION, 3 * D), 0.3, 1.5, ((0, 4), (1, 8))),
        "proj_matrix": normal_values(key_list[8], (N_SECTION, D, D), (D // 8) ** -0.5, 0.625, ((0, 4), (1, 8))),
        "proj_shift": normal_values(key_list[9], (N_SECTION, D), 0.3, 1.5, ((0, 4), (1, 8))),
        "gain_two": jnp.clip(1.0 + 0.1 * jax.random.normal(key_list[10], (N_SECTION, D), jnp.float32), 0.5, 1.5).astype(jnp.bfloat16),
        "shift_two": normal_values(key_list[11], (N_SECTION, D), 0.3, 1.5, ((0, 4), (1, 8))),
        "up_matrix": normal_values(key_list[12], (N_SECTION, D, FF), D ** -0.5, 0.21875, ((0, 4), (1, 8))),
        "up_shift": normal_values(key_list[13], (N_SECTION, FF), 0.3, 1.5, ((0, 4), (1, 8))),
        "down_matrix": normal_values(key_list[14], (N_SECTION, FF, D), FF ** -0.5, 0.109375, ((0, 4), (1, 8))),
        "down_shift": normal_values(key_list[15], (N_SECTION, D), 0.3, 1.5, ((0, 4), (1, 8))),
        "frequency": jnp.clip(jnp.exp(math.log(1.0) - 2.9996462 * jax.random.uniform(key_list[16], (N_SECTION, D), jnp.float32) ** block_levels(key_list[16], (N_SECTION, D), ((0, 4), (1, 8)), -0.2, 0.2)), 0.049804688, 1.0).astype(jnp.bfloat16),
    }


@jax.custom_vjp
def low(v):
    return lax.optimization_barrier(v.astype(jnp.bfloat16)).astype(jnp.float32)

@jax.custom_vjp
def low_back(v):
    return v

def low_keep(v):
    return (low(v), None)

def low_pass(kept, grad):
    return (grad,)

def back_keep(v):
    return (v, None)

def back_low(kept, grad):
    return (low(grad),)
low.defvjp(low_keep, low_pass)
low_back.defvjp(back_keep, back_low)
EPSILON = 1e-06
MASKED = -1e+30

def layer_norm(values, gain_vector, shift_vector):
    row_mean = lax.optimization_barrier(jnp.mean(values, axis=-1, keepdims=True))
    centred = values - row_mean
    variance = lax.optimization_barrier(jnp.mean(centred * centred, axis=-1, keepdims=True))
    return centred * lax.rsqrt(variance + EPSILON) * gain_vector + shift_vector

def exact_gelu(values):
    return jax.nn.gelu(values, approximate=False)

def rotate(values, cosine, sine_part):
    half_width = values.shape[-1] // 2
    first_half = values[..., :half_width]
    second_half = values[..., half_width:]
    return jnp.concatenate([first_half * cosine - second_half * sine_part, first_half * sine_part + second_half * cosine], axis=-1)

def rope_pair(queries, keys_raw, freq_vector, row_pos, col_pos):
    half_width = HD // 2
    freq_rows = freq_vector[:D // 2].reshape(H, half_width)
    freq_cols = freq_vector[D // 2:].reshape(H, half_width)
    angle = row_pos[:, :, None, None] * freq_rows + col_pos[:, :, None, None] * freq_cols
    cosine = jnp.cos(angle)
    sine_part = jnp.sin(angle)
    return (rotate(queries, cosine, sine_part), rotate(keys_raw, cosine, sine_part))

def vit_block(section_in, keep_rows, index_rows, weights):
    gain_one, shift_one, qkv_matrix, qkv_shift, proj_matrix, proj_shift, gain_two, shift_two, up_matrix, up_shift, down_matrix, down_shift, frequency = weights
    highest = lax.Precision.HIGHEST
    images_here = section_in.shape[0]
    patches = section_in.shape[1]
    normed = low(layer_norm(section_in, gain_one, shift_one))
    mixed = low_back(jnp.dot(normed, qkv_matrix, precision=highest) + qkv_shift)
    queries = mixed[..., :D].reshape(images_here, patches, H, HD)
    keys_raw = mixed[..., D:2 * D].reshape(images_here, patches, H, HD)
    values_raw = mixed[..., 2 * D:].reshape(images_here, patches, H, HD)
    row_pos = (index_rows // GRID).astype(jnp.float32)
    col_pos = (index_rows % GRID).astype(jnp.float32)
    turned_q, turned_k = rope_pair(queries, keys_raw, frequency, row_pos, col_pos)
    low_q = low(turned_q)
    low_k = low(turned_k)
    low_v = low(values_raw)
    scores = low_back(jnp.einsum('bqhd,bkhd->bhqk', low_q, low_k, precision=highest) * HD ** (-0.5))
    scores = jnp.where(keep_rows[:, None, None, :] > 0, scores, MASKED)
    soft_rows = low(jax.nn.softmax(scores, axis=-1))
    attended = jnp.einsum('bhqk,bkhd->bqhd', soft_rows, low_v, precision=highest).reshape(images_here, patches, D)
    attended = low(low_back(attended))
    branch_one = low_back(jnp.dot(attended, proj_matrix, precision=highest) + proj_shift)
    keep_col = keep_rows[..., None]
    middle = section_in + keep_col * branch_one
    normed_two = low(layer_norm(middle, gain_two, shift_two))
    hidden = low_back(jnp.dot(normed_two, up_matrix, precision=highest) + up_shift)
    active = low(exact_gelu(hidden))
    branch_two = low_back(jnp.dot(active, down_matrix, precision=highest) + down_shift)
    return middle + keep_col * branch_two

def section_chain(group_images, group_extra, group_counts, group_index, params):
    patches = group_images.shape[1]
    keep_rows = (jnp.arange(patches)[None, :] < group_counts[:, None]).astype(jnp.float32)
    current = group_images
    results = []
    for section_no in range(N_SECTION):
        section_params = tuple((values[section_no] for values in params))
        entered = current + group_extra[section_no]
        result = vit_block(entered, keep_rows, group_index, section_params)
        results.append(result)
        current = low_back(low(result))
    return jnp.stack(results)

def reference(images, cotangent, kept_count, kept_index, gain_one, shift_one, qkv_matrix, qkv_shift, proj_matrix, proj_shift, gain_two, shift_two, up_matrix, up_shift, down_matrix, down_shift, frequency):
    params = tuple((values.astype(jnp.float32) for values in (gain_one, shift_one, qkv_matrix, qkv_shift, proj_matrix, proj_shift, gain_two, shift_two, up_matrix, up_shift, down_matrix, down_shift, frequency)))
    per_group = IMAGES // N_DP
    patches = images.shape[1]

    def forward(image_values, extra_terms, weights):
        grouped = image_values.reshape(N_DP, per_group, patches, D)
        extra_grouped = jnp.swapaxes(extra_terms.reshape(N_SECTION, N_DP, per_group, patches, D), 0, 1)
        counts_grouped = kept_count.reshape(N_DP, per_group)
        index_grouped = kept_index.reshape(N_DP, per_group, patches)

        def run_group(group_images, group_extra, group_counts, group_index):
            return section_chain(group_images, group_extra, group_counts, group_index, weights)
        checked = jax.checkpoint(run_group)

        def visit_group(batch_item):
            return checked(batch_item[0], batch_item[1], batch_item[2], batch_item[3])
        stacked = lax.map(visit_group, (grouped, extra_grouped, counts_grouped, index_grouped))
        return jnp.swapaxes(stacked, 0, 1).reshape(N_SECTION, IMAGES, patches, D)
    image_values = images.astype(jnp.float32)
    extra_terms = jnp.zeros((N_SECTION, IMAGES, patches, D), jnp.float32)
    outputs, pullback = jax.vjp(forward, image_values, extra_terms, params)
    seed_grads = jnp.zeros_like(outputs).at[N_SECTION - 1].set(cotangent.astype(jnp.float32))
    unused_images, grad_extra, grad_params = pullback(seed_grads)
    return (outputs, grad_extra, grad_params[0], grad_params[1], grad_params[2], grad_params[3], grad_params[4], grad_params[5], grad_params[6], grad_params[7], grad_params[8], grad_params[9], grad_params[10], grad_params[11], grad_params[12])
```

```python
import functools

import jax
import jax.numpy as jnp
from jax import lax
from jax.experimental import pallas as pl
from jax.experimental.pallas import tpu as pltpu
from jax.sharding import PartitionSpec as P

D = 768
H = 12
HD = 64
GRID = 16
EPSILON = 1e-06
MASKED = -1e30
GROUPS = 8
LANES = 128
MESH = pl.DeviceIdType.MESH


def place(replicas):
    section = lax.axis_index("section")
    dp = lax.axis_index("dp")
    x, core = lax.div(section, 2), lax.rem(section, 2)
    group, m = lax.div(dp, replicas), lax.rem(dp, replicas)
    z, y = lax.div(group, 2), lax.rem(group, 2)
    return x, core, z, y, m


def device(replicas, x, core, z, y, m):
    return (2 * x + core, (2 * z + y) * replicas + m)


def next_pairs(sections, dp_size, step):
    replicas = dp_size // GROUPS
    pairs = []
    for section in range(sections):
        for dp in range(dp_size):
            x, core = divmod(section, 2)
            group, m = divmod(dp, replicas)
            z, y = divmod(group, 2)
            role = 2 * x + z % 2 + step
            if 0 <= role < sections:
                to = device(replicas, role // 2, core, z - z % 2 + role % 2, y, m)
                pairs.append((section * dp_size + dp, to[0] * dp_size + to[1]))
    return pairs


def enter(replicas):
    x, core, z, y, m = place(replicas)
    odd = lax.rem(z, 2)
    barrier = pltpu.get_barrier_semaphore()

    def greet(to):
        pl.semaphore_signal(barrier, inc=1, device_id=to, device_id_type=MESH)

    greet(device(replicas, x, 1 - core, z, y, m))
    greet(device(replicas, x, core, z, 1 - y, m))
    for k in range(2):

        @pl.when(jnp.logical_or(core != odd, lax.div(z, 2) != k))
        def _():
            greet(device(replicas, x, odd, core + 2 * k, y, m))

    pl.semaphore_wait(barrier, 4 - jnp.where(core == odd, 1, 0))


def remote(source, target, send, arrive, to):
    return pltpu.make_async_remote_copy(
        src_ref=source,
        dst_ref=target,
        send_sem=send,
        recv_sem=arrive,
        device_id=to,
        device_id_type=MESH,
    )


def swap_start(replicas, sources, targets, send, arrive):
    x, core, z, y, m = place(replicas)
    odd = lax.rem(z, 2)
    to = device(replicas, x, odd, z - odd + core, y, m)
    for n, (source, target) in enumerate(zip(sources, targets)):

        @pl.when(core == odd)
        def _():
            pltpu.make_async_copy(source, target, arrive.at[n]).start()

        @pl.when(core != odd)
        def _():
            remote(source, target, send.at[n], arrive.at[n], to).start()


def swap_wait(replicas, sources, targets, send, arrive):
    x, core, z, y, m = place(replicas)
    odd = lax.rem(z, 2)
    to = device(replicas, x, odd, z - odd + core, y, m)
    for n, (source, target) in enumerate(zip(sources, targets)):

        @pl.when(core == odd)
        def _():
            pltpu.make_async_copy(source, target, arrive.at[n]).wait()

        @pl.when(core != odd)
        def _():
            copy = remote(source, target, send.at[n], arrive.at[n], to)
            copy.wait_recv()
            copy.wait_send()


def gather_kernel(replicas, count, swaps, *refs):
    parts, refs = refs[:count], refs[count:]
    swap_in, refs = refs[:swaps], refs[swaps:]
    wholes, refs = refs[:count], refs[count:]
    swap_out, refs = refs[:swaps], refs[swaps:]
    send, arrive, swap_send, swap_arrive = refs
    x, core, z, y, m = place(replicas)
    odd = lax.rem(z, 2)
    half = lax.div(z, 2)
    mine = 2 * z + y
    sibling = device(replicas, x, 1 - core, z, y, m)
    across = device(replicas, x, core, z, 1 - y, m)
    enter(replicas)
    swap_start(replicas, swap_in, swap_out, swap_send, swap_arrive)

    def along(n, k):
        return remote(
            parts[n],
            wholes[n].at[mine],
            send.at[n, k],
            arrive.at[n, mine],
            device(replicas, x, odd, core + 2 * k, y, m),
        )

    def own(n):
        return pltpu.make_async_copy(parts[n], wholes[n].at[mine], arrive.at[n, mine])

    def relay(n, slot, group, to):
        block = wholes[n].at[group]
        return remote(block, block, send.at[n, slot], arrive.at[n, group], to)

    for n in range(count):
        for k in range(2):
            here = jnp.logical_and(core == odd, half == k)

            @pl.when(here)
            def _():
                own(n).start()

            @pl.when(jnp.logical_not(here))
            def _():
                along(n, k).start()

    for n in range(count):
        for k in range(2):
            here = jnp.logical_and(core == odd, half == k)
            group = 2 * (core + 2 * k) + y

            @pl.when(here)
            def _():
                own(n).wait()

            @pl.when(jnp.logical_not(here))
            def _():
                relay(n, 2 + k, group, sibling).wait_recv()

            relay(n, 4 + k, group, across).start()
            relay(n, 2 + k, group, sibling).start()
        for k in range(2):
            group = 2 * (core + 2 * k) + 1 - y
            relay(n, 6 + k, group, sibling).wait_recv()
            relay(n, 6 + k, group, sibling).start()
    for n in range(count):
        for k in range(2):
            for row in range(2):
                group = 2 * (1 - core + 2 * k) + row
                relay(n, 2 + k, group, sibling).wait_recv()
    for n in range(count):
        for k in range(2):
            here = jnp.logical_and(core == odd, half == k)
            group = 2 * (core + 2 * k) + y
            other = 2 * (core + 2 * k) + 1 - y

            @pl.when(jnp.logical_not(here))
            def _():
                along(n, k).wait_send()

            relay(n, 2 + k, group, sibling).wait_send()
            relay(n, 4 + k, group, across).wait_send()
            relay(n, 6 + k, other, sibling).wait_send()
    swap_wait(replicas, swap_in, swap_out, swap_send, swap_arrive)


def gather(replicas, parts, swaps):
    anywhere = pl.BlockSpec(memory_space=pl.ANY)
    count, extra = len(parts), len(swaps)
    outs = [jax.ShapeDtypeStruct((GROUPS, *part.shape), part.dtype) for part in parts]
    outs += [jax.ShapeDtypeStruct(value.shape, value.dtype) for value in swaps]
    results = pl.pallas_call(
        functools.partial(gather_kernel, replicas, count, extra),
        out_shape=outs,
        in_specs=[anywhere] * (count + extra),
        out_specs=[anywhere] * (count + extra),
        scratch_shapes=[
            pltpu.SemaphoreType.DMA((count, 8)),
            pltpu.SemaphoreType.DMA((count, GROUPS)),
            pltpu.SemaphoreType.DMA((extra,)),
            pltpu.SemaphoreType.DMA((extra,)),
        ],
        compiler_params=pltpu.CompilerParams(collective_id=0, has_side_effects=True),
        name="gather",
    )(*parts, *swaps)
    return results[:count], results[count:]


def rows_of(dtype):
    return 16 if dtype == jnp.bfloat16 else 8


def reduce_kernel(replicas, count, swaps, *refs):
    parts, refs = refs[:count], refs[count:]
    swap_in, refs = refs[:swaps], refs[swaps:]
    outs, refs = refs[:count], refs[count:]
    swap_out, refs = refs[:swaps], refs[swaps:]
    held, refs = refs[:count], refs[count:]
    first, refs = refs[:count], refs[count:]
    second, refs = refs[:count], refs[count:]
    third, refs = refs[:count], refs[count:]
    send, load, arrive, swap_send, swap_arrive = refs
    x, core, z, y, m = place(replicas)
    odd = lax.rem(z, 2)
    half = lax.div(z, 2)
    sibling = device(replicas, x, 1 - core, z, y, m)
    across = device(replicas, x, core, z, 1 - y, m)
    enter(replicas)
    swap_start(replicas, swap_in, swap_out, swap_send, swap_arrive)

    def to_sibling(n, slot):
        k, other = slot % 2, slot < 2
        group = 2 * (1 - core + 2 * k) + (1 - y if other else y)
        return remote(
            parts[n].at[group], first[n].at[slot], send.at[n, slot], arrive.at[n, slot], sibling
        )

    def loading(n, slot):
        k, other = slot % 2, slot < 2
        group = 2 * (core + 2 * k) + (1 - y if other else y)
        return pltpu.make_async_copy(parts[n].at[group], held[n].at[slot], load.at[n, slot])

    def to_across(n, k):
        return remote(
            held[n].at[k], second[n].at[k], send.at[n, 4 + k], arrive.at[n, 4 + k], across
        )

    def to_owner(n, k):
        return remote(
            held[n].at[2 + k],
            third[n].at[half],
            send.at[n, 6 + k],
            arrive.at[n, 6 + half],
            device(replicas, x, odd, core + 2 * k, y, m),
        )

    def from_other(n, k):
        return remote(
            held[n].at[2 + k],
            third[n].at[k],
            send.at[n, 6 + k],
            arrive.at[n, 6 + k],
            device(replicas, x, odd, core + 2 * k, y, m),
        )

    def add(n, slot, source, index):
        step = rows_of(held[n].dtype)
        count_rows = held[n].shape[1] // step

        def body(i, carry):
            rows = pl.ds(pl.multiple_of(i * step, step), step)
            total = held[n][slot, rows, :].astype(jnp.float32) + source[index, rows, :].astype(
                jnp.float32
            )
            held[n][slot, rows, :] = total.astype(held[n].dtype)
            return carry

        lax.fori_loop(0, count_rows, body, 0)

    for n in range(count):
        for slot in range(4):
            to_sibling(n, slot).start()
        for slot in range(4):
            loading(n, slot).start()

    for n in range(count):
        for k in range(2):
            loading(n, k).wait()
            to_sibling(n, k).wait_recv()
            add(n, k, first[n], k)
            to_across(n, k).start()
        for k in range(2):
            loading(n, 2 + k).wait()
            to_sibling(n, 2 + k).wait_recv()
            add(n, 2 + k, first[n], 2 + k)
        for k in range(2):
            here = jnp.logical_and(core == odd, half == k)
            to_across(n, k).wait_recv()
            add(n, 2 + k, second[n], k)

            @pl.when(jnp.logical_not(here))
            def _():
                to_owner(n, k).start()

    for n in range(count):
        step = rows_of(held[n].dtype)
        count_rows = held[n].shape[1] // step
        for k in range(2):
            here = jnp.logical_and(core == odd, half == k)

            @pl.when(jnp.logical_not(here))
            def _():
                from_other(n, k).wait_recv()

        def total(pick):
            def body(i, carry):
                rows = pl.ds(pl.multiple_of(i * step, step), step)
                low, high = pick(rows)
                outs[n][rows, :] = low.astype(jnp.float32) + high.astype(jnp.float32)
                return carry

            lax.fori_loop(0, count_rows, body, 0)

        @pl.when(core != odd)
        def _():
            total(lambda rows: (third[n][0, rows, :], third[n][1, rows, :]))

        @pl.when(jnp.logical_and(core == odd, half == 0))
        def _():
            total(lambda rows: (held[n][2, rows, :], third[n][1, rows, :]))

        @pl.when(jnp.logical_and(core == odd, half == 1))
        def _():
            total(lambda rows: (third[n][0, rows, :], held[n][3, rows, :]))

    for n in range(count):
        for slot in range(4):
            to_sibling(n, slot).wait_send()
        for k in range(2):
            here = jnp.logical_and(core == odd, half == k)
            to_across(n, k).wait_send()

            @pl.when(jnp.logical_not(here))
            def _():
                to_owner(n, k).wait_send()

    swap_wait(replicas, swap_in, swap_out, swap_send, swap_arrive)


def reduce(replicas, parts, swaps):
    anywhere = pl.BlockSpec(memory_space=pl.ANY)
    count, extra = len(parts), len(swaps)
    blocks = [part.shape[1:] for part in parts]
    outs = [jax.ShapeDtypeStruct(block, jnp.float32) for block in blocks]
    outs += [jax.ShapeDtypeStruct(value.shape, value.dtype) for value in swaps]

    def buffers(slots):
        return [pltpu.VMEM((slots, *part.shape[1:]), part.dtype) for part in parts]

    results = pl.pallas_call(
        functools.partial(reduce_kernel, replicas, count, extra),
        out_shape=outs,
        in_specs=[anywhere] * (count + extra),
        out_specs=[pl.BlockSpec(memory_space=pltpu.VMEM)] * count + [anywhere] * extra,
        scratch_shapes=buffers(4)
        + buffers(4)
        + buffers(2)
        + buffers(2)
        + [
            pltpu.SemaphoreType.DMA((count, 8)),
            pltpu.SemaphoreType.DMA((count, 4)),
            pltpu.SemaphoreType.DMA((count, 8)),
            pltpu.SemaphoreType.DMA((extra,)),
            pltpu.SemaphoreType.DMA((extra,)),
        ],
        compiler_params=pltpu.CompilerParams(
            collective_id=1, has_side_effects=True, vmem_limit_bytes=56 * 1024 * 1024
        ),
        name="reduce",
    )(*parts, *swaps)
    return results[:count], results[count:]


def layer_norm(values, gain_vector, shift_vector):
    row_mean = jnp.mean(values, axis=-1, keepdims=True)
    centred = values - row_mean
    variance = jnp.mean(centred * centred, axis=-1, keepdims=True)
    return centred * lax.rsqrt(variance + EPSILON) * gain_vector + shift_vector


def exact_gelu(values):
    return jax.nn.gelu(values, approximate=False)


def rotate(values, cosine, sine_part):
    half_width = values.shape[-1] // 2
    first_half = values[..., :half_width]
    second_half = values[..., half_width:]
    return jnp.concatenate(
        [
            first_half * cosine - second_half * sine_part,
            first_half * sine_part + second_half * cosine,
        ],
        axis=-1,
    )


def rope_pair(queries, keys_raw, freq_vector, row_pos, col_pos):
    half_width = HD // 2
    freq_rows = freq_vector[: D // 2].reshape(H, half_width)
    freq_cols = freq_vector[D // 2 :].reshape(H, half_width)
    angle = row_pos[:, :, None, None] * freq_rows + col_pos[:, :, None, None] * freq_cols
    cosine = jnp.cos(angle)
    sine_part = jnp.sin(angle)
    return (rotate(queries, cosine, sine_part), rotate(keys_raw, cosine, sine_part))


def positions(index_rows):
    return ((index_rows // GRID).astype(jnp.float32), (index_rows % GRID).astype(jnp.float32))


def attention_scores(low_q, low_k, keep_rows):
    scores = jnp.einsum(
        "bqhd,bkhd->bhqk", low_q, low_k, preferred_element_type=jnp.float32
    ) * HD ** (-0.5)
    return jnp.where(keep_rows[:, None, None, :] > 0, scores, MASKED)


def forward_block(section_in, keep_rows, index_rows, params):
    (
        gain_one,
        shift_one,
        qkv_matrix,
        qkv_shift,
        proj_matrix,
        proj_shift,
        gain_two,
        shift_two,
        up_matrix,
        up_shift,
        down_matrix,
        down_shift,
        frequency,
    ) = params
    images_here = section_in.shape[0]
    patches = section_in.shape[1]
    source = section_in.astype(jnp.float32)
    normed = layer_norm(source, gain_one.astype(jnp.float32), shift_one.astype(jnp.float32)).astype(
        jnp.bfloat16
    )
    mixed = jnp.dot(normed, qkv_matrix, preferred_element_type=jnp.float32) + qkv_shift.astype(
        jnp.float32
    )
    queries = mixed[..., :D].reshape(images_here, patches, H, HD)
    keys_raw = mixed[..., D : 2 * D].reshape(images_here, patches, H, HD)
    values_raw = mixed[..., 2 * D :].reshape(images_here, patches, H, HD)
    row_pos, col_pos = positions(index_rows)
    turned_q, turned_k = rope_pair(
        queries, keys_raw, frequency.astype(jnp.float32), row_pos, col_pos
    )
    low_q = turned_q.astype(jnp.bfloat16)
    low_k = turned_k.astype(jnp.bfloat16)
    low_v = values_raw.astype(jnp.bfloat16)
    scores = attention_scores(low_q, low_k, keep_rows)
    row_top = jnp.max(scores, axis=-1, keepdims=True)
    log_total = row_top + jnp.log(jnp.sum(jnp.exp(scores - row_top), axis=-1, keepdims=True))
    soft_rows = jnp.exp(scores - log_total).astype(jnp.bfloat16)
    attended = jnp.einsum("bhqk,bkhd->bqhd", soft_rows, low_v, preferred_element_type=jnp.float32)
    attended = attended.reshape(images_here, patches, D).astype(jnp.bfloat16)
    keep_col = keep_rows[..., None]
    branch_one = jnp.dot(
        attended, proj_matrix, preferred_element_type=jnp.float32
    ) + proj_shift.astype(jnp.float32)
    middle = source + keep_col * branch_one
    normed_two = layer_norm(
        middle, gain_two.astype(jnp.float32), shift_two.astype(jnp.float32)
    ).astype(jnp.bfloat16)
    hidden = jnp.dot(normed_two, up_matrix, preferred_element_type=jnp.float32) + up_shift.astype(
        jnp.float32
    )
    active = exact_gelu(hidden).astype(jnp.bfloat16)
    branch_two = jnp.dot(
        active, down_matrix, preferred_element_type=jnp.float32
    ) + down_shift.astype(jnp.float32)
    result = middle + keep_col * branch_two
    saved = (
        source,
        normed,
        queries,
        keys_raw,
        low_q,
        low_k,
        low_v,
        log_total,
        attended,
        middle,
        normed_two,
        hidden,
        active,
    )
    return (result, saved)


def backward_block(grad_out, keep_rows, index_rows, saved, params):
    (
        gain_one,
        shift_one,
        qkv_matrix,
        qkv_shift,
        proj_matrix,
        proj_shift,
        gain_two,
        shift_two,
        up_matrix,
        up_shift,
        down_matrix,
        down_shift,
        frequency,
    ) = params
    (
        source,
        normed,
        queries,
        keys_raw,
        low_q,
        low_k,
        low_v,
        log_total,
        attended,
        middle,
        normed_two,
        hidden,
        active,
    ) = saved
    images_here = grad_out.shape[0]
    patches = grad_out.shape[1]
    keep_col = keep_rows[..., None]
    grad_two = (grad_out * keep_col).astype(jnp.bfloat16)
    down_grad = jnp.einsum("bpf,bpd->fd", active, grad_two, preferred_element_type=jnp.float32)
    down_shift_grad = jnp.sum(grad_two.astype(jnp.float32), axis=(0, 1))
    grad_active = jnp.einsum(
        "bpd,fd->bpf", grad_two, down_matrix, preferred_element_type=jnp.float32
    )
    unused, gelu_pull = jax.vjp(exact_gelu, hidden)
    grad_hidden = gelu_pull(grad_active)[0].astype(jnp.bfloat16)
    up_grad = jnp.einsum("bpd,bpf->df", normed_two, grad_hidden, preferred_element_type=jnp.float32)
    up_shift_grad = jnp.sum(grad_hidden.astype(jnp.float32), axis=(0, 1))
    grad_normed_two = jnp.einsum(
        "bpf,df->bpd", grad_hidden, up_matrix, preferred_element_type=jnp.float32
    )
    unused, norm_pull = jax.vjp(
        layer_norm, middle, gain_two.astype(jnp.float32), shift_two.astype(jnp.float32)
    )
    grad_mid_part, gain_two_grad, shift_two_grad = norm_pull(grad_normed_two)
    grad_middle = grad_out + grad_mid_part
    grad_one = (grad_middle * keep_col).astype(jnp.bfloat16)
    proj_grad = jnp.einsum("bpi,bpo->io", attended, grad_one, preferred_element_type=jnp.float32)
    proj_shift_grad = jnp.sum(grad_one.astype(jnp.float32), axis=(0, 1))
    grad_attended = jnp.einsum(
        "bpo,io->bpi", grad_one, proj_matrix, preferred_element_type=jnp.float32
    )
    grad_attended = grad_attended.astype(jnp.bfloat16).reshape(images_here, patches, H, HD)
    scores = attention_scores(low_q, low_k, keep_rows)
    soft_exact = jnp.exp(scores - log_total)
    grad_soft = jnp.einsum(
        "bqhd,bkhd->bhqk", grad_attended, low_v, preferred_element_type=jnp.float32
    )
    grad_values = jnp.einsum(
        "bhqk,bqhd->bkhd",
        soft_exact.astype(jnp.bfloat16),
        grad_attended,
        preferred_element_type=jnp.float32,
    )
    centre = jnp.sum(soft_exact * grad_soft, axis=-1, keepdims=True)
    grad_scores = (soft_exact * (grad_soft - centre)).astype(jnp.bfloat16)
    score_scale = HD ** (-0.5)
    grad_turned_q = (
        jnp.einsum("bhqk,bkhd->bqhd", grad_scores, low_k, preferred_element_type=jnp.float32)
        * score_scale
    )
    grad_turned_k = (
        jnp.einsum("bhqk,bqhd->bkhd", grad_scores, low_q, preferred_element_type=jnp.float32)
        * score_scale
    )
    row_pos, col_pos = positions(index_rows)

    def turn_both(query_part, key_part, freq_part):
        return rope_pair(query_part, key_part, freq_part, row_pos, col_pos)

    unused, turn_pull = jax.vjp(turn_both, queries, keys_raw, frequency.astype(jnp.float32))
    grad_queries, grad_keys, frequency_grad = turn_pull((grad_turned_q, grad_turned_k))
    grad_mixed = jnp.concatenate(
        [
            grad_queries.reshape(images_here, patches, D),
            grad_keys.reshape(images_here, patches, D),
            grad_values.reshape(images_here, patches, D),
        ],
        axis=-1,
    ).astype(jnp.bfloat16)
    qkv_grad = jnp.einsum("bpd,bpe->de", normed, grad_mixed, preferred_element_type=jnp.float32)
    qkv_shift_grad = jnp.sum(grad_mixed.astype(jnp.float32), axis=(0, 1))
    grad_normed = jnp.einsum(
        "bpe,de->bpd", grad_mixed, qkv_matrix, preferred_element_type=jnp.float32
    )
    unused, first_pull = jax.vjp(
        layer_norm, source, gain_one.astype(jnp.float32), shift_one.astype(jnp.float32)
    )
    grad_source_part, gain_one_grad, shift_one_grad = first_pull(grad_normed)
    grad_input = grad_middle + grad_source_part
    grads = (
        gain_one_grad,
        shift_one_grad,
        qkv_grad,
        qkv_shift_grad,
        proj_grad,
        proj_shift_grad,
        gain_two_grad,
        shift_two_grad,
        up_grad,
        up_shift_grad,
        down_grad,
        down_shift_grad,
        frequency_grad,
    )
    return (grad_input, grads)


def rows_from(vector):
    short = -vector.shape[0] % LANES
    return jnp.pad(vector, (0, short)).reshape(-1, LANES)


def pack(vectors):
    block = jnp.concatenate([rows_from(vector) for vector in vectors], axis=0)
    return jnp.pad(block, ((0, -block.shape[0] % 16), (0, 0)))


def unpack(block, sizes):
    found, start = [], 0
    for size in sizes:
        count = -(-size // LANES)
        flat = block[:, start : start + count].reshape(block.shape[0], count * LANES)
        found.append(flat[:, :size])
        start += count
    return found


MATRICES = (2, 4, 8, 10)
VECTORS = (0, 1, 3, 5, 6, 7, 9, 11, 12)


def local(images, cotangent, kept_count, kept_index, *weights):
    sections = lax.axis_size("section")
    dp_size = lax.axis_size("dp")
    replicas = dp_size // GROUPS
    x, core, z, y, m = place(replicas)
    role = 2 * x + lax.rem(z, 2)
    subgroups = [[g * replicas + r for r in range(replicas)] for g in range(GROUPS)]
    if replicas > 1:
        weights = tuple(
            lax.all_gather(value, "dp", axis=1, tiled=True, axis_index_groups=subgroups)
            for value in weights
        )
    weights = tuple(value[0] for value in weights)
    sizes = [weights[n].shape[0] for n in VECTORS]
    per_device, patches = images.shape[:2]
    keep = (jnp.arange(patches)[None, :] < kept_count[:, None]).astype(jnp.int32)
    facts = jnp.stack([keep, kept_index], axis=1).astype(jnp.float32)
    facts = jnp.pad(facts, ((0, 0), (0, 6), (0, 0)))

    parts = [weights[n] for n in MATRICES] + [pack([weights[n] for n in VECTORS])]
    wholes, swapped = gather(replicas, parts, [images, cotangent, facts])
    images, cotangent, facts = swapped
    params = [None] * len(weights)
    for n, whole in zip(MATRICES, wholes):
        params[n] = whole.reshape(GROUPS * whole.shape[1], whole.shape[2])
    for n, vector in zip(VECTORS, unpack(wholes[-1], sizes)):
        params[n] = vector.reshape(-1)
    keep_all = facts[:, 0]
    index_all = facts[:, 1].astype(jnp.int32)

    total_steps = per_device + sections - 1
    forth = next_pairs(sections, dp_size, 1)
    back = next_pairs(sections, dp_size, -1)
    axes = ("section", "dp")
    incoming = jnp.zeros((1, patches, D), jnp.bfloat16)
    outputs = jnp.zeros((per_device, patches, D), jnp.float32)
    kept_steps = []
    for moment in range(total_steps):
        batch_no = moment - role
        valid = (batch_no >= 0) & (batch_no < per_device)
        start = jnp.clip(batch_no, 0, per_device - 1)
        if moment < per_device:
            fresh = lax.slice_in_dim(images, moment, moment + 1, axis=0)
            section_in = jnp.where(role == 0, fresh, incoming)
        else:
            section_in = incoming
        keep_rows = lax.dynamic_slice_in_dim(keep_all, start, 1, 0)
        index_rows = lax.dynamic_slice_in_dim(index_all, start, 1, 0)
        result, saved = forward_block(section_in, keep_rows, index_rows, params)
        kept_steps.append((saved, keep_rows, index_rows))
        outputs = jnp.where(
            valid, lax.dynamic_update_slice_in_dim(outputs, result, start, 0), outputs
        )
        if moment < total_steps - 1:
            incoming = lax.ppermute(result.astype(jnp.bfloat16), axes, forth)
    totals = tuple(jnp.zeros(values.shape, jnp.float32) for values in params)
    incoming = jnp.zeros((1, patches, D), jnp.bfloat16)
    input_grads = jnp.zeros((per_device, patches, D), jnp.float32)
    for moment in range(total_steps):
        earlier = total_steps - 1 - moment
        batch_no = earlier - role
        valid = (batch_no >= 0) & (batch_no < per_device)
        start = jnp.clip(batch_no, 0, per_device - 1)
        from_next = jnp.where(
            role == sections - 1, lax.dynamic_slice_in_dim(cotangent, start, 1, 0), incoming
        )
        grad_out = jnp.where(valid, from_next.astype(jnp.float32), 0.0)
        saved, keep_rows, index_rows = kept_steps[earlier]
        grad_input, grads = backward_block(grad_out, keep_rows, index_rows, saved, params)
        totals = tuple(running + fresh_grad for running, fresh_grad in zip(totals, grads))
        input_grads = jnp.where(
            valid, lax.dynamic_update_slice_in_dim(input_grads, grad_input, start, 0), input_grads
        )
        if moment < total_steps - 1:
            incoming = lax.ppermute(grad_input.astype(jnp.bfloat16), axes, back)

    parts = [
        totals[n].astype(jnp.bfloat16).reshape(GROUPS, -1, totals[n].shape[1]) for n in MATRICES
    ]
    vectors = [totals[n].reshape(GROUPS, -1) for n in VECTORS]
    small = jnp.stack([pack([vector[g] for vector in vectors]) for g in range(GROUPS)])
    sums, swapped = reduce(replicas, parts[::-1] + [small], [outputs, input_grads])
    outputs, input_grads = swapped
    grads = [None] * len(weights)
    for n, value in zip(MATRICES[::-1], sums):
        grads[n] = value
    for n, vector in zip(VECTORS, unpack(sums[-1][None], sizes)):
        grads[n] = vector[0]
    if replicas > 1:
        grads = [
            lax.psum_scatter(
                value, "dp", scatter_dimension=0, tiled=True, axis_index_groups=subgroups
            )
            for value in grads
        ]
    return (outputs[None], input_grads[None], *(value[None] for value in grads))


def solution(mesh):
    in_specs = (
        P("dp", None, None),
        P("dp", None, None),
        P("dp"),
        P("dp", None),
        P("section", "dp"),
        P("section", "dp"),
        P("section", "dp", None),
        P("section", "dp"),
        P("section", "dp", None),
        P("section", "dp"),
        P("section", "dp"),
        P("section", "dp"),
        P("section", "dp", None),
        P("section", "dp"),
        P("section", "dp", None),
        P("section", "dp"),
        P("section", "dp"),
    )
    out_specs = (
        P("section", "dp", None, None),
        P("section", "dp", None, None),
        P("section", "dp"),
        P("section", "dp"),
        P("section", "dp", None),
        P("section", "dp"),
        P("section", "dp", None),
        P("section", "dp"),
        P("section", "dp"),
        P("section", "dp"),
        P("section", "dp", None),
        P("section", "dp"),
        P("section", "dp", None),
        P("section", "dp"),
        P("section", "dp"),
    )
    return jax.shard_map(local, mesh=mesh, in_specs=in_specs, out_specs=out_specs, check_vma=False)
```

```python
import functools
import math

import jax
import jax.numpy as jnp
from jax import lax
from jax.experimental import pallas as pl
from jax.experimental.pallas import tpu as pltpu
from jax.sharding import PartitionSpec as P

D = 768
H = 12
HD = 64
GRID = 16
EPSILON = 1e-06
MASKED = -1e30
GROUPS = 8
LANES = 128
TILE = 256
CHUNK = 64
MESH = pl.DeviceIdType.MESH
F32 = jnp.float32
LOW = jnp.bfloat16


class Place:
    def __init__(self, replicas):
        section = lax.axis_index("section")
        dp = lax.axis_index("dp")
        self.replicas = replicas
        self.x, self.core = lax.div(section, 2), lax.rem(section, 2)
        group, self.m = lax.div(dp, replicas), lax.rem(dp, replicas)
        self.z, self.y = lax.div(group, 2), lax.rem(group, 2)
        self.half, self.odd = lax.div(self.z, 2), lax.rem(self.z, 2)
        self.role = 2 * self.x + self.odd
        self.mine = 2 * self.z + self.y
        self.home = self.core == self.odd
        self.away = self.core != self.odd

    def device(self, x, core, z, y):
        return (2 * x + core, (2 * z + y) * self.replicas + self.m)

    def sibling(self):
        return self.device(self.x, 1 - self.core, self.z, self.y)

    def across(self):
        return self.device(self.x, self.core, self.z, 1 - self.y)

    def along(self, k):
        return self.device(self.x, self.odd, self.core + 2 * k, self.y)

    def twin(self):
        return self.along(self.half)

    def is_self(self, k):
        return jnp.logical_and(self.home, self.half == k)

    def section(self, role):
        return self.device(
            lax.div(role, 2), self.core, 2 * self.half + lax.rem(role, 2), self.y
        )


def remote(source, target, send, arrive, to):
    return pltpu.make_async_remote_copy(
        src_ref=source,
        dst_ref=target,
        send_sem=send,
        recv_sem=arrive,
        device_id=to,
        device_id_type=MESH,
    )


def enter(at, sections):
    barrier = pltpu.get_barrier_semaphore()

    def greet(to):
        pl.semaphore_signal(barrier, inc=1, device_id=to, device_id_type=MESH)

    greet(at.sibling())
    greet(at.across())
    for k in range(2):

        @pl.when(jnp.logical_not(at.is_self(k)))
        def _():
            greet(at.along(k))

    @pl.when(at.role > 0)
    def _():
        greet(at.section(at.role - 1))

    @pl.when(at.role < sections - 1)
    def _():
        greet(at.section(at.role + 1))

    ends = jnp.where(jnp.logical_or(at.role == 0, at.role == sections - 1), 1, 0)
    pl.semaphore_wait(barrier, 6 - jnp.where(at.home, 1, 0) - ends)


def span(start, size):
    return pl.ds(pl.multiple_of(start, size), size)


def dot(a, b):
    return jnp.dot(a, b, preferred_element_type=F32)


def dot_nt(a, b):
    return lax.dot_general(a, b, (((1,), (1,)), ((), ())), preferred_element_type=F32)


def dot_tn(a, b):
    return lax.dot_general(a, b, (((0,), (0,)), ((), ())), preferred_element_type=F32)


def loop(count, body):
    def step(i, carry):
        body(i)
        return carry

    lax.fori_loop(0, count, step, 0)


SMALL_ROWS = 16


def quotient(values, divisor):
    return jnp.floor((values + 0.5) * (1.0 / divisor))


def selectors(size, first_row, index):
    group = quotient(index, size)
    inside = index - group * size
    row_in = quotient(inside, LANES)
    lane = inside - row_in * LANES
    row = group * SMALL_ROWS + as_float(first_row) + row_in
    ids = lax.broadcasted_iota(jnp.int32, (GROUPS * SMALL_ROWS, index.shape[1]), 0).astype(F32)
    return (ids == row).astype(F32), (ids == lane).astype(F32)


def positions(count):
    return lax.broadcasted_iota(jnp.int32, (1, count), 1).astype(F32)


def as_float(value):
    return lax.convert_element_type(value, F32)


def spread_positions():
    at = positions(D)
    head = quotient(at, HD)
    inside = at - head * HD
    return head * (HD // 2) + inside - quotient(inside, HD // 2) * (HD // 2)


def expand(block, size, first_row, index):
    rows, lanes = selectors(size, first_row, index)
    values = dot(block, lanes.astype(LOW))
    return jnp.sum(values * rows, axis=0, keepdims=True)


def fold(vector, size, first_row, index):
    rows, lanes = selectors(size, first_row, index)
    return lax.dot_general(
        rows * vector,
        lanes,
        (((1,), (1,)), ((), ())),
        precision=lax.Precision.HIGHEST,
        preferred_element_type=F32,
    )


def normalise(values):
    mean = jnp.mean(values, axis=-1, keepdims=True)
    centred = values - mean
    variance = jnp.mean(centred * centred, axis=-1, keepdims=True)
    scale = lax.rsqrt(variance + EPSILON)
    return centred * scale, scale


def first_half(shape):
    return jnp.bitwise_and(lax.broadcasted_iota(jnp.int32, shape, 1), HD - 1) < HD // 2


def partner(values):
    left = pltpu.roll(values, values.shape[1] - HD // 2, 1)
    right = pltpu.roll(values, HD // 2, 1)
    return jnp.where(first_half(values.shape), left, right)


def unfold_turn(table):
    first, other = first_half(table.shape), partner(table)
    return jnp.where(first, table, other), jnp.where(first, -other, table)


def gelu_pair(u):
    phi = 0.5 * (1.0 + lax.erf(u * math.sqrt(0.5)))
    density = jnp.exp(-0.5 * u * u) * (1.0 / math.sqrt(2.0 * math.pi))
    return u * phi, phi + u * density


GAIN_ONE, SHIFT_ONE, PROJ_SHIFT, GAIN_TWO, SHIFT_TWO, DOWN_SHIFT, FREQ_ROW, FREQ_COL = range(8)


def block_kernel(replicas, sections, images_here, patches, *refs):
    ins, refs = refs[:9], refs[9:]
    outs, refs = refs[:7], refs[7:]
    parts = ins[:5]
    images, cotangent, facts_col, facts_row = ins[5:]
    result_out, grad_out_ref = outs[:2]
    sums = outs[2:]
    (
        qkv_w, proj_w, up_w, down_w, small_w,
        first_0, first_1, first_2, first_3, first_4,
        second_0, second_1, second_2, second_3, second_4,
        third_0, third_1, third_2, third_3, third_4,
        xin, gin, fcol, frow, qkv, probs, att, mid, n2, act, slope, g1, wide,
        shipped, stage, turns, vec, qkv_b, up_b, vec_g, qkv_bg, up_bg, small_f,
        gather_send, gather_arrive, reduce_send, reduce_arrive,
        swap_send, swap_arrive, pipe_send, pipe_arrive, ship_send, ship_arrive, tile_sem,
    ) = refs
    wholes = (small_w, qkv_w, proj_w, up_w, down_w)
    shares = (parts[4], parts[0], parts[1], parts[2], parts[3])
    firsts = (first_4, first_0, first_1, first_2, first_3)
    seconds = (second_4, second_0, second_1, second_2, second_3)
    thirds = (third_4, third_0, third_1, third_2, third_3)
    totals = (sums[4], sums[0], sums[1], sums[2], sums[3])
    partials = (small_f, qkv_w, proj_w, up_w, down_w)
    at = Place(replicas)
    last = sections - 1

    enter(at, sections)

    def swap_copy(n, source, target):
        return remote(source, target, swap_send.at[n], swap_arrive.at[n], at.twin())

    def swap_local(n, source, target):
        return pltpu.make_async_copy(source, target, swap_arrive.at[n])

    every = at.core >= 0
    moves = (
        (0, facts_col, fcol, every, every),
        (1, facts_row, frow, every, every),
        (
            2, images, xin,
            jnp.logical_and(at.x == 0, at.core == 0),
            at.role == 0,
        ),
        (
            3, cotangent, gin,
            jnp.logical_and(at.x == last // 2, at.core == last % 2),
            at.role == last,
        ),
    )

    def swap_start(n):
        number, source, target, sends, takes = moves[n]

        @pl.when(jnp.logical_and(sends, at.home))
        def _():
            swap_local(number, source, target).start()

        @pl.when(jnp.logical_and(sends, at.away))
        def _():
            swap_copy(number, source, target).start()

    def swap_wait(n):
        number, source, target, sends, takes = moves[n]

        @pl.when(jnp.logical_and(takes, at.home))
        def _():
            swap_local(number, source, target).wait()

        @pl.when(jnp.logical_and(takes, at.away))
        def _():
            swap_copy(number, source, target).wait_recv()

    def swap_sent(n):
        number, source, target, sends, takes = moves[n]

        @pl.when(jnp.logical_and(sends, at.away))
        def _():
            swap_copy(number, source, target).wait_send()

    def block_of(ref, group):
        size = ref.shape[0] // GROUPS
        return ref.at[span(group * size, size), :]

    def along(n, k):
        return remote(
            shares[n], block_of(wholes[n], at.mine),
            gather_send.at[n, k], gather_arrive.at[n, at.mine], at.along(k),
        )

    def own(n):
        return pltpu.make_async_copy(
            shares[n], block_of(wholes[n], at.mine), gather_arrive.at[n, at.mine]
        )

    def relay(n, slot, group, to):
        block = block_of(wholes[n], group)
        return remote(block, block, gather_send.at[n, slot], gather_arrive.at[n, group], to)

    def gather_start(n):
        for k in range(2):

            @pl.when(at.is_self(k))
            def _():
                own(n).start()

            @pl.when(jnp.logical_not(at.is_self(k)))
            def _():
                along(n, k).start()

    def gather_relay(n):
        for k in range(2):
            group = 2 * (at.core + 2 * k) + at.y

            @pl.when(at.is_self(k))
            def _():
                own(n).wait()

            @pl.when(jnp.logical_not(at.is_self(k)))
            def _():
                relay(n, 2 + k, group, at.sibling()).wait_recv()

            relay(n, 4 + k, group, at.across()).start()
            relay(n, 2 + k, group, at.sibling()).start()
        for k in range(2):
            group = 2 * (at.core + 2 * k) + 1 - at.y
            relay(n, 6 + k, group, at.sibling()).wait_recv()
            relay(n, 6 + k, group, at.sibling()).start()

    def gather_wait(n):
        for k in range(2):
            for row in range(2):
                group = 2 * (1 - at.core + 2 * k) + row
                relay(n, 2 + k, group, at.sibling()).wait_recv()

    def gather_sent(n):
        for k in range(2):
            group = 2 * (at.core + 2 * k) + at.y
            other = 2 * (at.core + 2 * k) + 1 - at.y

            @pl.when(jnp.logical_not(at.is_self(k)))
            def _():
                along(n, k).wait_send()

            relay(n, 2 + k, group, at.sibling()).wait_send()
            relay(n, 4 + k, group, at.across()).wait_send()
            relay(n, 6 + k, other, at.sibling()).wait_send()

    for n in range(2):
        swap_start(n)
    gather_start(0)
    swap_start(2)
    for n in range(1, 5):
        gather_start(n)
    gather_relay(0)
    gather_wait(0)
    for n in range(2):
        swap_wait(n)

    block = small_w[...]
    q = D // GROUPS
    plain = positions(D)
    apart = spread_positions()

    def take_vector(row):
        vec[row] = expand(block, q, row, plain)

    def take_frequency(t):
        vec[FREQ_ROW + t] = expand(block, q, FREQ_ROW, apart + as_float(t) * (D // 2))

    def take_qkv(t):
        qkv_b[:, span(t * D, D)] = expand(block, 3 * q, 7, plain + as_float(t) * D)

    def take_up(t):
        up_b[:, span(t * D, D)] = expand(block, 4 * q, 10, plain + as_float(t) * D)

    loop(FREQ_ROW, take_vector)
    loop(2, take_frequency)
    loop(3, take_qkv)
    loop(4, take_up)
    vec_g[...] = jnp.zeros_like(vec_g)
    qkv_bg[...] = jnp.zeros_like(qkv_bg)
    up_bg[...] = jnp.zeros_like(up_bg)

    def vector(row):
        return vec[row]

    def vector_at(row, cols):
        return vec[row, :, cols]

    def tables(b):
        rows = span(b * patches, patches)
        facts = fcol[rows, :].astype(F32)
        row_at, col_at = facts[:, 1:2], facts[:, 2:3]
        first = first_half((patches, TILE))

        def piece(t):
            cols = span(t * TILE, TILE)
            angle = row_at * vector_at(FREQ_ROW, cols) + col_at * vector_at(FREQ_COL, cols)
            turns[rows, cols] = jnp.where(first, jnp.cos(angle), jnp.sin(angle))

        loop(D // TILE, piece)

    loop(images_here, tables)

    for n in range(1, 5):
        gather_relay(n)
    swap_start(3)
    for n in range(1, 5):
        gather_wait(n)
    swap_wait(2)

    def ship_start(n, b, source, target):
        rows = span(b * patches, patches)

        @pl.when(at.home)
        def _():
            ship_here(n, b, source, target).start()

        @pl.when(at.away)
        def _():
            ship_away(n, b, source, target).start()

    def ship_here(n, b, source, target):
        rows = span(b * patches, patches)
        return pltpu.make_async_copy(
            source.at[rows, :], target.at[rows, :], ship_arrive.at[n, b]
        )

    def ship_away(n, b, source, target):
        rows = span(b * patches, patches)
        return remote(
            source.at[rows, :], target.at[rows, :],
            ship_send.at[n, b], ship_arrive.at[n, b], at.twin(),
        )

    def ship_wait(n, b, source, target):
        @pl.when(at.home)
        def _():
            ship_here(n, b, source, target).wait()

        @pl.when(at.away)
        def _():
            ship_away(n, b, source, target).wait_recv()
            ship_away(n, b, source, target).wait_send()

    def pipe(n, b, target, role):
        rows = span(b * patches, patches)
        return remote(
            shipped.at[rows, :], target.at[rows, :],
            pipe_send.at[n, b], pipe_arrive.at[n, b], at.section(role),
        )

    def chunks(b, body):
        loop(
            patches // CHUNK,
            lambda i: body(span(b * patches + i * CHUNK, CHUNK), span(i * CHUNK, CHUNK)),
        )

    def forward(b):
        rows = span(b * patches, patches)

        @pl.when(at.role > 0)
        def _():
            pipe(0, b, xin, at.role - 1).wait_recv()

        keep_col = fcol[rows, :].astype(F32)[:, 0:1]
        keep_row = frow[span(b * 8, 8), :][0:1, :]

        def norm_one(here, inside):
            hat, _ = normalise(xin[here, :].astype(F32))
            shipped[here, :] = (hat * vector(GAIN_ONE) + vector(SHIFT_ONE)).astype(LOW)

        chunks(b, norm_one)

        def turn(t):
            cols = span(t * TILE, TILE)
            table = span(lax.rem(t, D // TILE) * TILE, TILE)
            raw = dot(shipped[rows, :], qkv_w[:, cols]) + qkv_b[:, cols]
            cosine, sine = unfold_turn(turns[rows, table])
            turned = raw * cosine + partner(raw) * sine
            qkv[rows, cols] = turned.astype(LOW)

        loop(2 * D // TILE, turn)

        def plain_values(t):
            cols = span(t * TILE + 2 * D, TILE)
            qkv[rows, cols] = (dot(shipped[rows, :], qkv_w[:, cols]) + qkv_b[:, cols]).astype(LOW)

        loop(D // TILE, plain_values)

        def heads(pair):
            cols = span(pair * 2 * HD, 2 * HD)
            query = qkv[rows, cols]
            key = qkv[rows, span(D + pair * 2 * HD, 2 * HD)]
            value = qkv[rows, span(2 * D + pair * 2 * HD, 2 * HD)]
            found = []
            for e in range(2):
                inside = slice(e * HD, (e + 1) * HD)
                scores = dot_nt(query[:, inside], key[:, inside]) * HD ** (-0.5)
                scores = jnp.where(keep_row > 0, scores, MASKED)
                powers = jnp.exp(scores - jnp.max(scores, axis=-1, keepdims=True))
                share = 1.0 / jnp.sum(powers, axis=-1, keepdims=True)
                soft = (powers * share).astype(LOW)
                probs[b * H + 2 * pair + e] = soft
                found.append(dot(soft, value[:, inside]))
            att[rows, cols] = jnp.concatenate(found, axis=-1).astype(LOW)

        loop(H // 2, heads)

        def project(t):
            cols = span(t * TILE, TILE)
            branch = dot(att[rows, :], proj_w[:, cols]) + vector_at(PROJ_SHIFT, cols)
            mid[rows, cols] = xin[rows, cols].astype(F32) + keep_col * branch

        loop(D // TILE, project)

        def norm_two(here, inside):
            hat, _ = normalise(mid[here, :])
            n2[here, :] = (hat * vector(GAIN_TWO) + vector(SHIFT_TWO)).astype(LOW)

        chunks(b, norm_two)

        def raise_tile(t):
            cols = span(t * TILE, TILE)
            hidden = dot(n2[rows, :], up_w[:, cols]) + up_b[:, cols]
            value, gradient = gelu_pair(hidden)
            act[rows, cols] = value.astype(LOW)
            slope[rows, cols] = gradient.astype(LOW)

        loop(up_w.shape[1] // TILE, raise_tile)

        def lower_tile(t):
            cols = span(t * TILE, TILE)
            branch = dot(act[rows, :], down_w[:, cols]) + vector_at(DOWN_SHIFT, cols)
            result = mid[rows, cols] + keep_col * branch
            stage[rows, cols] = result
            shipped[rows, cols] = result.astype(LOW)

        loop(D // TILE, lower_tile)

        @pl.when(at.role < last)
        def _():
            pipe(0, b, xin, at.role + 1).start()

        ship_start(0, b, stage, result_out)

    loop(images_here, forward)

    for b in range(images_here):
        ship_wait(0, b, stage, result_out)

        @pl.when(at.role < last)
        def _():
            pipe(0, b, xin, at.role + 1).wait_send()

    swap_wait(3)
    for n in range(4):
        swap_sent(n)
    for n in range(5):
        gather_sent(n)

    def norm_back(values, gain_row, grad):
        hat, scale = normalise(values)
        vec_g[gain_row] += jnp.sum(grad * hat, axis=0, keepdims=True)
        vec_g[gain_row + 1] += jnp.sum(grad, axis=0, keepdims=True)
        inner = grad * vector(gain_row)
        along_hat = jnp.mean(inner * hat, axis=-1, keepdims=True)
        level = jnp.mean(inner, axis=-1, keepdims=True)
        return scale * (inner - level - hat * along_hat), hat

    def add_row(ref, cols, values):
        ref[:, cols] += jnp.sum(values.astype(F32), axis=0, keepdims=True)

    def backward(b):
        rows = span(b * patches, patches)

        @pl.when(at.role < last)
        def _():
            pipe(1, b, gin, at.role + 1).wait_recv()

        facts = fcol[rows, :].astype(F32)
        row_at, col_at = facts[:, 1:2], facts[:, 2:3]

        def mask_coming(here, inside):
            coming = gin[here, :].astype(F32)
            stage[here, :] = coming
            grad_two = (coming * fcol[here, :].astype(F32)[:, 0:1]).astype(LOW)
            gin[here, :] = grad_two
            vec_g[DOWN_SHIFT] += jnp.sum(grad_two.astype(F32), axis=0, keepdims=True)

        chunks(b, mask_coming)

        def hidden_tile(t):
            cols = span(t * TILE, TILE)
            grad = dot_nt(gin[rows, :], down_w[cols, :])
            low = (grad * slope[rows, cols].astype(F32)).astype(LOW)
            slope[rows, cols] = low
            add_row(up_bg, cols, low)

        loop(up_w.shape[1] // TILE, hidden_tile)

        def normed_two_tile(t):
            cols = span(t * TILE, TILE)
            wide[:, cols] = dot_nt(slope[rows, :], up_w[cols, :])

        loop(D // TILE, normed_two_tile)

        def middle_back(here, inside):
            part, _ = norm_back(mid[here, :], GAIN_TWO, wide[inside, :])
            grad_mid = stage[here, :] + part
            mid[here, :] = grad_mid
            grad_one = (grad_mid * fcol[here, :].astype(F32)[:, 0:1]).astype(LOW)
            g1[here, :] = grad_one
            vec_g[PROJ_SHIFT] += jnp.sum(grad_one.astype(F32), axis=0, keepdims=True)

        chunks(b, middle_back)

        def attended_tile(t):
            cols = span(t * TILE, TILE)
            shipped[rows, cols] = dot_nt(g1[rows, :], proj_w[cols, :]).astype(LOW)

        loop(D // TILE, attended_tile)

        def heads(pair):
            cols = span(pair * 2 * HD, 2 * HD)
            key_cols = span(D + pair * 2 * HD, 2 * HD)
            value_cols = span(2 * D + pair * 2 * HD, 2 * HD)
            query, key, value = qkv[rows, cols], qkv[rows, key_cols], qkv[rows, value_cols]
            grad = shipped[rows, cols]
            to_q, to_k, to_v = [], [], []
            for e in range(2):
                inside = slice(e * HD, (e + 1) * HD)
                soft_low = probs[b * H + 2 * pair + e]
                soft = soft_low.astype(F32)
                grad_soft = dot_nt(grad[:, inside], value[:, inside])
                centre = jnp.sum(soft * grad_soft, axis=-1, keepdims=True)
                grad_scores = (soft * (grad_soft - centre)).astype(LOW)
                to_v.append(dot_tn(soft_low, grad[:, inside]))
                to_q.append(dot(grad_scores, key[:, inside]))
                to_k.append(dot_tn(grad_scores, query[:, inside]))
            turned_q = jnp.concatenate(to_q, axis=-1) * HD ** (-0.5)
            turned_k = jnp.concatenate(to_k, axis=-1) * HD ** (-0.5)
            grad_v = jnp.concatenate(to_v, axis=-1).astype(LOW)
            cosine, sine = unfold_turn(turns[rows, cols])
            lane = lax.broadcasted_iota(jnp.int32, (1, 2 * HD), 1)
            sign = jnp.where(jnp.bitwise_and(lane, HD - 1) < HD // 2, -1.0, 1.0)
            swing = sign * (
                turned_q * partner(query.astype(F32)) + turned_k * partner(key.astype(F32))
            )
            for n, place_at in enumerate((row_at, col_at)):
                vec_g[FREQ_ROW + n, :, cols] += jnp.sum(swing * place_at, axis=0, keepdims=True)
            grad_q = (turned_q * cosine - partner(turned_q) * sine).astype(LOW)
            grad_k = (turned_k * cosine - partner(turned_k) * sine).astype(LOW)
            for where, low in ((cols, grad_q), (key_cols, grad_k), (value_cols, grad_v)):
                qkv[rows, where] = low
                add_row(qkv_bg, where, low)

        loop(H // 2, heads)

        def normed_tile(t):
            cols = span(t * TILE, TILE)
            wide[:, cols] = dot_nt(qkv[rows, :], qkv_w[cols, :])

        loop(D // TILE, normed_tile)

        def source_back(here, inside):
            part, hat = norm_back(xin[here, :].astype(F32), GAIN_ONE, wide[inside, :])
            grad_in = mid[here, :] + part
            mid[here, :] = grad_in
            xin[here, :] = (hat * vector(GAIN_ONE) + vector(SHIFT_ONE)).astype(LOW)
            shipped[here, :] = grad_in.astype(LOW)

        chunks(b, source_back)

        @pl.when(at.role > 0)
        def _():
            pipe(1, b, gin, at.role - 1).start()

        ship_start(1, b, mid, grad_out_ref)

    loop(images_here, backward)

    def to_sibling(n, slot):
        k, other = slot % 2, slot < 2
        group = 2 * (1 - at.core + 2 * k) + (1 - at.y if other else at.y)
        return remote(
            block_of(partials[n], group), firsts[n].at[slot],
            reduce_send.at[n, slot], reduce_arrive.at[n, slot], at.sibling(),
        )

    def held(n, slot):
        k, other = slot % 2, slot < 2
        return 2 * (at.core + 2 * k) + (1 - at.y if other else at.y)

    def to_across(n, k):
        return remote(
            block_of(partials[n], held(n, k)), seconds[n].at[k],
            reduce_send.at[n, 4 + k], reduce_arrive.at[n, 4 + k], at.across(),
        )

    def to_owner(n, k):
        return remote(
            block_of(partials[n], held(n, 2 + k)), thirds[n].at[at.half],
            reduce_send.at[n, 6 + k], reduce_arrive.at[n, 6 + at.half], at.along(k),
        )

    def from_other(n, k):
        return remote(
            block_of(partials[n], held(n, 2 + k)), thirds[n].at[k],
            reduce_send.at[n, 6 + k], reduce_arrive.at[n, 6 + k], at.along(k),
        )

    def add(n, slot, sources, index):
        ref = partials[n]
        size = ref.shape[0] // GROUPS
        base = held(n, slot) * size
        step = 16

        def body(i):
            here = pl.ds(pl.multiple_of(base + i * step, step), step)
            there = span(i * step, step)
            total = ref[here, :].astype(F32)
            for source in sources:
                total = total + source[index, there, :].astype(F32)
            ref[here, :] = total.astype(ref.dtype)

        loop(size // step, body)

    def reduce_start(n):
        for slot in range(4):
            to_sibling(n, slot).start()

    def reduce_across(n):
        for k in range(2):
            to_sibling(n, k).wait_recv()
            add(n, k, [firsts[n]], k)
            to_across(n, k).start()
        for k in range(2):
            to_sibling(n, 2 + k).wait_recv()
            add(n, 2 + k, [firsts[n]], 2 + k)

    def reduce_along(n):
        for k in range(2):
            to_across(n, k).wait_recv()
            add(n, 2 + k, [seconds[n]], k)

            @pl.when(jnp.logical_not(at.is_self(k)))
            def _():
                to_owner(n, k).start()

    def down_tile(t):
        cols = span(t * TILE, TILE)
        down_w[cols, :] = dot_tn(act[:, cols], gin[...]).astype(LOW)

    loop(down_w.shape[0] // TILE, down_tile)
    reduce_start(4)

    def up_tile(t):
        cols = span(t * TILE, TILE)
        up_w[:, cols] = dot_tn(n2[...], slope[:, cols]).astype(LOW)

    loop(up_w.shape[1] // TILE, up_tile)
    reduce_start(3)
    reduce_across(4)

    def proj_tile(t):
        cols = span(t * TILE, TILE)
        proj_w[:, cols] = dot_tn(att[...], g1[:, cols]).astype(LOW)

    loop(D // TILE, proj_tile)
    reduce_start(2)

    def qkv_tile(t):
        cols = span(t * TILE, TILE)
        qkv_w[:, cols] = dot_tn(xin[...], qkv[:, cols]).astype(LOW)

    loop(qkv_w.shape[1] // TILE, qkv_tile)
    reduce_start(1)
    reduce_across(3)

    small_f[...] = jnp.zeros_like(small_f)

    def give_vector(row):
        small_f[...] += fold(vec_g[row], q, row, plain)

    def give_frequency(t):
        small_f[...] += fold(vec_g[FREQ_ROW + t], q, FREQ_ROW, apart + as_float(t) * (D // 2))

    def give_qkv(t):
        small_f[...] += fold(qkv_bg[:, span(t * D, D)], 3 * q, 7, plain + as_float(t) * D)

    def give_up(t):
        small_f[...] += fold(up_bg[:, span(t * D, D)], 4 * q, 10, plain + as_float(t) * D)

    loop(FREQ_ROW, give_vector)
    loop(2, give_frequency)
    loop(3, give_qkv)
    loop(4, give_up)
    reduce_start(0)

    reduce_along(4)
    reduce_across(2)
    reduce_across(1)
    reduce_across(0)
    for n in (3, 2, 1, 0):
        reduce_along(n)

    used = [0]

    def tile_copy(slot, target):
        return pltpu.make_async_copy(
            stage.at[pl.ds(slot * q, q), :], target, tile_sem.at[slot]
        )

    pending = [None] * 4

    def total(n, row, col, size, width, target):
        slot = used[0] % 4
        used[0] += 1
        if pending[slot] is not None:
            tile_copy(slot, pending[slot]).wait()
        base = held(n, 2)

        def run(pick):
            step = 16

            def body(i):
                there = pl.ds(pl.multiple_of(row + i * step, step), step)
                low, high = pick(there, i * step)
                stage[pl.ds(pl.multiple_of(slot * q + i * step, step), step), :] = low.astype(F32) + high.astype(F32)

            loop(size // step, body)

        cols = pl.ds(col, width)

        def mine(k):
            start = held(n, 2 + k) * (partials[n].shape[0] // GROUPS) + row

            def read(offset):
                return partials[n][pl.ds(pl.multiple_of(start + offset, 16), 16), cols]

            return read

        @pl.when(at.away)
        def _():
            run(lambda there, offset: (thirds[n][0, there, cols], thirds[n][1, there, cols]))

        @pl.when(at.is_self(0))
        def _():
            run(lambda there, offset: (mine(0)(offset), thirds[n][1, there, cols]))

        @pl.when(at.is_self(1))
        def _():
            run(lambda there, offset: (thirds[n][0, there, cols], mine(1)(offset)))

        tile_copy(slot, target).start()
        pending[slot] = target

    def total_wait(n):
        for k in range(2):

            @pl.when(jnp.logical_not(at.is_self(k)))
            def _():
                from_other(n, k).wait_recv()

    for n in (4, 3, 2, 1):
        total_wait(n)
        size, width = totals[n].shape
        for row in range(0, size, q):
            for col in range(0, width, D):
                target = totals[n].at[pl.ds(row, q), pl.ds(col, D)]
                total(n, row, col, q, D, target)
    total_wait(0)

    @pl.when(at.away)
    def _():
        totals[0][...] = third_4[0] + third_4[1]

    for k in range(2):

        @pl.when(at.is_self(k))
        def _():
            totals[0][...] = third_4[1 - k] + small_f[span(held(0, 2 + k) * SMALL_ROWS, SMALL_ROWS), :]

    for slot, target in enumerate(pending):
        if target is not None:
            tile_copy(slot, target).wait()

    for b in range(images_here):
        ship_wait(1, b, mid, grad_out_ref)

        @pl.when(at.role > 0)
        def _():
            pipe(1, b, gin, at.role - 1).wait_send()

    for n in range(5):
        for slot in range(4):
            to_sibling(n, slot).wait_send()
        for k in range(2):
            to_across(n, k).wait_send()

            @pl.when(jnp.logical_not(at.is_self(k)))
            def _():
                to_owner(n, k).wait_send()


def run_block(replicas, sections, parts, images, cotangent, facts_col, facts_row):
    images_here, patches = images.shape[:2]
    rows = images_here * patches
    hidden = parts[2].shape[1]
    anywhere = pl.BlockSpec(memory_space=pl.ANY)
    flat = [value.reshape(-1, value.shape[-1]) for value in (images, cotangent, facts_col, facts_row)]
    shapes = [part.shape for part in parts]
    outs = [jax.ShapeDtypeStruct((rows, D), F32)] * 2
    outs += [jax.ShapeDtypeStruct(shape, F32) for shape in shapes]
    vmem, dma = pltpu.VMEM, pltpu.SemaphoreType.DMA
    kinds = [part.dtype for part in parts[:4]] + [F32]

    def buffers(slots):
        return [vmem((slots, *shape), kind) for shape, kind in zip(shapes, kinds)]

    scratch = [vmem((GROUPS * shape[0], shape[1]), LOW) for shape in shapes]
    scratch += buffers(4) + buffers(2) + buffers(2)
    scratch += [
        vmem((rows, D), LOW),
        vmem((rows, D), LOW),
        vmem((rows, LANES), LOW),
        vmem((images_here * 8, patches), F32),
        vmem((rows, 3 * D), LOW),
        vmem((images_here * H, patches, patches), LOW),
        vmem((rows, D), LOW),
        vmem((rows, D), F32),
        vmem((rows, D), LOW),
        vmem((rows, hidden), LOW),
        vmem((rows, hidden), LOW),
        vmem((rows, D), LOW),
        vmem((patches, D), F32),
        vmem((rows, D), LOW),
        vmem((rows, D), F32),
        vmem((rows, D), F32),
        vmem((8, 1, D), F32),
        vmem((1, 3 * D), F32),
        vmem((1, hidden), F32),
        vmem((8, 1, D), F32),
        vmem((1, 3 * D), F32),
        vmem((1, hidden), F32),
        vmem((GROUPS * SMALL_ROWS, LANES), F32),
        dma((5, 8)),
        dma((5, GROUPS)),
        dma((5, 8)),
        dma((5, 8)),
        dma((4,)),
        dma((4,)),
        dma((2, images_here)),
        dma((2, images_here)),
        dma((2, images_here)),
        dma((2, images_here)),
        dma((4,)),
    ]
    results = pl.pallas_call(
        functools.partial(block_kernel, replicas, sections, images_here, patches),
        out_shape=outs,
        in_specs=[anywhere] * 9,
        out_specs=[anywhere] * 6 + [pl.BlockSpec(memory_space=vmem)],
        scratch_shapes=scratch,
        compiler_params=pltpu.CompilerParams(
            collective_id=0, has_side_effects=True, vmem_limit_bytes=63 * 1024 * 1024
        ),
        name="block",
    )(*parts, *flat)
    outputs, input_grads = (value.reshape(images.shape) for value in results[:2])
    return outputs, input_grads, results[2:]


def rows_from(vector):
    short = -vector.shape[0] % LANES
    return jnp.pad(vector, (0, short)).reshape(-1, LANES)


def pack(vectors):
    block = jnp.concatenate([rows_from(vector) for vector in vectors], axis=0)
    return jnp.pad(block, ((0, SMALL_ROWS - block.shape[0]), (0, 0)))


def unpack(block, sizes):
    found, start = [], 0
    for size in sizes:
        count = -(-size // LANES)
        found.append(block[start : start + count].reshape(-1)[:size])
        start += count
    return found


MATRICES = (2, 4, 8, 10)
VECTORS = (0, 1, 5, 6, 7, 11, 12, 3, 9)


def local(images, cotangent, kept_count, kept_index, *weights):
    sections = lax.axis_size("section")
    replicas = lax.axis_size("dp") // GROUPS
    subgroups = [[g * replicas + r for r in range(replicas)] for g in range(GROUPS)]
    if replicas > 1:
        weights = tuple(
            lax.all_gather(value, "dp", axis=1, tiled=True, axis_index_groups=subgroups)
            for value in weights
        )
    weights = tuple(value[0] for value in weights)
    sizes = [weights[n].shape[0] for n in VECTORS]
    patches = images.shape[1]
    keep = (jnp.arange(patches)[None, :] < kept_count[:, None]).astype(jnp.int32)
    facts = jnp.stack([keep, kept_index // GRID, kept_index % GRID], axis=1).astype(F32)
    facts_row = jnp.pad(facts, ((0, 0), (0, 5), (0, 0)))
    facts_col = jnp.pad(jnp.swapaxes(facts, 1, 2), ((0, 0), (0, 0), (0, LANES - 3))).astype(LOW)
    parts = [weights[n] for n in MATRICES] + [pack([weights[n] for n in VECTORS])]
    outputs, input_grads, sums = run_block(
        replicas, sections, parts, images, cotangent, facts_col, facts_row
    )
    grads = [None] * len(weights)
    for n, value in zip(MATRICES, sums):
        grads[n] = value
    for n, vector in zip(VECTORS, unpack(sums[-1], sizes)):
        grads[n] = vector
    if replicas > 1:
        grads = [
            lax.psum_scatter(
                value, "dp", scatter_dimension=0, tiled=True, axis_index_groups=subgroups
            )
            for value in grads
        ]
    return (outputs[None], input_grads[None], *(value[None] for value in grads))


def solution(mesh):
    in_specs = (
        P("dp", None, None),
        P("dp", None, None),
        P("dp"),
        P("dp", None),
        P("section", "dp"),
        P("section", "dp"),
        P("section", "dp", None),
        P("section", "dp"),
        P("section", "dp", None),
        P("section", "dp"),
        P("section", "dp"),
        P("section", "dp"),
        P("section", "dp", None),
        P("section", "dp"),
        P("section", "dp", None),
        P("section", "dp"),
        P("section", "dp"),
    )
    out_specs = (
        P("section", "dp", None, None),
        P("section", "dp", None, None),
        P("section", "dp"),
        P("section", "dp"),
        P("section", "dp", None),
        P("section", "dp"),
        P("section", "dp", None),
        P("section", "dp"),
        P("section", "dp"),
        P("section", "dp"),
        P("section", "dp", None),
        P("section", "dp"),
        P("section", "dp", None),
        P("section", "dp"),
        P("section", "dp"),
    )
    return jax.shard_map(local, mesh=mesh, in_specs=in_specs, out_specs=out_specs, check_vma=False)
```

```python
import functools
import math

import jax
import jax.numpy as jnp
from jax import lax
from jax.experimental import pallas as pl
from jax.experimental.pallas import tpu as pltpu
from jax.sharding import PartitionSpec as P

D = 768
H = 12
HD = 64
GRID = 16
EPSILON = 1e-06
MASKED = -1e30
GROUPS = 8
LANES = 128
TILE = 768
CHUNK = 64
GRAD_TILE = 768
MESH = pl.DeviceIdType.MESH
F32 = jnp.float32
LOW = jnp.bfloat16


class Place:
    def __init__(self, replicas):
        section = lax.axis_index("section")
        dp = lax.axis_index("dp")
        self.replicas = replicas
        self.x, self.core = lax.div(section, 2), lax.rem(section, 2)
        group, self.m = lax.div(dp, replicas), lax.rem(dp, replicas)
        self.z, self.y = lax.div(group, 2), lax.rem(group, 2)
        self.half, self.odd = lax.div(self.z, 2), lax.rem(self.z, 2)
        self.role = 2 * self.x + self.odd
        self.mine = 2 * self.z + self.y
        self.home = self.core == self.odd
        self.away = self.core != self.odd

    def device(self, x, core, z, y):
        return (2 * x + core, (2 * z + y) * self.replicas + self.m)

    def sibling(self):
        return self.device(self.x, 1 - self.core, self.z, self.y)

    def across(self):
        return self.device(self.x, self.core, self.z, 1 - self.y)

    def along(self, k):
        return self.device(self.x, self.odd, self.core + 2 * k, self.y)

    def twin(self):
        return self.along(self.half)

    def is_self(self, k):
        return jnp.logical_and(self.home, self.half == k)

    def section(self, role):
        return self.device(
            lax.div(role, 2), self.core, 2 * self.half + lax.rem(role, 2), self.y
        )


def remote(source, target, send, arrive, to):
    return pltpu.make_async_remote_copy(
        src_ref=source,
        dst_ref=target,
        send_sem=send,
        recv_sem=arrive,
        device_id=to,
        device_id_type=MESH,
    )


def enter(at, sections):
    barrier = pltpu.get_barrier_semaphore()

    def greet(to):
        pl.semaphore_signal(barrier, inc=1, device_id=to, device_id_type=MESH)

    greet(at.sibling())
    greet(at.across())
    for k in range(2):

        @pl.when(jnp.logical_not(at.is_self(k)))
        def _():
            greet(at.along(k))

    @pl.when(at.role > 0)
    def _():
        greet(at.section(at.role - 1))

    @pl.when(at.role < sections - 1)
    def _():
        greet(at.section(at.role + 1))

    ends = jnp.where(jnp.logical_or(at.role == 0, at.role == sections - 1), 1, 0)
    pl.semaphore_wait(barrier, 6 - jnp.where(at.home, 1, 0) - ends)


def span(start, size):
    return pl.ds(pl.multiple_of(start, size), size)


def dot(a, b):
    return jnp.dot(a, b, preferred_element_type=F32)


def dot_nt(a, b):
    return lax.dot_general(a, b, (((1,), (1,)), ((), ())), preferred_element_type=F32)


def dot_tn(a, b):
    return lax.dot_general(a, b, (((0,), (0,)), ((), ())), preferred_element_type=F32)


def loop(count, body, unroll=1):
    def step(i, carry):
        body(i)
        return carry

    lax.fori_loop(0, count, step, 0, unroll=unroll)


SMALL_ROWS = 16


def quotient(values, divisor):
    return jnp.floor((values + 0.5) * (1.0 / divisor))


def selectors(size, first_row, index):
    group = quotient(index, size)
    inside = index - group * size
    row_in = quotient(inside, LANES)
    lane = inside - row_in * LANES
    row = group * SMALL_ROWS + as_float(first_row) + row_in
    ids = lax.broadcasted_iota(jnp.int32, (GROUPS * SMALL_ROWS, index.shape[1]), 0).astype(F32)
    return (ids == row).astype(F32), (ids == lane).astype(F32)


def positions(count):
    return lax.broadcasted_iota(jnp.int32, (1, count), 1).astype(F32)


def as_float(value):
    return lax.convert_element_type(value, F32)


def spread_positions():
    at = positions(D)
    pair = quotient(at, 2 * HD)
    return at - quotient(at, HD) * HD + pair * HD


def paired_positions():
    at = positions(D)
    pair = quotient(at, 2 * HD)
    inside = at - pair * (2 * HD)
    half = quotient(inside, HD)
    rest = inside - half * HD
    head = quotient(rest, HD // 2)
    return pair * (2 * HD) + head * HD + half * (HD // 2) + rest - head * (HD // 2)


def expand(block, size, first_row, index):
    rows, lanes = selectors(size, first_row, index)
    values = dot(block, lanes.astype(LOW))
    return jnp.sum(values * rows, axis=0, keepdims=True)


def fold(vector, size, first_row, index):
    rows, lanes = selectors(size, first_row, index)
    return lax.dot_general(
        rows * vector,
        lanes,
        (((1,), (1,)), ((), ())),
        precision=lax.Precision.HIGHEST,
        preferred_element_type=F32,
    )


def normalise(values):
    mean = jnp.mean(values, axis=-1, keepdims=True)
    centred = values - mean
    variance = jnp.mean(centred * centred, axis=-1, keepdims=True)
    scale = lax.rsqrt(variance + EPSILON)
    return centred * scale, scale


def lanes_of(shape):
    return lax.broadcasted_iota(jnp.int32, shape, 1)


def first_half(shape):
    return jnp.bitwise_and(lanes_of(shape), 2 * HD - 1) < HD


def partner(values):
    pieces = [
        pltpu.roll(values[:, start : start + 2 * HD], HD, 1)
        for start in range(0, values.shape[1], 2 * HD)
    ]
    return jnp.concatenate(pieces, axis=1) if len(pieces) > 1 else pieces[0]


def unfold_turn(table):
    first, other = first_half(table.shape), partner(table)
    return jnp.where(first, table, other), jnp.where(first, -other, table)


LOG2_E = 1.0 / math.log(2.0)


def gelu_pair(u):
    phi = 0.5 * (1.0 + lax.erf(u * math.sqrt(0.5)))
    density = jnp.exp2(u * u * (-0.5 * LOG2_E)) * (1.0 / math.sqrt(2.0 * math.pi))
    return u * phi, phi + u * density


GAIN_ONE, SHIFT_ONE, PROJ_SHIFT, GAIN_TWO, SHIFT_TWO, DOWN_SHIFT, FREQ_ROW, FREQ_COL = range(8)


def block_kernel(replicas, sections, images_here, patches, *refs):
    ins, refs = refs[:9], refs[9:]
    outs, refs = refs[:7], refs[7:]
    parts = ins[:5]
    images, cotangent, facts_col, facts_row = ins[5:]
    result_out, grad_out_ref = outs[:2]
    sums = outs[2:]
    (
        qkv_w, proj_w, up_w, down_w, small_w,
        first_0, first_1, first_2, first_3, first_4,
        second_0, second_1, second_2, second_3, second_4,
        third_0, third_1, third_2, third_3, third_4,
        xin, gin, fcol, frow, qkv, probs, att, mid, n2, act, slope, g1, wide,
        shipped, stage, turns, vec, qkv_b, up_b, vec_g, qkv_bg, up_bg, small_f,
        gather_send, gather_arrive, reduce_send, reduce_arrive,
        swap_send, swap_arrive, pipe_send, pipe_arrive, ship_send, ship_arrive, tile_sem,
    ) = refs
    wholes = (small_w, qkv_w, proj_w, up_w, down_w)
    shares = (parts[4], parts[0], parts[1], parts[2], parts[3])
    firsts = (first_4, first_0, first_1, first_2, first_3)
    seconds = (second_4, second_0, second_1, second_2, second_3)
    thirds = (third_4, third_0, third_1, third_2, third_3)
    totals = (sums[4], sums[0], sums[1], sums[2], sums[3])
    partials = (small_f, qkv_w, proj_w, up_w, down_w)
    at = Place(replicas)
    last = sections - 1

    enter(at, sections)

    def swap_copy(n, source, target):
        return remote(source, target, swap_send.at[n], swap_arrive.at[n], at.twin())

    def swap_local(n, source, target):
        return pltpu.make_async_copy(source, target, swap_arrive.at[n])

    every = at.core >= 0
    moves = (
        (0, facts_col, fcol, every, every),
        (1, facts_row, frow, every, every),
        (
            2, images, xin,
            jnp.logical_and(at.x == 0, at.core == 0),
            at.role == 0,
        ),
        (
            3, cotangent, gin,
            jnp.logical_and(at.x == last // 2, at.core == last % 2),
            at.role == last,
        ),
    )

    def swap_start(n):
        number, source, target, sends, takes = moves[n]

        @pl.when(jnp.logical_and(sends, at.home))
        def _():
            swap_local(number, source, target).start()

        @pl.when(jnp.logical_and(sends, at.away))
        def _():
            swap_copy(number, source, target).start()

    def swap_wait(n):
        number, source, target, sends, takes = moves[n]

        @pl.when(jnp.logical_and(takes, at.home))
        def _():
            swap_local(number, source, target).wait()

        @pl.when(jnp.logical_and(takes, at.away))
        def _():
            swap_copy(number, source, target).wait_recv()

    def swap_sent(n):
        number, source, target, sends, takes = moves[n]

        @pl.when(jnp.logical_and(sends, at.away))
        def _():
            swap_copy(number, source, target).wait_send()

    def block_of(ref, group):
        size = ref.shape[0] // GROUPS
        return ref.at[span(group * size, size), :]

    def along(n, k):
        return remote(
            shares[n], block_of(wholes[n], at.mine),
            gather_send.at[n, k], gather_arrive.at[n, at.mine], at.along(k),
        )

    def own(n):
        return pltpu.make_async_copy(
            shares[n], block_of(wholes[n], at.mine), gather_arrive.at[n, at.mine]
        )

    def relay(n, slot, group, to):
        block = block_of(wholes[n], group)
        return remote(block, block, gather_send.at[n, slot], gather_arrive.at[n, group], to)

    def gather_start(n):
        for k in range(2):

            @pl.when(at.is_self(k))
            def _():
                own(n).start()

            @pl.when(jnp.logical_not(at.is_self(k)))
            def _():
                along(n, k).start()

    def gather_relay(n):
        for k in range(2):
            group = 2 * (at.core + 2 * k) + at.y

            @pl.when(at.is_self(k))
            def _():
                own(n).wait()

            @pl.when(jnp.logical_not(at.is_self(k)))
            def _():
                relay(n, 2 + k, group, at.sibling()).wait_recv()

            relay(n, 4 + k, group, at.across()).start()
            relay(n, 2 + k, group, at.sibling()).start()
        for k in range(2):
            group = 2 * (at.core + 2 * k) + 1 - at.y
            relay(n, 6 + k, group, at.sibling()).wait_recv()
            relay(n, 6 + k, group, at.sibling()).start()

    def gather_wait(n):
        for k in range(2):
            for row in range(2):
                group = 2 * (1 - at.core + 2 * k) + row
                relay(n, 2 + k, group, at.sibling()).wait_recv()

    def gather_sent(n):
        for k in range(2):
            group = 2 * (at.core + 2 * k) + at.y
            other = 2 * (at.core + 2 * k) + 1 - at.y

            @pl.when(jnp.logical_not(at.is_self(k)))
            def _():
                along(n, k).wait_send()

            relay(n, 2 + k, group, at.sibling()).wait_send()
            relay(n, 4 + k, group, at.across()).wait_send()
            relay(n, 6 + k, other, at.sibling()).wait_send()

    for n in range(2):
        swap_start(n)
    gather_start(0)
    swap_start(2)
    for n in range(1, 5):
        gather_start(n)
    gather_relay(0)
    gather_wait(0)
    for n in range(2):
        swap_wait(n)

    block = small_w[...]
    q = D // GROUPS
    plain = positions(D)
    apart = spread_positions()
    paired = paired_positions()

    def qkv_positions(t):
        return jnp.where(t < 2, paired, plain) + as_float(t) * D

    def take_vector(row):
        vec[row] = expand(block, q, row, plain)

    def take_frequency(t):
        vec[FREQ_ROW + t] = expand(block, q, FREQ_ROW, apart + as_float(t) * (D // 2))

    def take_qkv(t):
        qkv_b[:, span(t * D, D)] = expand(block, 3 * q, 7, qkv_positions(t))

    def take_up(t):
        up_b[:, span(t * D, D)] = expand(block, 4 * q, 10, plain + as_float(t) * D)

    loop(FREQ_ROW, take_vector)
    loop(2, take_frequency)
    loop(3, take_qkv)
    loop(4, take_up)
    vec_g[...] = jnp.zeros_like(vec_g)
    qkv_bg[...] = jnp.zeros_like(qkv_bg)
    up_bg[...] = jnp.zeros_like(up_bg)

    def vector(row):
        return vec[row]

    def vector_at(row, cols):
        return vec[row, :, cols]

    def tables(b):
        rows = span(b * patches, patches)
        facts = fcol[rows, :].astype(F32)
        row_at, col_at = facts[:, 1:2], facts[:, 2:3]
        first = first_half((patches, TILE))

        def piece(t):
            cols = span(t * TILE, TILE)
            angle = row_at * vector_at(FREQ_ROW, cols) + col_at * vector_at(FREQ_COL, cols)
            turns[rows, cols] = jnp.where(first, jnp.cos(angle), jnp.sin(angle))

        loop(D // TILE, piece)

    loop(images_here, tables)

    for n in range(1, 5):
        gather_relay(n)
    swap_start(3)
    for n in range(1, 5):
        gather_wait(n)
    swap_wait(2)

    def ship_start(n, b, source, target):
        rows = span(b * patches, patches)

        @pl.when(at.home)
        def _():
            ship_here(n, b, source, target).start()

        @pl.when(at.away)
        def _():
            ship_away(n, b, source, target).start()

    def ship_here(n, b, source, target):
        rows = span(b * patches, patches)
        return pltpu.make_async_copy(
            source.at[rows, :], target.at[rows, :], ship_arrive.at[n, b]
        )

    def ship_away(n, b, source, target):
        rows = span(b * patches, patches)
        return remote(
            source.at[rows, :], target.at[rows, :],
            ship_send.at[n, b], ship_arrive.at[n, b], at.twin(),
        )

    def ship_wait(n, b, source, target):
        @pl.when(at.home)
        def _():
            ship_here(n, b, source, target).wait()

        @pl.when(at.away)
        def _():
            ship_away(n, b, source, target).wait_recv()
            ship_away(n, b, source, target).wait_send()

    def pipe(n, b, target, role):
        rows = span(b * patches, patches)
        return remote(
            shipped.at[rows, :], target.at[rows, :],
            pipe_send.at[n, b], pipe_arrive.at[n, b], at.section(role),
        )

    def chunks(b, body):
        loop(
            patches // CHUNK,
            lambda i: body(span(b * patches + i * CHUNK, CHUNK), span(i * CHUNK, CHUNK)),
            unroll=patches // CHUNK,
        )

    def own_lanes(e):
        inside = jnp.bitwise_and(lanes_of((patches, 2 * HD)), HD - 1) < HD // 2
        return inside if e == 0 else jnp.logical_not(inside)

    def value_lanes(e):
        inside = lanes_of((patches, 2 * HD)) < HD
        return inside if e == 0 else jnp.logical_not(inside)

    def forward(b):
        rows = span(b * patches, patches)

        @pl.when(at.role > 0)
        def _():
            pipe(0, b, xin, at.role - 1).wait_recv()

        keep_col = fcol[rows, :].astype(F32)[:, 0:1]
        barred = jnp.where(frow[span(b * 8, 8), :][0:1, :] > 0, 0.0, MASKED)

        def norm_one(here, inside):
            hat, _ = normalise(xin[here, :].astype(F32))
            shipped[here, :] = (hat * vector(GAIN_ONE) + vector(SHIFT_ONE)).astype(LOW)

        chunks(b, norm_one)

        def turn(t):
            cols = span(t * TILE, TILE)
            table = span(lax.rem(t, D // TILE) * TILE, TILE)
            raw = dot(shipped[rows, :], qkv_w[:, cols]) + qkv_b[:, cols]
            cosine, sine = unfold_turn(turns[rows, table])
            turned = raw * cosine + partner(raw) * sine
            qkv[rows, cols] = turned.astype(LOW)

        loop(2 * D // TILE, turn, unroll=2)

        def plain_values(t):
            cols = span(t * TILE + 2 * D, TILE)
            qkv[rows, cols] = (dot(shipped[rows, :], qkv_w[:, cols]) + qkv_b[:, cols]).astype(LOW)

        loop(D // TILE, plain_values)

        def heads(pair):
            cols = span(pair * 2 * HD, 2 * HD)
            query = qkv[rows, cols]
            key = qkv[rows, span(D + pair * 2 * HD, 2 * HD)]
            value = qkv[rows, span(2 * D + pair * 2 * HD, 2 * HD)]
            value = jnp.concatenate([value, jnp.ones_like(value)], axis=1)
            found = []
            for e in range(2):
                own_query = jnp.where(own_lanes(e), query, jnp.zeros_like(query))
                scores = dot_nt(own_query, key) * (HD ** (-0.5) * LOG2_E) + barred
                powers = jnp.exp2(scores - jnp.max(scores, axis=1, keepdims=True))
                both = dot(powers.astype(LOW), value)
                share = 1.0 / both[:, 2 * HD :]
                probs[b * H + 2 * pair + e] = (
                    powers * jnp.concatenate([share] * (patches // (2 * HD)), axis=1)
                ).astype(LOW)
                found.append(both[:, : 2 * HD] * share)
            att[rows, cols] = jnp.where(value_lanes(0), found[0], found[1]).astype(LOW)

        loop(H // 2, heads, unroll=H // 2)

        def project(t):
            cols = span(t * TILE, TILE)
            branch = dot(att[rows, :], proj_w[:, cols]) + vector_at(PROJ_SHIFT, cols)
            mid[rows, cols] = xin[rows, cols].astype(F32) + keep_col * branch

        loop(D // TILE, project)

        def norm_two(here, inside):
            hat, _ = normalise(mid[here, :])
            n2[here, :] = (hat * vector(GAIN_TWO) + vector(SHIFT_TWO)).astype(LOW)

        chunks(b, norm_two)

        hidden = dot(n2[rows, :], up_w[...]) + up_b[...]
        value, gradient = gelu_pair(hidden)
        act[rows, :] = value.astype(LOW)
        slope[rows, :] = gradient.astype(LOW)

        def lower_tile(t):
            cols = span(t * TILE, TILE)
            branch = dot(act[rows, :], down_w[:, cols]) + vector_at(DOWN_SHIFT, cols)
            result = mid[rows, cols] + keep_col * branch
            stage[rows, cols] = result
            shipped[rows, cols] = result.astype(LOW)

        loop(D // TILE, lower_tile)

        @pl.when(at.role < last)
        def _():
            pipe(0, b, xin, at.role + 1).start()

        ship_start(0, b, stage, result_out)

    loop(images_here, forward)

    for b in range(images_here):
        ship_wait(0, b, stage, result_out)

        @pl.when(at.role < last)
        def _():
            pipe(0, b, xin, at.role + 1).wait_send()

    swap_wait(3)
    for n in range(4):
        swap_sent(n)
    for n in range(5):
        gather_sent(n)

    def norm_back(values, gain_row, grad):
        hat, scale = normalise(values)
        vec_g[gain_row] += jnp.sum(grad * hat, axis=0, keepdims=True)
        vec_g[gain_row + 1] += jnp.sum(grad, axis=0, keepdims=True)
        inner = grad * vector(gain_row)
        along_hat = jnp.mean(inner * hat, axis=-1, keepdims=True)
        level = jnp.mean(inner, axis=-1, keepdims=True)
        return scale * (inner - level - hat * along_hat), hat

    def add_row(ref, cols, values):
        ref[:, cols] += jnp.sum(values.astype(F32), axis=0, keepdims=True)

    def backward(b):
        rows = span(b * patches, patches)

        @pl.when(at.role < last)
        def _():
            pipe(1, b, gin, at.role + 1).wait_recv()

        facts = fcol[rows, :].astype(F32)
        row_at, col_at = facts[:, 1:2], facts[:, 2:3]

        def mask_coming(here, inside):
            coming = gin[here, :].astype(F32)
            stage[here, :] = coming
            grad_two = (coming * fcol[here, :].astype(F32)[:, 0:1]).astype(LOW)
            gin[here, :] = grad_two
            vec_g[DOWN_SHIFT] += jnp.sum(grad_two.astype(F32), axis=0, keepdims=True)

        chunks(b, mask_coming)

        grad = dot_nt(gin[rows, :], down_w[...])
        low = (grad * slope[rows, :].astype(F32)).astype(LOW)
        slope[rows, :] = low
        up_bg[...] += jnp.sum(low.astype(F32), axis=0, keepdims=True)

        def normed_two_tile(t):
            cols = span(t * TILE, TILE)
            wide[:, cols] = dot_nt(slope[rows, :], up_w[cols, :])

        loop(D // TILE, normed_two_tile)

        def middle_back(here, inside):
            part, _ = norm_back(mid[here, :], GAIN_TWO, wide[inside, :])
            grad_mid = stage[here, :] + part
            mid[here, :] = grad_mid
            grad_one = (grad_mid * fcol[here, :].astype(F32)[:, 0:1]).astype(LOW)
            g1[here, :] = grad_one
            vec_g[PROJ_SHIFT] += jnp.sum(grad_one.astype(F32), axis=0, keepdims=True)

        chunks(b, middle_back)

        def attended_tile(t):
            cols = span(t * TILE, TILE)
            shipped[rows, cols] = dot_nt(g1[rows, :], proj_w[cols, :]).astype(LOW)

        loop(D // TILE, attended_tile)

        def heads(pair):
            cols = span(pair * 2 * HD, 2 * HD)
            key_cols = span(D + pair * 2 * HD, 2 * HD)
            value_cols = span(2 * D + pair * 2 * HD, 2 * HD)
            query, key, value = qkv[rows, cols], qkv[rows, key_cols], qkv[rows, value_cols]
            grad = shipped[rows, cols]
            to_q, to_k, to_v = [], [], []
            for e in range(2):
                own_grad = jnp.where(value_lanes(e), grad, jnp.zeros_like(grad))
                soft_low = probs[b * H + 2 * pair + e]
                soft = soft_low.astype(F32)
                grad_soft = dot_nt(own_grad, value)
                centre = jnp.sum(soft * grad_soft, axis=1, keepdims=True)
                grad_scores = (soft * (grad_soft - centre)).astype(LOW)
                to_q.append(dot(grad_scores, key))
                to_k.append(dot_tn(grad_scores, query))
                to_v.append(dot_tn(soft_low, grad))
            scale = HD ** (-0.5)
            turned_q = jnp.where(own_lanes(0), to_q[0], to_q[1]) * scale
            turned_k = jnp.where(own_lanes(0), to_k[0], to_k[1]) * scale
            grad_v = jnp.where(value_lanes(0), to_v[0], to_v[1]).astype(LOW)
            cosine, sine = unfold_turn(turns[rows, cols])
            other_q, other_k = partner(turned_q), partner(turned_k)
            sign = jnp.where(first_half((1, 2 * HD)), 1.0, -1.0)
            swing = sign * (other_q * query.astype(F32) + other_k * key.astype(F32))
            for n, place_at in enumerate((row_at, col_at)):
                vec_g[FREQ_ROW + n, :, cols] += jnp.sum(swing * place_at, axis=0, keepdims=True)
            grad_q = (turned_q * cosine - other_q * sine).astype(LOW)
            grad_k = (turned_k * cosine - other_k * sine).astype(LOW)
            for where, low in ((cols, grad_q), (key_cols, grad_k), (value_cols, grad_v)):
                qkv[rows, where] = low
                add_row(qkv_bg, where, low)

        loop(H // 2, heads, unroll=H // 2)

        def normed_tile(t):
            cols = span(t * TILE, TILE)
            wide[:, cols] = dot_nt(qkv[rows, :], qkv_w[cols, :])

        loop(D // TILE, normed_tile)

        def source_back(here, inside):
            part, hat = norm_back(xin[here, :].astype(F32), GAIN_ONE, wide[inside, :])
            grad_in = mid[here, :] + part
            mid[here, :] = grad_in
            xin[here, :] = (hat * vector(GAIN_ONE) + vector(SHIFT_ONE)).astype(LOW)
            shipped[here, :] = grad_in.astype(LOW)

        chunks(b, source_back)

        @pl.when(at.role > 0)
        def _():
            pipe(1, b, gin, at.role - 1).start()

        ship_start(1, b, mid, grad_out_ref)

    loop(images_here, backward)

    def to_sibling(n, slot):
        k, other = slot % 2, slot < 2
        group = 2 * (1 - at.core + 2 * k) + (1 - at.y if other else at.y)
        return remote(
            block_of(partials[n], group), firsts[n].at[slot],
            reduce_send.at[n, slot], reduce_arrive.at[n, slot], at.sibling(),
        )

    def held(n, slot):
        k, other = slot % 2, slot < 2
        return 2 * (at.core + 2 * k) + (1 - at.y if other else at.y)

    def to_across(n, k):
        return remote(
            block_of(partials[n], held(n, k)), seconds[n].at[k],
            reduce_send.at[n, 4 + k], reduce_arrive.at[n, 4 + k], at.across(),
        )

    def to_owner(n, k):
        return remote(
            block_of(partials[n], held(n, 2 + k)), thirds[n].at[at.half],
            reduce_send.at[n, 6 + k], reduce_arrive.at[n, 6 + at.half], at.along(k),
        )

    def from_other(n, k):
        return remote(
            block_of(partials[n], held(n, 2 + k)), thirds[n].at[k],
            reduce_send.at[n, 6 + k], reduce_arrive.at[n, 6 + k], at.along(k),
        )

    def add(n, slot, sources, index):
        ref = partials[n]
        size = ref.shape[0] // GROUPS
        base = held(n, slot) * size
        step = 16

        def body(i):
            here = pl.ds(pl.multiple_of(base + i * step, step), step)
            there = span(i * step, step)
            total = ref[here, :].astype(F32)
            for source in sources:
                total = total + source[index, there, :].astype(F32)
            ref[here, :] = total.astype(ref.dtype)

        loop(size // step, body)

    def reduce_start(n):
        for slot in range(4):
            to_sibling(n, slot).start()

    def reduce_across(n):
        for k in range(2):
            to_sibling(n, k).wait_recv()
            add(n, k, [firsts[n]], k)
            to_across(n, k).start()
        for k in range(2):
            to_sibling(n, 2 + k).wait_recv()
            add(n, 2 + k, [firsts[n]], 2 + k)

    def reduce_along(n):
        for k in range(2):
            to_across(n, k).wait_recv()
            add(n, 2 + k, [seconds[n]], k)

            @pl.when(jnp.logical_not(at.is_self(k)))
            def _():
                to_owner(n, k).start()

    def down_tile(t):
        cols = span(t * GRAD_TILE, GRAD_TILE)
        down_w[cols, :] = dot_tn(act[:, cols], gin[...]).astype(LOW)

    loop(down_w.shape[0] // GRAD_TILE, down_tile)
    reduce_start(4)

    def up_tile(t):
        cols = span(t * GRAD_TILE, GRAD_TILE)
        up_w[:, cols] = dot_tn(n2[...], slope[:, cols]).astype(LOW)

    loop(up_w.shape[1] // GRAD_TILE, up_tile)
    reduce_start(3)
    reduce_across(4)
    proj_w[...] = dot_tn(att[...], g1[...]).astype(LOW)
    reduce_start(2)

    def qkv_tile(t):
        cols = span(t * D, D)
        qkv_w[:, cols] = dot_tn(xin[...], qkv[:, cols]).astype(LOW)

    loop(qkv_w.shape[1] // D, qkv_tile)
    reduce_start(1)
    reduce_across(3)

    small_f[...] = jnp.zeros_like(small_f)

    def give_vector(row):
        small_f[...] += fold(vec_g[row], q, row, plain)

    def give_frequency(t):
        small_f[...] += fold(vec_g[FREQ_ROW + t], q, FREQ_ROW, apart + as_float(t) * (D // 2))

    def give_qkv(t):
        small_f[...] += fold(qkv_bg[:, span(t * D, D)], 3 * q, 7, qkv_positions(t))

    def give_up(t):
        small_f[...] += fold(up_bg[:, span(t * D, D)], 4 * q, 10, plain + as_float(t) * D)

    loop(FREQ_ROW, give_vector)
    loop(2, give_frequency)
    loop(3, give_qkv)
    loop(4, give_up)
    reduce_start(0)

    reduce_along(4)
    reduce_across(2)
    reduce_across(1)
    reduce_across(0)
    for n in (3, 2, 1, 0):
        reduce_along(n)

    used = [0]

    def tile_copy(slot, target):
        return pltpu.make_async_copy(
            stage.at[pl.ds(slot * q, q), :], target, tile_sem.at[slot]
        )

    pending = [None] * 4

    def total(n, row, col, size, width, target):
        slot = used[0] % 4
        used[0] += 1
        if pending[slot] is not None:
            tile_copy(slot, pending[slot]).wait()
        base = held(n, 2)

        def run(pick):
            step = 16

            def body(i):
                there = pl.ds(pl.multiple_of(row + i * step, step), step)
                low, high = pick(there, i * step)
                stage[pl.ds(pl.multiple_of(slot * q + i * step, step), step), :] = low.astype(F32) + high.astype(F32)

            loop(size // step, body)

        cols = pl.ds(col, width)

        def mine(k):
            start = held(n, 2 + k) * (partials[n].shape[0] // GROUPS) + row

            def read(offset):
                return partials[n][pl.ds(pl.multiple_of(start + offset, 16), 16), cols]

            return read

        @pl.when(at.away)
        def _():
            run(lambda there, offset: (thirds[n][0, there, cols], thirds[n][1, there, cols]))

        @pl.when(at.is_self(0))
        def _():
            run(lambda there, offset: (mine(0)(offset), thirds[n][1, there, cols]))

        @pl.when(at.is_self(1))
        def _():
            run(lambda there, offset: (thirds[n][0, there, cols], mine(1)(offset)))

        tile_copy(slot, target).start()
        pending[slot] = target

    def total_wait(n):
        for k in range(2):

            @pl.when(jnp.logical_not(at.is_self(k)))
            def _():
                from_other(n, k).wait_recv()

    for n in (4, 3, 2, 1):
        total_wait(n)
        size, width = totals[n].shape
        for row in range(0, size, q):
            for col in range(0, width, D):
                target = totals[n].at[pl.ds(row, q), pl.ds(col, D)]
                total(n, row, col, q, D, target)
    total_wait(0)

    @pl.when(at.away)
    def _():
        totals[0][...] = third_4[0] + third_4[1]

    for k in range(2):

        @pl.when(at.is_self(k))
        def _():
            totals[0][...] = third_4[1 - k] + small_f[span(held(0, 2 + k) * SMALL_ROWS, SMALL_ROWS), :]

    for slot, target in enumerate(pending):
        if target is not None:
            tile_copy(slot, target).wait()

    for b in range(images_here):
        ship_wait(1, b, mid, grad_out_ref)

        @pl.when(at.role > 0)
        def _():
            pipe(1, b, gin, at.role - 1).wait_send()

    for n in range(5):
        for slot in range(4):
            to_sibling(n, slot).wait_send()
        for k in range(2):
            to_across(n, k).wait_send()

            @pl.when(jnp.logical_not(at.is_self(k)))
            def _():
                to_owner(n, k).wait_send()


def run_block(replicas, sections, parts, images, cotangent, facts_col, facts_row):
    images_here, patches = images.shape[:2]
    rows = images_here * patches
    hidden = parts[2].shape[1]
    anywhere = pl.BlockSpec(memory_space=pl.ANY)
    flat = [value.reshape(-1, value.shape[-1]) for value in (images, cotangent, facts_col, facts_row)]
    shapes = [part.shape for part in parts]
    outs = [jax.ShapeDtypeStruct((rows, D), F32)] * 2
    outs += [jax.ShapeDtypeStruct(shape, F32) for shape in shapes]
    vmem, dma = pltpu.VMEM, pltpu.SemaphoreType.DMA
    kinds = [part.dtype for part in parts[:4]] + [F32]

    def buffers(slots):
        return [vmem((slots, *shape), kind) for shape, kind in zip(shapes, kinds)]

    scratch = [vmem((GROUPS * shape[0], shape[1]), LOW) for shape in shapes]
    scratch += buffers(4) + buffers(2) + buffers(2)
    scratch += [
        vmem((rows, D), LOW),
        vmem((rows, D), LOW),
        vmem((rows, LANES), LOW),
        vmem((images_here * 8, patches), F32),
        vmem((rows, 3 * D), LOW),
        vmem((images_here * H, patches, patches), LOW),
        vmem((rows, D), LOW),
        vmem((rows, D), F32),
        vmem((rows, D), LOW),
        vmem((rows, hidden), LOW),
        vmem((rows, hidden), LOW),
        vmem((rows, D), LOW),
        vmem((patches, D), F32),
        vmem((rows, D), LOW),
        vmem((rows, D), F32),
        vmem((rows, D), F32),
        vmem((8, 1, D), F32),
        vmem((1, 3 * D), F32),
        vmem((1, hidden), F32),
        vmem((8, 1, D), F32),
        vmem((1, 3 * D), F32),
        vmem((1, hidden), F32),
        vmem((GROUPS * SMALL_ROWS, LANES), F32),
        dma((5, 8)),
        dma((5, GROUPS)),
        dma((5, 8)),
        dma((5, 8)),
        dma((4,)),
        dma((4,)),
        dma((2, images_here)),
        dma((2, images_here)),
        dma((2, images_here)),
        dma((2, images_here)),
        dma((4,)),
    ]
    results = pl.pallas_call(
        functools.partial(block_kernel, replicas, sections, images_here, patches),
        out_shape=outs,
        in_specs=[anywhere] * 9,
        out_specs=[anywhere] * 6 + [pl.BlockSpec(memory_space=vmem)],
        scratch_shapes=scratch,
        compiler_params=pltpu.CompilerParams(
            collective_id=0, has_side_effects=True, vmem_limit_bytes=63 * 1024 * 1024
        ),
        name="block",
    )(*parts, *flat)
    outputs, input_grads = (value.reshape(images.shape) for value in results[:2])
    return outputs, input_grads, results[2:]


def rows_from(vector):
    short = -vector.shape[0] % LANES
    return jnp.pad(vector, (0, short)).reshape(-1, LANES)


def pack(vectors):
    block = jnp.concatenate([rows_from(vector) for vector in vectors], axis=0)
    return jnp.pad(block, ((0, SMALL_ROWS - block.shape[0]), (0, 0)))


def unpack(block, sizes):
    found, start = [], 0
    for size in sizes:
        count = -(-size // LANES)
        found.append(block[start : start + count].reshape(-1)[:size])
        start += count
    return found


MATRICES = (2, 4, 8, 10)
VECTORS = (0, 1, 5, 6, 7, 11, 12, 3, 9)


def pair_heads(matrix):
    rows = matrix.shape[0]
    split = matrix[:, : 2 * D].reshape(rows, H, 2, 2, HD // 2)
    turned = jnp.swapaxes(split, 2, 3).reshape(rows, 2 * D)
    return jnp.concatenate([turned, matrix[:, 2 * D :]], axis=1)


def local(images, cotangent, kept_count, kept_index, *weights):
    sections = lax.axis_size("section")
    replicas = lax.axis_size("dp") // GROUPS
    subgroups = [[g * replicas + r for r in range(replicas)] for g in range(GROUPS)]
    if replicas > 1:
        weights = tuple(
            lax.all_gather(value, "dp", axis=1, tiled=True, axis_index_groups=subgroups)
            for value in weights
        )
    weights = tuple(value[0] for value in weights)
    sizes = [weights[n].shape[0] for n in VECTORS]
    patches = images.shape[1]
    keep = (jnp.arange(patches)[None, :] < kept_count[:, None]).astype(jnp.int32)
    facts = jnp.stack([keep, kept_index // GRID, kept_index % GRID], axis=1).astype(F32)
    facts_row = jnp.pad(facts, ((0, 0), (0, 5), (0, 0)))
    facts_col = jnp.pad(jnp.swapaxes(facts, 1, 2), ((0, 0), (0, 0), (0, LANES - 3))).astype(LOW)
    parts = [pair_heads(weights[2])] + [weights[n] for n in MATRICES[1:]] + [pack([weights[n] for n in VECTORS])]
    outputs, input_grads, sums = run_block(
        replicas, sections, parts, images, cotangent, facts_col, facts_row
    )
    grads = [None] * len(weights)
    for n, value in zip(MATRICES, sums):
        grads[n] = value
    grads[2] = pair_heads(grads[2])
    for n, vector in zip(VECTORS, unpack(sums[-1], sizes)):
        grads[n] = vector
    if replicas > 1:
        grads = [
            lax.psum_scatter(
                value, "dp", scatter_dimension=0, tiled=True, axis_index_groups=subgroups
            )
            for value in grads
        ]
    return (outputs[None], input_grads[None], *(value[None] for value in grads))


def solution(mesh):
    in_specs = (
        P("dp", None, None),
        P("dp", None, None),
        P("dp"),
        P("dp", None),
        P("section", "dp"),
        P("section", "dp"),
        P("section", "dp", None),
        P("section", "dp"),
        P("section", "dp", None),
        P("section", "dp"),
        P("section", "dp"),
        P("section", "dp"),
        P("section", "dp", None),
        P("section", "dp"),
        P("section", "dp", None),
        P("section", "dp"),
        P("section", "dp"),
    )
    out_specs = (
        P("section", "dp", None, None),
        P("section", "dp", None, None),
        P("section", "dp"),
        P("section", "dp"),
        P("section", "dp", None),
        P("section", "dp"),
        P("section", "dp", None),
        P("section", "dp"),
        P("section", "dp"),
        P("section", "dp"),
        P("section", "dp", None),
        P("section", "dp"),
        P("section", "dp", None),
        P("section", "dp"),
        P("section", "dp"),
    )
    return jax.shard_map(local, mesh=mesh, in_specs=in_specs, out_specs=out_specs, check_vma=False)
```

```python
import functools
import math

import jax
import jax.numpy as jnp
from jax import lax
from jax.experimental import pallas as pl
from jax.experimental.pallas import tpu as pltpu
from jax.sharding import PartitionSpec as P

D = 768
H = 12
HD = 64
GRID = 16
GRID_BITS = 4
EPSILON = 1e-06
MASKED = -1e30
GROUPS = 8
LANES = 128
TILE = 768
CHUNK = 64
GRAD_TILE = 768
GATHER_PARTS = (1, 3, 1, 6, 6)
AHEAD = 3
LAG = 3
MESH = pl.DeviceIdType.MESH
F32 = jnp.float32
LOW = jnp.bfloat16


class Place:
    def __init__(self, replicas):
        section = lax.axis_index("section")
        dp = lax.axis_index("dp")
        self.replicas = replicas
        self.x, self.core = lax.div(section, 2), lax.rem(section, 2)
        group, self.m = lax.div(dp, replicas), lax.rem(dp, replicas)
        self.z, self.y = lax.div(group, 2), lax.rem(group, 2)
        self.half, self.odd = lax.div(self.z, 2), lax.rem(self.z, 2)
        self.role = 2 * self.x + self.odd
        self.mine = 2 * self.z + self.y
        self.home = self.core == self.odd
        self.away = self.core != self.odd

    def device(self, x, core, z, y):
        return (2 * x + core, (2 * z + y) * self.replicas + self.m)

    def sibling(self):
        return self.device(self.x, 1 - self.core, self.z, self.y)

    def across(self):
        return self.device(self.x, self.core, self.z, 1 - self.y)

    def along(self, k):
        return self.device(self.x, self.odd, self.core + 2 * k, self.y)

    def twin(self):
        return self.along(self.half)

    def is_self(self, k):
        return jnp.logical_and(self.home, self.half == k)

    def section(self, role):
        return self.device(
            lax.div(role, 2), self.core, 2 * self.half + lax.rem(role, 2), self.y
        )


def remote(source, target, send, arrive, to):
    return pltpu.make_async_remote_copy(
        src_ref=source,
        dst_ref=target,
        send_sem=send,
        recv_sem=arrive,
        device_id=to,
        device_id_type=MESH,
    )


def enter(at, sections):
    barrier = pltpu.get_barrier_semaphore()

    def greet(to):
        pl.semaphore_signal(barrier, inc=1, device_id=to, device_id_type=MESH)

    greet(at.sibling())
    greet(at.across())
    for k in range(2):

        @pl.when(jnp.logical_not(at.is_self(k)))
        def _():
            greet(at.along(k))

    @pl.when(at.role > 0)
    def _():
        greet(at.section(at.role - 1))

    @pl.when(at.role < sections - 1)
    def _():
        greet(at.section(at.role + 1))

    ends = jnp.where(jnp.logical_or(at.role == 0, at.role == sections - 1), 1, 0)
    pl.semaphore_wait(barrier, 6 - jnp.where(at.home, 1, 0) - ends)


def span(start, size):
    return pl.ds(pl.multiple_of(start, size), size)


def dot(a, b):
    return jnp.dot(a, b, preferred_element_type=F32)


def dot_nt(a, b):
    return lax.dot_general(a, b, (((1,), (1,)), ((), ())), preferred_element_type=F32)


def dot_tn(a, b):
    return lax.dot_general(a, b, (((0,), (0,)), ((), ())), preferred_element_type=F32)


def gather_pieces(sizes):
    pieces = []
    for n, (size, parts) in enumerate(zip(sizes, GATHER_PARTS)):
        rows = size // parts
        pieces += [(n, start, rows) for start in range(0, size, rows)]
    return pieces


def loop(count, body, unroll=1):
    def step(i, carry):
        body(i)
        return carry

    lax.fori_loop(0, count, step, 0, unroll=unroll)


SMALL_ROWS = 16


def quotient(values, divisor):
    return jnp.floor((values + 0.5) * (1.0 / divisor))


def selectors(size, first_row, index):
    group = quotient(index, size)
    inside = index - group * size
    row_in = quotient(inside, LANES)
    lane = inside - row_in * LANES
    row = group * SMALL_ROWS + as_float(first_row) + row_in
    ids = lax.broadcasted_iota(jnp.int32, (GROUPS * SMALL_ROWS, index.shape[1]), 0).astype(F32)
    return (ids == row).astype(F32), (ids == lane).astype(F32)


def positions(count):
    return lax.broadcasted_iota(jnp.int32, (1, count), 1).astype(F32)


def as_float(value):
    return lax.convert_element_type(value, F32)


def spread_positions():
    at = positions(D)
    pair = quotient(at, 2 * HD)
    return at - quotient(at, HD) * HD + pair * HD


def paired_positions():
    at = positions(D)
    pair = quotient(at, 2 * HD)
    inside = at - pair * (2 * HD)
    half = quotient(inside, HD)
    rest = inside - half * HD
    head = quotient(rest, HD // 2)
    return pair * (2 * HD) + head * HD + half * (HD // 2) + rest - head * (HD // 2)


def expand(block, size, first_row, index):
    rows, lanes = selectors(size, first_row, index)
    values = dot(block, lanes.astype(LOW))
    return jnp.sum(values * rows, axis=0, keepdims=True)


def fold(vector, size, first_row, index):
    rows, lanes = selectors(size, first_row, index)
    return lax.dot_general(
        rows * vector,
        lanes,
        (((1,), (1,)), ((), ())),
        precision=lax.Precision.HIGHEST,
        preferred_element_type=F32,
    )


def normalise(values):
    mean = jnp.mean(values, axis=-1, keepdims=True)
    centred = values - mean
    variance = jnp.mean(centred * centred, axis=-1, keepdims=True)
    scale = lax.rsqrt(variance + EPSILON)
    return centred * scale, scale


def pairing():
    shape = (2 * HD, 2 * HD)
    source = lax.broadcasted_iota(jnp.int32, shape, 0)
    target = lax.broadcasted_iota(jnp.int32, shape, 1)
    half, head = lax.div(target, HD), lax.rem(lax.div(target, HD // 2), 2)
    return jnp.where(
        source == head * HD + half * (HD // 2) + lax.rem(target, HD // 2), 1.0, 0.0
    ).astype(LOW)


def lanes_of(shape):
    return lax.broadcasted_iota(jnp.int32, shape, 1)


def first_half(shape):
    return jnp.bitwise_and(lanes_of(shape), 2 * HD - 1) < HD


def partner(values):
    pieces = [
        pltpu.roll(values[:, start : start + 2 * HD], HD, 1)
        for start in range(0, values.shape[1], 2 * HD)
    ]
    return jnp.concatenate(pieces, axis=1) if len(pieces) > 1 else pieces[0]


def unfold_turn(table):
    first, other = first_half(table.shape), partner(table)
    return jnp.where(first, table, other), jnp.where(first, -other, table)


LOG2_E = 1.0 / math.log(2.0)


def gelu_pair(u):
    phi = 0.5 * (1.0 + lax.erf(u * math.sqrt(0.5)))
    density = jnp.exp2(u * u * (-0.5 * LOG2_E)) * (1.0 / math.sqrt(2.0 * math.pi))
    return u * phi, phi + u * density


MATRICES = (2, 4, 8, 10)
VECTORS = (0, 1, 5, 6, 7, 11, 12, 3, 9)

GAIN_ONE, SHIFT_ONE, PROJ_SHIFT, GAIN_TWO, SHIFT_TWO, DOWN_SHIFT, FREQ_ROW, FREQ_COL = range(8)


def block_kernel(replicas, sections, images_here, patches, *refs):
    ins, refs = refs[:8], refs[8:]
    given, refs = refs[: len(VECTORS)], refs[len(VECTORS) :]
    outs, refs = refs[:7], refs[7:]
    qkv_part, proj_part, up_part, down_part, images, cotangent, counts, indices = ins
    result_out, grad_out_ref = outs[:2]
    totals = outs[2:]
    (
        small_w, qkv_w, proj_w, up_w, down_w,
        first_0, first_1, first_2, first_3, first_4,
        second_0, second_1, second_2, second_3, second_4,
        xin, gin, gcopy, fcol, frow, qkv, probs, att, mid, n2, act, slope, g1, wide,
        shipped, back_shipped, gat, turns, vec, qkv_b, up_b, vec_g, qkv_bg, up_bg, small_f,
        qkv_own, small_own, facts_own,
        gather_send, gather_arrive, reduce_send, reduce_arrive,
        swap_send, swap_arrive, pipe_send, pipe_arrive, ship_send, ship_arrive, load, token,
    ) = refs
    wholes = (small_w, qkv_w, proj_w, up_w, down_w)
    shares = (small_own, qkv_own, proj_part, up_part, down_part)
    firsts = (first_0, first_1, first_2, first_3, first_4)
    seconds = (second_0, second_1, second_2, second_3, second_4)
    partials = (small_f, qkv_w, proj_w, up_w, down_w)
    at = Place(replicas)
    last = sections - 1
    q = D // GROUPS

    own_qkv = pltpu.make_async_copy(qkv_part, qkv_own, load)
    own_qkv.start()
    small_f[...] = jnp.zeros_like(small_f)
    row = 0
    for vector_ref in given:
        size = vector_ref.shape[1]
        for start in range(0, size, LANES):
            width = min(LANES, size - start)
            small_f[row : row + 1, 0:width] = vector_ref[:, start : start + width].astype(F32)
            row += 1
    small_own[...] = small_f[0:SMALL_ROWS, :].astype(LOW)
    facts_own[...] = jnp.zeros_like(facts_own)
    for b in range(images_here):
        slot = lax.broadcasted_iota(jnp.int32, (1, patches), 1)
        index = indices[b : b + 1, :]
        facts_own[8 * b : 8 * b + 1, :] = jnp.where(slot < counts[b], 1.0, 0.0)
        facts_own[8 * b + 1 : 8 * b + 2, :] = as_float(lax.shift_right_logical(index, GRID_BITS))
        facts_own[8 * b + 2 : 8 * b + 3, :] = as_float(jnp.bitwise_and(index, GRID - 1))
    own_qkv.wait()
    for block_no in range(2 * H // 2):
        cols = slice(block_no * 2 * HD, (block_no + 1) * 2 * HD)
        qkv_own[:, cols] = dot(qkv_own[:, cols], pairing()).astype(LOW)

    enter(at, sections)

    def swap_copy(n, source, target):
        return remote(source, target, swap_send.at[n], swap_arrive.at[n], at.twin())

    def swap_local(n, source, target):
        return pltpu.make_async_copy(source, target, swap_arrive.at[n])

    every = at.core >= 0
    moves = (
        (0, facts_own, frow, every, every),
        (
            1, images, xin,
            jnp.logical_and(at.x == 0, at.core == 0),
            at.role == 0,
        ),
        (
            2, cotangent, gin,
            jnp.logical_and(at.x == last // 2, at.core == last % 2),
            at.role == last,
        ),
    )

    def swap_start(n):
        number, source, target, sends, takes = moves[n]

        @pl.when(jnp.logical_and(sends, at.home))
        def _():
            swap_local(number, source, target).start()

        @pl.when(jnp.logical_and(sends, at.away))
        def _():
            swap_copy(number, source, target).start()

    def swap_wait(n):
        number, source, target, sends, takes = moves[n]

        @pl.when(jnp.logical_and(takes, at.home))
        def _():
            swap_local(number, source, target).wait()

        @pl.when(jnp.logical_and(takes, at.away))
        def _():
            swap_copy(number, source, target).wait_recv()

    def swap_sent(n):
        number, source, target, sends, takes = moves[n]

        @pl.when(jnp.logical_and(sends, at.away))
        def _():
            swap_copy(number, source, target).wait_send()

    pieces = gather_pieces([share.shape[0] for share in shares])

    def block_of(ref, group):
        size = ref.shape[0] // GROUPS
        return ref.at[span(group * size, size), :]

    def piece_of(i, group):
        n, start, size = pieces[i]
        first = group * (wholes[n].shape[0] // GROUPS) + start
        return wholes[n].at[pl.ds(pl.multiple_of(first, 16), size), :]

    def share_of(i):
        n, start, size = pieces[i]
        return shares[n].at[pl.ds(start, size), :]

    def along(i, k):
        return remote(
            share_of(i), piece_of(i, at.mine),
            gather_send.at[i, k], gather_arrive.at[i, at.mine], at.along(k),
        )

    def own(i):
        return pltpu.make_async_copy(
            share_of(i), piece_of(i, at.mine), gather_arrive.at[i, at.mine]
        )

    def relay(i, slot, group, to):
        block = piece_of(i, group)
        return remote(block, block, gather_send.at[i, slot], gather_arrive.at[i, group], to)

    def gather_start(i):
        for k in range(2):

            @pl.when(at.is_self(k))
            def _():
                own(i).start()

            @pl.when(jnp.logical_not(at.is_self(k)))
            def _():
                along(i, k).start()

    def gather_started(i):
        for k in range(2):

            @pl.when(jnp.logical_not(at.is_self(k)))
            def _():
                along(i, k).wait_send()

    def gather_relay(i):
        for k in range(2):
            group = 2 * (at.core + 2 * k) + at.y

            @pl.when(at.is_self(k))
            def _():
                own(i).wait()

            @pl.when(jnp.logical_not(at.is_self(k)))
            def _():
                relay(i, 2 + k, group, at.sibling()).wait_recv()

            relay(i, 4 + k, group, at.across()).start()
            relay(i, 2 + k, group, at.sibling()).start()

    def gather_pass(i):
        for k in range(2):
            group = 2 * (at.core + 2 * k) + 1 - at.y
            relay(i, 6 + k, group, at.sibling()).wait_recv()
            relay(i, 6 + k, group, at.sibling()).start()

    def gather_wait(i):
        for k in range(2):
            for row in range(2):
                group = 2 * (1 - at.core + 2 * k) + row
                relay(i, 2 + k, group, at.sibling()).wait_recv()

    def gather_sent(i):
        for k in range(2):
            group = 2 * (at.core + 2 * k) + at.y
            other = 2 * (at.core + 2 * k) + 1 - at.y
            relay(i, 2 + k, group, at.sibling()).wait_send()
            relay(i, 4 + k, group, at.across()).wait_send()
            relay(i, 6 + k, other, at.sibling()).wait_send()

    count = len(pieces)

    def gather_step(i):
        gather_relay(i)
        gather_started(i)
        if i + AHEAD < count:
            gather_start(i + AHEAD)

    swap_start(0)
    gather_start(0)
    swap_start(1)
    for i in range(1, AHEAD):
        gather_start(i)
    gather_step(0)
    swap_wait(0)
    gather_pass(0)
    gather_wait(0)
    for b in range(images_here):
        filled = jnp.concatenate(
            [frow[8 * b : 8 * b + 8, :], jnp.zeros((LANES - 8, patches), F32)], axis=0
        )
        fcol[b * patches : (b + 1) * patches, :] = jnp.transpose(filled)

    block = small_w[...]
    plain = positions(D)
    apart = spread_positions()
    paired = paired_positions()

    def qkv_positions(t):
        return jnp.where(t < 2, paired, plain) + as_float(t) * D

    def take_vector(row):
        vec[row] = expand(block, q, row, plain)

    def take_frequency(t):
        vec[FREQ_ROW + t] = expand(block, q, FREQ_ROW, apart + as_float(t) * (D // 2))

    def take_qkv(t):
        qkv_b[:, span(t * D, D)] = expand(block, 3 * q, 7, qkv_positions(t))

    def take_up(t):
        up_b[:, span(t * D, D)] = expand(block, 4 * q, 10, plain + as_float(t) * D)

    loop(FREQ_ROW, take_vector)
    loop(2, take_frequency)
    loop(3, take_qkv)
    loop(4, take_up)
    vec_g[...] = jnp.zeros_like(vec_g)
    qkv_bg[...] = jnp.zeros_like(qkv_bg)
    up_bg[...] = jnp.zeros_like(up_bg)

    def vector(row):
        return vec[row]

    def vector_at(row, cols):
        return vec[row, :, cols]

    def tables(b):
        rows = span(b * patches, patches)
        facts = fcol[rows, :]
        row_at, col_at = facts[:, 1:2], facts[:, 2:3]
        first = first_half((patches, TILE))

        def piece(t):
            cols = span(t * TILE, TILE)
            angle = row_at * vector_at(FREQ_ROW, cols) + col_at * vector_at(FREQ_COL, cols)
            turns[rows, cols] = jnp.where(first, jnp.cos(angle), jnp.sin(angle))

        loop(D // TILE, piece)

    def ship_start(n, b, source, target):
        rows = span(b * patches, patches)

        @pl.when(at.home)
        def _():
            ship_here(n, b, source, target).start()

        @pl.when(at.away)
        def _():
            ship_away(n, b, source, target).start()

    def ship_here(n, b, source, target):
        rows = span(b * patches, patches)
        return pltpu.make_async_copy(
            source.at[rows, :], target.at[rows, :], ship_arrive.at[n, b]
        )

    def ship_away(n, b, source, target):
        rows = span(b * patches, patches)
        return remote(
            source.at[rows, :], target.at[rows, :],
            ship_send.at[n, b], ship_arrive.at[n, b], at.twin(),
        )

    def ship_wait(n, b, source, target):
        @pl.when(at.home)
        def _():
            ship_here(n, b, source, target).wait()

        @pl.when(at.away)
        def _():
            ship_away(n, b, source, target).wait_recv()
            ship_away(n, b, source, target).wait_send()

    def pipe(n, b, target, role):
        rows = span(b * patches, patches)
        source = shipped if n == 0 else back_shipped
        return remote(
            source.at[rows, :], target.at[rows, :],
            pipe_send.at[n, b], pipe_arrive.at[n, b], at.section(role),
        )

    def chunks(b, body):
        loop(
            patches // CHUNK,
            lambda i: body(span(b * patches + i * CHUNK, CHUNK), span(i * CHUNK, CHUNK)),
            unroll=patches // CHUNK,
        )

    def own_lanes(e):
        inside = jnp.bitwise_and(lanes_of((patches, 2 * HD)), HD - 1) < HD // 2
        return inside if e == 0 else jnp.logical_not(inside)

    def value_lanes(e):
        inside = lanes_of((patches, 2 * HD)) < HD
        return inside if e == 0 else jnp.logical_not(inside)

    def rows_at(b):
        return span(b * patches, patches)

    def attention_inputs(b):
        rows = rows_at(b)

        def norm_one(here, inside):
            hat, _ = normalise(xin[here, :].astype(F32))
            shipped[here, :] = (hat * vector(GAIN_ONE) + vector(SHIFT_ONE)).astype(LOW)

        chunks(b, norm_one)

        def turn(t):
            cols = span(t * D, D)
            raw = dot(shipped[rows, :], qkv_w[:, cols]) + qkv_b[:, cols]
            cosine, sine = unfold_turn(turns[rows, :])
            turned = raw * cosine + partner(raw) * sine
            qkv[rows, cols] = turned.astype(LOW)

        loop(2, turn, unroll=2)
        cols = pl.ds(2 * D, D)
        qkv[rows, cols] = (dot(shipped[rows, :], qkv_w[:, cols]) + qkv_b[:, cols]).astype(LOW)

    def attention(b):
        rows = rows_at(b)
        barred = jnp.where(frow[span(b * 8, 8), :][0:1, :] > 0, 0.0, MASKED)

        def heads(pair):
            cols = span(pair * 2 * HD, 2 * HD)
            query = qkv[rows, cols]
            key = qkv[rows, span(D + pair * 2 * HD, 2 * HD)]
            value = qkv[rows, span(2 * D + pair * 2 * HD, 2 * HD)]
            value = jnp.concatenate([value, jnp.ones_like(value)], axis=1)
            found = []
            for e in range(2):
                own_query = jnp.where(own_lanes(e), query, jnp.zeros_like(query))
                scores = dot_nt(own_query, key) * (HD ** (-0.5) * LOG2_E) + barred
                powers = jnp.exp2(scores - jnp.max(scores, axis=1, keepdims=True))
                both = dot(powers.astype(LOW), value)
                share = 1.0 / both[:, 2 * HD :]
                probs[b * H + 2 * pair + e] = (
                    powers * jnp.concatenate([share] * (patches // (2 * HD)), axis=1)
                ).astype(LOW)
                found.append(both[:, : 2 * HD] * share)
            att[rows, cols] = jnp.where(value_lanes(0), found[0], found[1]).astype(LOW)

        loop(H // 2, heads, unroll=H // 2)

    def middle(b):
        rows = rows_at(b)
        keep_col = fcol[rows, :][:, 0:1]
        branch = dot(att[rows, :], proj_w[...]) + vector(PROJ_SHIFT)
        mid[rows, :] = xin[rows, :].astype(F32) + keep_col * branch

        def norm_two(here, inside):
            hat, _ = normalise(mid[here, :])
            n2[here, :] = (hat * vector(GAIN_TWO) + vector(SHIFT_TWO)).astype(LOW)

        chunks(b, norm_two)

    def raised(b):
        rows = rows_at(b)
        hidden = dot(n2[rows, :], up_w[...]) + up_b[...]
        value, gradient = gelu_pair(hidden)
        act[rows, :] = value.astype(LOW)
        slope[rows, :] = gradient.astype(LOW)

    def lowered(b):
        rows = rows_at(b)
        keep_col = fcol[rows, :][:, 0:1]
        branch = dot(act[rows, :], down_w[...]) + vector(DOWN_SHIFT)
        shipped[rows, :] = (mid[rows, :] + keep_col * branch).astype(LOW)

    def piece_range(n):
        return [i for i, piece in enumerate(pieces) if piece[0] == n]

    def ready(n):
        for i in piece_range(n):
            gather_wait(i)

    def section_zero(stages):
        @pl.when(at.role == 0)
        def _():
            for stage_now, b in stages:
                stage_now(b)

    slots = {}
    for step, stages in (
        (1, [(tables, 0)]),
        (2, [(tables, 1)]),
        (LAG + piece_range(1)[-1], [1, (attention_inputs, 0)]),
        (LAG + piece_range(1)[-1] + 1, [(attention_inputs, 1)]),
        (LAG + piece_range(1)[-1] + 2, [(attention, 0)]),
        (LAG + piece_range(1)[-1] + 3, [(attention, 1)]),
        (LAG + piece_range(1)[-1] + 4, [2, (middle, 0)]),
        (LAG + piece_range(1)[-1] + 5, [(middle, 1)]),
        (LAG + piece_range(3)[-1], [3, (raised, 0)]),
        (LAG + piece_range(3)[-1] + 2, [(raised, 1)]),
    ):
        slots.setdefault(step, []).extend(stages)
    for i in range(1, count + LAG):
        if i < count:
            gather_step(i)
        if 1 <= i - LAG:
            gather_pass(i - LAG)
        if i == piece_range(1)[-1]:
            swap_wait(1)
        for item in slots.get(i, []):
            if isinstance(item, int):
                ready(item)
            elif item[0] is tables:
                tables(item[1])
            else:
                section_zero([item])
    swap_start(2)
    ready(4)

    def pass_token():
        pl.semaphore_signal(token, inc=1, device_id=at.sibling(), device_id_type=MESH)

    def send_on(b):
        pipe(0, b, xin, at.role + 1).start()

    @pl.when(at.role == 0)
    def _():
        for b in range(images_here):
            lowered(b)

            @pl.when(jnp.logical_and(at.core == 0, b == 0))
            def _():
                send_on(b)

        for b in range(images_here):

            @pl.when(at.core == 0)
            def _():
                if b > 0:
                    pl.semaphore_wait(token, 1)
                    send_on(b)
                pipe(0, b, xin, at.role + 1).wait_send()
                pass_token()

            @pl.when(at.core == 1)
            def _():
                pl.semaphore_wait(token, 1)
                send_on(b)
                pipe(0, b, xin, at.role + 1).wait_send()
                if b < images_here - 1:
                    pass_token()

    @pl.when(at.role > 0)
    def _():
        def forward(b):
            pipe(0, b, xin, at.role - 1).wait_recv()
            for stage_now in (attention_inputs, attention, middle, raised, lowered):
                stage_now(b)

            @pl.when(at.role < last)
            def _():
                send_on(b)

        loop(images_here, forward)
        for b in range(images_here):

            @pl.when(at.role < last)
            def _():
                pipe(0, b, xin, at.role + 1).wait_send()

    for b in range(images_here):
        ship_start(0, b, shipped, result_out)
    swap_wait(2)
    for n in range(3):
        swap_sent(n)
    for i in range(count):
        gather_sent(i)

    def norm_back(values, gain_row, grad):
        hat, scale = normalise(values)
        vec_g[gain_row] += jnp.sum(grad * hat, axis=0, keepdims=True)
        vec_g[gain_row + 1] += jnp.sum(grad, axis=0, keepdims=True)
        inner = grad * vector(gain_row)
        along_hat = jnp.mean(inner * hat, axis=-1, keepdims=True)
        level = jnp.mean(inner, axis=-1, keepdims=True)
        return scale * (inner - level - hat * along_hat), hat

    def add_row(ref, cols, values):
        ref[:, cols] += jnp.sum(values.astype(F32), axis=0, keepdims=True)

    def hidden_back(b):
        rows = rows_at(b)

        def mask_coming(here, inside):
            coming = gin[here, :].astype(F32)
            gcopy[inside, :] = gin[here, :]
            grad_two = (coming * fcol[here, :][:, 0:1]).astype(LOW)
            gin[here, :] = grad_two
            vec_g[DOWN_SHIFT] += jnp.sum(grad_two.astype(F32), axis=0, keepdims=True)

        chunks(b, mask_coming)
        grad = dot_nt(gin[rows, :], down_w[...])
        low = (grad * slope[rows, :].astype(F32)).astype(LOW)
        slope[rows, :] = low
        up_bg[...] += jnp.sum(low.astype(F32), axis=0, keepdims=True)
        wide[...] = dot_nt(slope[rows, :], up_w[...])

    def middle_back(b):
        rows = rows_at(b)

        def norm_two_back(here, inside):
            part, _ = norm_back(mid[here, :], GAIN_TWO, wide[inside, :])
            grad_mid = gcopy[inside, :].astype(F32) + part
            mid[here, :] = grad_mid
            grad_one = (grad_mid * fcol[here, :][:, 0:1]).astype(LOW)
            g1[here, :] = grad_one
            vec_g[PROJ_SHIFT] += jnp.sum(grad_one.astype(F32), axis=0, keepdims=True)

        chunks(b, norm_two_back)
        gat[...] = dot_nt(g1[rows, :], proj_w[...]).astype(LOW)

    def attention_back(b):
        rows = rows_at(b)
        facts = fcol[rows, :]
        row_at, col_at = facts[:, 1:2], facts[:, 2:3]

        def heads(pair):
            cols = span(pair * 2 * HD, 2 * HD)
            key_cols = span(D + pair * 2 * HD, 2 * HD)
            value_cols = span(2 * D + pair * 2 * HD, 2 * HD)
            query, key, value = qkv[rows, cols], qkv[rows, key_cols], qkv[rows, value_cols]
            grad = gat[:, cols]
            to_q, to_k, to_v = [], [], []
            for e in range(2):
                own_grad = jnp.where(value_lanes(e), grad, jnp.zeros_like(grad))
                soft_low = probs[b * H + 2 * pair + e]
                soft = soft_low.astype(F32)
                grad_soft = dot_nt(own_grad, value)
                centre = jnp.sum(soft * grad_soft, axis=1, keepdims=True)
                grad_scores = (soft * (grad_soft - centre)).astype(LOW)
                to_q.append(dot(grad_scores, key))
                to_k.append(dot_tn(grad_scores, query))
                to_v.append(dot_tn(soft_low, grad))
            scale = HD ** (-0.5)
            turned_q = jnp.where(own_lanes(0), to_q[0], to_q[1]) * scale
            turned_k = jnp.where(own_lanes(0), to_k[0], to_k[1]) * scale
            grad_v = jnp.where(value_lanes(0), to_v[0], to_v[1]).astype(LOW)
            cosine, sine = unfold_turn(turns[rows, cols])
            other_q, other_k = partner(turned_q), partner(turned_k)
            sign = jnp.where(first_half((1, 2 * HD)), 1.0, -1.0)
            swing = sign * (other_q * query.astype(F32) + other_k * key.astype(F32))
            for n, place_at in enumerate((row_at, col_at)):
                vec_g[FREQ_ROW + n, :, cols] += jnp.sum(swing * place_at, axis=0, keepdims=True)
            grad_q = (turned_q * cosine - other_q * sine).astype(LOW)
            grad_k = (turned_k * cosine - other_k * sine).astype(LOW)
            for where, low in ((cols, grad_q), (key_cols, grad_k), (value_cols, grad_v)):
                qkv[rows, where] = low
                add_row(qkv_bg, where, low)

        loop(H // 2, heads, unroll=H // 2)

    def source_back(b):
        rows = rows_at(b)
        wide[...] = dot_nt(qkv[rows, :], qkv_w[...])

        def norm_one_back(here, inside):
            part, hat = norm_back(xin[here, :].astype(F32), GAIN_ONE, wide[inside, :])
            xin[here, :] = (hat * vector(GAIN_ONE) + vector(SHIFT_ONE)).astype(LOW)
            back_shipped[here, :] = (mid[here, :] + part).astype(LOW)

        chunks(b, norm_one_back)

        @pl.when(at.role > 0)
        def _():
            pipe(1, b, gin, at.role - 1).start()

        @pl.when(at.role == 0)
        def _():
            ship_start(1, b, back_shipped, grad_out_ref)

    def backward_wait(b):
        @pl.when(at.role < last)
        def _():
            pipe(1, b, gin, at.role + 1).wait_recv()

    def to_sibling(n, slot):
        k, other = slot % 2, slot < 2
        group = 2 * (1 - at.core + 2 * k) + (1 - at.y if other else at.y)
        return remote(
            block_of(partials[n], group), firsts[n].at[slot],
            reduce_send.at[n, slot], reduce_arrive.at[n, slot], at.sibling(),
        )

    def held(n, slot):
        k, other = slot % 2, slot < 2
        return 2 * (at.core + 2 * k) + (1 - at.y if other else at.y)

    def to_across(n, k):
        return remote(
            block_of(partials[n], held(n, k)), seconds[n].at[k],
            reduce_send.at[n, 4 + k], reduce_arrive.at[n, 4 + k], at.across(),
        )

    def to_owner(n, k):
        return remote(
            block_of(partials[n], held(n, 2 + k)), totals[n].at[at.half],
            reduce_send.at[n, 6 + k], reduce_arrive.at[n, 6 + at.half], at.along(k),
        )

    def to_self(n, k):
        return pltpu.make_async_copy(
            block_of(partials[n], held(n, 2 + k)), totals[n].at[k], reduce_arrive.at[n, 6 + k]
        )

    def from_other(n, k):
        return remote(
            block_of(partials[n], held(n, 2 + k)), totals[n].at[k],
            reduce_send.at[n, 6 + k], reduce_arrive.at[n, 6 + k], at.along(k),
        )

    def add(n, slot, sources, index):
        ref = partials[n]
        size = ref.shape[0] // GROUPS
        base = held(n, slot) * size
        step = 16

        def body(i):
            here = pl.ds(pl.multiple_of(base + i * step, step), step)
            there = span(i * step, step)
            total = ref[here, :].astype(F32)
            for source in sources:
                total = total + source[index, there, :].astype(F32)
            ref[here, :] = total.astype(ref.dtype)

        loop(size // step, body)

    def reduce_start(n):
        for slot in range(4):
            to_sibling(n, slot).start()

    def reduce_across(n):
        for k in range(2):
            to_sibling(n, k).wait_recv()
            add(n, k, [firsts[n]], k)
            to_across(n, k).start()
        for k in range(2):
            to_sibling(n, 2 + k).wait_recv()
            add(n, 2 + k, [firsts[n]], 2 + k)

    def reduce_along(n):
        for k in range(2):
            to_across(n, k).wait_recv()
            add(n, 2 + k, [seconds[n]], k)

            @pl.when(jnp.logical_not(at.is_self(k)))
            def _():
                to_owner(n, k).start()

            @pl.when(at.is_self(k))
            def _():
                to_self(n, k).start()

    def down_grad():
        def tile(t):
            cols = span(t * GRAD_TILE, GRAD_TILE)
            down_w[cols, :] = dot_tn(act[:, cols], gin[...]).astype(LOW)

        loop(down_w.shape[0] // GRAD_TILE, tile)
        reduce_start(4)

    def up_grad():
        def tile(t):
            cols = span(t * GRAD_TILE, GRAD_TILE)
            up_w[:, cols] = dot_tn(n2[...], slope[:, cols]).astype(LOW)

        loop(up_w.shape[1] // GRAD_TILE, tile)
        reduce_start(3)

    def proj_grad():
        proj_w[...] = dot_tn(att[...], g1[...]).astype(LOW)
        reduce_start(2)

    def qkv_grad():
        for block_no in range(2 * H // 2):
            cols = slice(block_no * 2 * HD, (block_no + 1) * 2 * HD)
            qkv[:, cols] = dot_nt(qkv[:, cols], pairing()).astype(LOW)

        def tile(t):
            cols = span(t * D, D)
            qkv_w[:, cols] = dot_tn(xin[...], qkv[:, cols]).astype(LOW)

        loop(qkv_w.shape[1] // D, tile)
        reduce_start(1)

    def vector_grads():
        small_f[...] = jnp.zeros_like(small_f)

        def give_vector(row):
            small_f[...] += fold(vec_g[row], q, row, plain)

        def give_frequency(t):
            small_f[...] += fold(vec_g[FREQ_ROW + t], q, FREQ_ROW, apart + as_float(t) * (D // 2))

        def give_qkv(t):
            small_f[...] += fold(qkv_bg[:, span(t * D, D)], 3 * q, 7, qkv_positions(t))

        def give_up(t):
            small_f[...] += fold(up_bg[:, span(t * D, D)], 4 * q, 10, plain + as_float(t) * D)

        loop(FREQ_ROW, give_vector)
        loop(2, give_frequency)
        loop(3, give_qkv)
        loop(4, give_up)
        reduce_start(0)

    stages = (hidden_back, middle_back, attention_back, source_back)

    def backward(b):
        backward_wait(b)
        for stage_now in stages:
            stage_now(b)

    loop(images_here - 1, backward)
    final = images_here - 1
    backward_wait(final)
    hidden_back(final)

    @pl.when(at.role == 0)
    def _():
        down_grad()
        up_grad()
        reduce_across(4)

    middle_back(final)
    attention_back(final)

    @pl.when(at.role == 0)
    def _():
        reduce_across(3)

    source_back(final)

    @pl.when(at.role > 0)
    def _():
        down_grad()
        up_grad()
        reduce_across(4)

    qkv_grad()

    @pl.when(at.role > 0)
    def _():
        reduce_across(3)

    reduce_along(4)
    reduce_across(1)
    proj_grad()
    vector_grads()
    for b in range(images_here):

        @pl.when(at.role > 0)
        def _():
            pipe(1, b, gin, at.role - 1).wait_send()
            ship_start(1, b, back_shipped, grad_out_ref)

    reduce_across(2)
    reduce_across(0)
    for n in (3, 1, 2, 0):
        reduce_along(n)

    for b in range(images_here):
        ship_wait(0, b, shipped, result_out)
        ship_wait(1, b, back_shipped, grad_out_ref)
    for n in range(5):
        for slot in range(4):
            to_sibling(n, slot).wait_send()
        for k in range(2):
            to_across(n, k).wait_send()

            @pl.when(jnp.logical_not(at.is_self(k)))
            def _():
                to_owner(n, k).wait_send()
                from_other(n, k).wait_recv()

            @pl.when(at.is_self(k))
            def _():
                to_self(n, k).wait()


def run_block(replicas, sections, matrices, images, cotangent, counts, indices, vectors):
    images_here, patches = images.shape[:2]
    rows = images_here * patches
    hidden = matrices[2].shape[1]
    anywhere = pl.BlockSpec(memory_space=pl.ANY)
    vmem, dma = pltpu.VMEM, pltpu.SemaphoreType.DMA
    inside = pl.BlockSpec(memory_space=vmem)
    flat = [value.reshape(rows, D) for value in (images, cotangent)]
    shapes = [(SMALL_ROWS, LANES)] + [matrix.shape for matrix in matrices]
    kinds = [F32] + [LOW] * 4
    outs = [jax.ShapeDtypeStruct((rows, D), LOW)] * 2
    outs += [jax.ShapeDtypeStruct((2, *shape), kind) for shape, kind in zip(shapes, kinds)]

    def buffers(slots):
        return [vmem((slots, *shape), kind) for shape, kind in zip(shapes, kinds)]

    scratch = [vmem((GROUPS * shape[0], shape[1]), LOW) for shape in shapes]
    scratch += buffers(4) + buffers(2)
    scratch += [
        vmem((rows, D), LOW),
        vmem((rows, D), LOW),
        vmem((patches, D), LOW),
        vmem((rows, LANES), F32),
        vmem((images_here * 8, patches), F32),
        vmem((rows, 3 * D), LOW),
        vmem((images_here * H, patches, patches), LOW),
        vmem((rows, D), LOW),
        vmem((rows, D), F32),
        vmem((rows, D), LOW),
        vmem((rows, hidden), LOW),
        vmem((rows, hidden), LOW),
        vmem((rows, D), LOW),
        vmem((patches, D), F32),
        vmem((rows, D), LOW),
        vmem((rows, D), LOW),
        vmem((patches, D), LOW),
        vmem((rows, D), F32),
        vmem((8, 1, D), F32),
        vmem((1, 3 * D), F32),
        vmem((1, hidden), F32),
        vmem((8, 1, D), F32),
        vmem((1, 3 * D), F32),
        vmem((1, hidden), F32),
        vmem((GROUPS * SMALL_ROWS, LANES), F32),
        vmem(matrices[0].shape, LOW),
        vmem((SMALL_ROWS, LANES), LOW),
        vmem((images_here * 8, patches), F32),
        dma((sum(GATHER_PARTS), 8)),
        dma((sum(GATHER_PARTS), GROUPS)),
        dma((5, 8)),
        dma((5, 8)),
        dma((3,)),
        dma((3,)),
        dma((2, images_here)),
        dma((2, images_here)),
        dma((2, images_here)),
        dma((2, images_here)),
        dma,
        pltpu.SemaphoreType.REGULAR,
    ]
    results = pl.pallas_call(
        functools.partial(block_kernel, replicas, sections, images_here, patches),
        out_shape=outs,
        in_specs=[anywhere] * 6
        + [pl.BlockSpec(memory_space=pltpu.SMEM), inside]
        + [inside] * len(vectors),
        out_specs=[anywhere] * 7,
        scratch_shapes=scratch,
        compiler_params=pltpu.CompilerParams(
            collective_id=0, has_side_effects=True, vmem_limit_bytes=63 * 1024 * 1024
        ),
        name="block",
    )(*matrices, *flat, counts, indices, *vectors)
    outputs, input_grads = (value.reshape(images.shape).astype(F32) for value in results[:2])
    return outputs, input_grads, [value[0].astype(F32) + value[1].astype(F32) for value in results[2:]]


def unpack(block, sizes):
    found, start = [], 0
    for size in sizes:
        count = -(-size // LANES)
        found.append(block[start : start + count].reshape(-1)[:size])
        start += count
    return found


def local(images, cotangent, kept_count, kept_index, *weights):
    sections = lax.axis_size("section")
    replicas = lax.axis_size("dp") // GROUPS
    subgroups = [[g * replicas + r for r in range(replicas)] for g in range(GROUPS)]
    if replicas > 1:
        weights = tuple(
            lax.all_gather(value, "dp", axis=1, tiled=True, axis_index_groups=subgroups)
            for value in weights
        )
    matrices = [weights[n][0] for n in MATRICES]
    vectors = [weights[n] for n in VECTORS]
    outputs, input_grads, sums = run_block(
        replicas, sections, matrices, images, cotangent, kept_count, kept_index, vectors
    )
    grads = [None] * len(weights)
    for n, value in zip(MATRICES, sums[1:]):
        grads[n] = value
    for n, vector in zip(VECTORS, unpack(sums[0], [value.shape[1] for value in vectors])):
        grads[n] = vector
    if replicas > 1:
        grads = [
            lax.psum_scatter(
                value, "dp", scatter_dimension=0, tiled=True, axis_index_groups=subgroups
            )
            for value in grads
        ]
    return (outputs[None], input_grads[None], *(value[None] for value in grads))


def solution(mesh):
    in_specs = (
        P("dp", None, None),
        P("dp", None, None),
        P("dp"),
        P("dp", None),
        P("section", "dp"),
        P("section", "dp"),
        P("section", "dp", None),
        P("section", "dp"),
        P("section", "dp", None),
        P("section", "dp"),
        P("section", "dp"),
        P("section", "dp"),
        P("section", "dp", None),
        P("section", "dp"),
        P("section", "dp", None),
        P("section", "dp"),
        P("section", "dp"),
    )
    out_specs = (
        P("section", "dp", None, None),
        P("section", "dp", None, None),
        P("section", "dp"),
        P("section", "dp"),
        P("section", "dp", None),
        P("section", "dp"),
        P("section", "dp", None),
        P("section", "dp"),
        P("section", "dp"),
        P("section", "dp"),
        P("section", "dp", None),
        P("section", "dp"),
        P("section", "dp", None),
        P("section", "dp"),
        P("section", "dp"),
    )
    return jax.shard_map(local, mesh=mesh, in_specs=in_specs, out_specs=out_specs, check_vma=False)
```

```python
import functools
import math

import jax
import jax.numpy as jnp
from jax import lax
from jax.experimental import pallas as pl
from jax.experimental.pallas import tpu as pltpu
from jax.sharding import PartitionSpec as P

D = 768
H = 12
HD = 64
GRID = 16
GRID_BITS = 4
EPSILON = 1e-06
MASKED = -1e30
GROUPS = 8
LANES = 128
TILE = 768
CHUNK = 64
GRAD_TILE = 768
GATHER_PARTS = (1, 3, 1, 6, 6)
AHEAD = 3
REDUCE_PARTS = ((4, 3), (3, 3), (1, 3), (2, 1), (0, 1))
WINDOW = 3
FINISH_STEPS = 2
LAG = 3
MESH = pl.DeviceIdType.MESH
F32 = jnp.float32
LOW = jnp.bfloat16


class Place:
    def __init__(self, replicas):
        section = lax.axis_index("section")
        dp = lax.axis_index("dp")
        self.replicas = replicas
        self.x, self.core = lax.div(section, 2), lax.rem(section, 2)
        group, self.m = lax.div(dp, replicas), lax.rem(dp, replicas)
        self.z, self.y = lax.div(group, 2), lax.rem(group, 2)
        self.half, self.odd = lax.div(self.z, 2), lax.rem(self.z, 2)
        self.role = 2 * self.x + self.odd
        self.mine = 2 * self.z + self.y
        self.home = self.core == self.odd
        self.away = self.core != self.odd

    def device(self, x, core, z, y):
        return (2 * x + core, (2 * z + y) * self.replicas + self.m)

    def sibling(self):
        return self.device(self.x, 1 - self.core, self.z, self.y)

    def across(self):
        return self.device(self.x, self.core, self.z, 1 - self.y)

    def along(self, k):
        return self.device(self.x, self.odd, self.core + 2 * k, self.y)

    def twin(self):
        return self.along(self.half)

    def is_self(self, k):
        return jnp.logical_and(self.home, self.half == k)

    def section(self, role):
        return self.device(
            lax.div(role, 2), self.core, 2 * self.half + lax.rem(role, 2), self.y
        )


def remote(source, target, send, arrive, to):
    return pltpu.make_async_remote_copy(
        src_ref=source,
        dst_ref=target,
        send_sem=send,
        recv_sem=arrive,
        device_id=to,
        device_id_type=MESH,
    )


def enter(at, sections):
    barrier = pltpu.get_barrier_semaphore()

    def greet(to):
        pl.semaphore_signal(barrier, inc=1, device_id=to, device_id_type=MESH)

    greet(at.sibling())
    greet(at.across())
    for k in range(2):

        @pl.when(jnp.logical_not(at.is_self(k)))
        def _():
            greet(at.along(k))

    @pl.when(at.role > 0)
    def _():
        greet(at.section(at.role - 1))

    @pl.when(at.role < sections - 1)
    def _():
        greet(at.section(at.role + 1))

    ends = jnp.where(jnp.logical_or(at.role == 0, at.role == sections - 1), 1, 0)
    pl.semaphore_wait(barrier, 6 - jnp.where(at.home, 1, 0) - ends)


def span(start, size):
    return pl.ds(pl.multiple_of(start, size), size)


def dot(a, b):
    return jnp.dot(a, b, preferred_element_type=F32)


def dot_nt(a, b):
    return lax.dot_general(a, b, (((1,), (1,)), ((), ())), preferred_element_type=F32)


def dot_tn(a, b):
    return lax.dot_general(a, b, (((0,), (0,)), ((), ())), preferred_element_type=F32)


def gather_pieces(sizes):
    pieces = []
    for n, (size, parts) in enumerate(zip(sizes, GATHER_PARTS)):
        rows = size // parts
        pieces += [(n, start, rows) for start in range(0, size, rows)]
    return pieces


def reduce_pieces(sizes):
    pieces = []
    for n, parts in REDUCE_PARTS:
        rows = sizes[n] // parts
        pieces += [(n, start, rows) for start in range(0, sizes[n], rows)]
    return pieces


def loop(count, body, unroll=1):
    def step(i, carry):
        body(i)
        return carry

    lax.fori_loop(0, count, step, 0, unroll=unroll)


SMALL_ROWS = 16


def quotient(values, divisor):
    return jnp.floor((values + 0.5) * (1.0 / divisor))


def selectors(size, first_row, index):
    group = quotient(index, size)
    inside = index - group * size
    row_in = quotient(inside, LANES)
    lane = inside - row_in * LANES
    row = group * SMALL_ROWS + as_float(first_row) + row_in
    ids = lax.broadcasted_iota(jnp.int32, (GROUPS * SMALL_ROWS, index.shape[1]), 0).astype(F32)
    return (ids == row).astype(F32), (ids == lane).astype(F32)


def positions(count):
    return lax.broadcasted_iota(jnp.int32, (1, count), 1).astype(F32)


def as_float(value):
    return lax.convert_element_type(value, F32)


def spread_positions():
    at = positions(D)
    pair = quotient(at, 2 * HD)
    return at - quotient(at, HD) * HD + pair * HD


def paired_positions():
    at = positions(D)
    pair = quotient(at, 2 * HD)
    inside = at - pair * (2 * HD)
    half = quotient(inside, HD)
    rest = inside - half * HD
    head = quotient(rest, HD // 2)
    return pair * (2 * HD) + head * HD + half * (HD // 2) + rest - head * (HD // 2)


def expand(block, size, first_row, index):
    rows, lanes = selectors(size, first_row, index)
    values = dot(block, lanes.astype(LOW))
    return jnp.sum(values * rows, axis=0, keepdims=True)


def fold(vector, size, first_row, index):
    rows, lanes = selectors(size, first_row, index)
    return lax.dot_general(
        rows * vector,
        lanes,
        (((1,), (1,)), ((), ())),
        precision=lax.Precision.HIGHEST,
        preferred_element_type=F32,
    )


def normalise(values):
    mean = jnp.mean(values, axis=-1, keepdims=True)
    centred = values - mean
    variance = jnp.mean(centred * centred, axis=-1, keepdims=True)
    scale = lax.rsqrt(variance + EPSILON)
    return centred * scale, scale


def pairing():
    shape = (2 * HD, 2 * HD)
    source = lax.broadcasted_iota(jnp.int32, shape, 0)
    target = lax.broadcasted_iota(jnp.int32, shape, 1)
    half, head = lax.div(target, HD), lax.rem(lax.div(target, HD // 2), 2)
    return jnp.where(
        source == head * HD + half * (HD // 2) + lax.rem(target, HD // 2), 1.0, 0.0
    ).astype(LOW)


def lanes_of(shape):
    return lax.broadcasted_iota(jnp.int32, shape, 1)


def first_half(shape):
    return jnp.bitwise_and(lanes_of(shape), 2 * HD - 1) < HD


def partner(values):
    pieces = [
        pltpu.roll(values[:, start : start + 2 * HD], HD, 1)
        for start in range(0, values.shape[1], 2 * HD)
    ]
    return jnp.concatenate(pieces, axis=1) if len(pieces) > 1 else pieces[0]


def unfold_turn(table):
    first, other = first_half(table.shape), partner(table)
    return jnp.where(first, table, other), jnp.where(first, -other, table)


LOG2_E = 1.0 / math.log(2.0)


def gelu_pair(u):
    phi = 0.5 * (1.0 + lax.erf(u * math.sqrt(0.5)))
    density = jnp.exp2(u * u * (-0.5 * LOG2_E)) * (1.0 / math.sqrt(2.0 * math.pi))
    return u * phi, phi + u * density


MATRICES = (2, 4, 8, 10)
VECTORS = (0, 1, 5, 6, 7, 11, 12, 3, 9)

GAIN_ONE, SHIFT_ONE, PROJ_SHIFT, GAIN_TWO, SHIFT_TWO, DOWN_SHIFT, FREQ_ROW, FREQ_COL = range(8)


def block_kernel(replicas, sections, images_here, patches, *refs):
    ins, refs = refs[:8], refs[8:]
    given, refs = refs[: len(VECTORS)], refs[len(VECTORS) :]
    outs, refs = refs[:7], refs[7:]
    qkv_part, proj_part, up_part, down_part, images, cotangent, counts, indices = ins
    result_out, grad_out_ref = outs[:2]
    totals = outs[2:]
    (
        small_w, qkv_w, proj_w, up_w, down_w,
        first_0, first_1, first_2, first_3, first_4,
        second_0, second_1, second_2, second_3, second_4,
        xin, gin, gcopy, fcol, frow, qkv, probs, att, mid, n2, act, slope, g1, wide,
        shipped, back_shipped, gat, turns, vec, qkv_b, up_b, vec_g, qkv_bg, up_bg, small_f,
        qkv_own, small_own, facts_own,
        gather_send, gather_arrive, near_send, near_arrive,
        across_send, across_arrive, along_send, along_arrive,
        swap_send, swap_arrive, pipe_send, pipe_arrive, ship_send, ship_arrive, load, token,
    ) = refs
    wholes = (small_w, qkv_w, proj_w, up_w, down_w)
    shares = (small_own, qkv_own, proj_part, up_part, down_part)
    firsts = (first_0, first_1, first_2, first_3, first_4)
    seconds = (second_0, second_1, second_2, second_3, second_4)
    partials = (small_f, qkv_w, proj_w, up_w, down_w)
    at = Place(replicas)
    last = sections - 1
    q = D // GROUPS

    own_qkv = pltpu.make_async_copy(qkv_part, qkv_own, load)
    own_qkv.start()
    small_f[...] = jnp.zeros_like(small_f)
    row = 0
    for vector_ref in given:
        size = vector_ref.shape[1]
        for start in range(0, size, LANES):
            width = min(LANES, size - start)
            small_f[row : row + 1, 0:width] = vector_ref[:, start : start + width].astype(F32)
            row += 1
    small_own[...] = small_f[0:SMALL_ROWS, :].astype(LOW)
    facts_own[...] = jnp.zeros_like(facts_own)
    for b in range(images_here):
        slot = lax.broadcasted_iota(jnp.int32, (1, patches), 1)
        index = indices[b : b + 1, :]
        facts_own[8 * b : 8 * b + 1, :] = jnp.where(slot < counts[b], 1.0, 0.0)
        facts_own[8 * b + 1 : 8 * b + 2, :] = as_float(lax.shift_right_logical(index, GRID_BITS))
        facts_own[8 * b + 2 : 8 * b + 3, :] = as_float(jnp.bitwise_and(index, GRID - 1))
    own_qkv.wait()
    for block_no in range(2 * H // 2):
        cols = slice(block_no * 2 * HD, (block_no + 1) * 2 * HD)
        qkv_own[:, cols] = dot(qkv_own[:, cols], pairing()).astype(LOW)

    enter(at, sections)

    def swap_copy(n, source, target):
        return remote(source, target, swap_send.at[n], swap_arrive.at[n], at.twin())

    def swap_local(n, source, target):
        return pltpu.make_async_copy(source, target, swap_arrive.at[n])

    every = at.core >= 0
    moves = (
        (0, facts_own, frow, every, every),
        (
            1, images, xin,
            jnp.logical_and(at.x == 0, at.core == 0),
            at.role == 0,
        ),
        (
            2, cotangent, gin,
            jnp.logical_and(at.x == last // 2, at.core == last % 2),
            at.role == last,
        ),
    )

    def swap_start(n):
        number, source, target, sends, takes = moves[n]

        @pl.when(jnp.logical_and(sends, at.home))
        def _():
            swap_local(number, source, target).start()

        @pl.when(jnp.logical_and(sends, at.away))
        def _():
            swap_copy(number, source, target).start()

    def swap_wait(n):
        number, source, target, sends, takes = moves[n]

        @pl.when(jnp.logical_and(takes, at.home))
        def _():
            swap_local(number, source, target).wait()

        @pl.when(jnp.logical_and(takes, at.away))
        def _():
            swap_copy(number, source, target).wait_recv()

    def swap_sent(n):
        number, source, target, sends, takes = moves[n]

        @pl.when(jnp.logical_and(sends, at.away))
        def _():
            swap_copy(number, source, target).wait_send()

    pieces = gather_pieces([share.shape[0] for share in shares])

    def block_of(ref, group):
        size = ref.shape[0] // GROUPS
        return ref.at[span(group * size, size), :]

    def piece_of(i, group):
        n, start, size = pieces[i]
        first = group * (wholes[n].shape[0] // GROUPS) + start
        return wholes[n].at[pl.ds(pl.multiple_of(first, 16), size), :]

    def share_of(i):
        n, start, size = pieces[i]
        return shares[n].at[pl.ds(start, size), :]

    def along(i, k):
        return remote(
            share_of(i), piece_of(i, at.mine),
            gather_send.at[i, k], gather_arrive.at[i, at.mine], at.along(k),
        )

    def own(i):
        return pltpu.make_async_copy(
            share_of(i), piece_of(i, at.mine), gather_arrive.at[i, at.mine]
        )

    def relay(i, slot, group, to):
        block = piece_of(i, group)
        return remote(block, block, gather_send.at[i, slot], gather_arrive.at[i, group], to)

    def gather_start(i):
        for k in range(2):

            @pl.when(at.is_self(k))
            def _():
                own(i).start()

            @pl.when(jnp.logical_not(at.is_self(k)))
            def _():
                along(i, k).start()

    def gather_started(i):
        for k in range(2):

            @pl.when(jnp.logical_not(at.is_self(k)))
            def _():
                along(i, k).wait_send()

    def gather_relay(i):
        for k in range(2):
            group = 2 * (at.core + 2 * k) + at.y

            @pl.when(at.is_self(k))
            def _():
                own(i).wait()

            @pl.when(jnp.logical_not(at.is_self(k)))
            def _():
                relay(i, 2 + k, group, at.sibling()).wait_recv()

            relay(i, 4 + k, group, at.across()).start()
            relay(i, 2 + k, group, at.sibling()).start()

    def gather_pass(i):
        for k in range(2):
            group = 2 * (at.core + 2 * k) + 1 - at.y
            relay(i, 6 + k, group, at.sibling()).wait_recv()
            relay(i, 6 + k, group, at.sibling()).start()

    def gather_wait(i):
        for k in range(2):
            for row in range(2):
                group = 2 * (1 - at.core + 2 * k) + row
                relay(i, 2 + k, group, at.sibling()).wait_recv()

    def gather_sent(i):
        for k in range(2):
            group = 2 * (at.core + 2 * k) + at.y
            other = 2 * (at.core + 2 * k) + 1 - at.y
            relay(i, 2 + k, group, at.sibling()).wait_send()
            relay(i, 4 + k, group, at.across()).wait_send()
            relay(i, 6 + k, other, at.sibling()).wait_send()

    count = len(pieces)

    def gather_step(i):
        gather_relay(i)
        gather_started(i)
        if i + AHEAD < count:
            gather_start(i + AHEAD)

    swap_start(0)
    gather_start(0)
    swap_start(1)
    for i in range(1, AHEAD):
        gather_start(i)
    gather_step(0)
    swap_wait(0)
    gather_pass(0)
    gather_wait(0)
    for b in range(images_here):
        filled = jnp.concatenate(
            [frow[8 * b : 8 * b + 8, :], jnp.zeros((LANES - 8, patches), F32)], axis=0
        )
        fcol[b * patches : (b + 1) * patches, :] = jnp.transpose(filled)

    block = small_w[...]
    plain = positions(D)
    apart = spread_positions()
    paired = paired_positions()

    def qkv_positions(t):
        return jnp.where(t < 2, paired, plain) + as_float(t) * D

    def take_vector(row):
        vec[row] = expand(block, q, row, plain)

    def take_frequency(t):
        vec[FREQ_ROW + t] = expand(block, q, FREQ_ROW, apart + as_float(t) * (D // 2))

    def take_qkv(t):
        qkv_b[:, span(t * D, D)] = expand(block, 3 * q, 7, qkv_positions(t))

    def take_up(t):
        up_b[:, span(t * D, D)] = expand(block, 4 * q, 10, plain + as_float(t) * D)

    loop(FREQ_ROW, take_vector)
    loop(2, take_frequency)
    loop(3, take_qkv)
    loop(4, take_up)
    vec_g[...] = jnp.zeros_like(vec_g)
    qkv_bg[...] = jnp.zeros_like(qkv_bg)
    up_bg[...] = jnp.zeros_like(up_bg)

    def vector(row):
        return vec[row]

    def vector_at(row, cols):
        return vec[row, :, cols]

    def tables(b):
        rows = span(b * patches, patches)
        facts = fcol[rows, :]
        row_at, col_at = facts[:, 1:2], facts[:, 2:3]
        first = first_half((patches, TILE))

        def piece(t):
            cols = span(t * TILE, TILE)
            angle = row_at * vector_at(FREQ_ROW, cols) + col_at * vector_at(FREQ_COL, cols)
            turns[rows, cols] = jnp.where(first, jnp.cos(angle), jnp.sin(angle))

        loop(D // TILE, piece)

    def ship_start(n, b, source, target):
        rows = span(b * patches, patches)

        @pl.when(at.home)
        def _():
            ship_here(n, b, source, target).start()

        @pl.when(at.away)
        def _():
            ship_away(n, b, source, target).start()

    def ship_here(n, b, source, target):
        rows = span(b * patches, patches)
        return pltpu.make_async_copy(
            source.at[rows, :], target.at[rows, :], ship_arrive.at[n, b]
        )

    def ship_away(n, b, source, target):
        rows = span(b * patches, patches)
        return remote(
            source.at[rows, :], target.at[rows, :],
            ship_send.at[n, b], ship_arrive.at[n, b], at.twin(),
        )

    def ship_wait(n, b, source, target):
        @pl.when(at.home)
        def _():
            ship_here(n, b, source, target).wait()

        @pl.when(at.away)
        def _():
            ship_away(n, b, source, target).wait_recv()
            ship_away(n, b, source, target).wait_send()

    def pipe(n, b, target, role):
        rows = span(b * patches, patches)
        source = shipped if n == 0 else back_shipped
        return remote(
            source.at[rows, :], target.at[rows, :],
            pipe_send.at[n, b], pipe_arrive.at[n, b], at.section(role),
        )

    def chunks(b, body):
        loop(
            patches // CHUNK,
            lambda i: body(span(b * patches + i * CHUNK, CHUNK), span(i * CHUNK, CHUNK)),
            unroll=patches // CHUNK,
        )

    def own_lanes(e):
        inside = jnp.bitwise_and(lanes_of((patches, 2 * HD)), HD - 1) < HD // 2
        return inside if e == 0 else jnp.logical_not(inside)

    def value_lanes(e):
        inside = lanes_of((patches, 2 * HD)) < HD
        return inside if e == 0 else jnp.logical_not(inside)

    def rows_at(b):
        return span(b * patches, patches)

    def attention_inputs(b):
        rows = rows_at(b)

        def norm_one(here, inside):
            hat, _ = normalise(xin[here, :].astype(F32))
            shipped[here, :] = (hat * vector(GAIN_ONE) + vector(SHIFT_ONE)).astype(LOW)

        chunks(b, norm_one)

        def turn(t):
            cols = span(t * D, D)
            raw = dot(shipped[rows, :], qkv_w[:, cols]) + qkv_b[:, cols]
            cosine, sine = unfold_turn(turns[rows, :])
            turned = raw * cosine + partner(raw) * sine
            qkv[rows, cols] = turned.astype(LOW)

        loop(2, turn, unroll=2)
        cols = pl.ds(2 * D, D)
        qkv[rows, cols] = (dot(shipped[rows, :], qkv_w[:, cols]) + qkv_b[:, cols]).astype(LOW)

    def attention(b):
        rows = rows_at(b)
        barred = jnp.where(frow[span(b * 8, 8), :][0:1, :] > 0, 0.0, MASKED)

        def heads(pair):
            cols = span(pair * 2 * HD, 2 * HD)
            query = qkv[rows, cols]
            key = qkv[rows, span(D + pair * 2 * HD, 2 * HD)]
            value = qkv[rows, span(2 * D + pair * 2 * HD, 2 * HD)]
            value = jnp.concatenate([value, jnp.ones_like(value)], axis=1)
            found = []
            for e in range(2):
                own_query = jnp.where(own_lanes(e), query, jnp.zeros_like(query))
                scores = dot_nt(own_query, key) * (HD ** (-0.5) * LOG2_E) + barred
                powers = jnp.exp2(scores - jnp.max(scores, axis=1, keepdims=True))
                both = dot(powers.astype(LOW), value)
                share = 1.0 / both[:, 2 * HD :]
                probs[b * H + 2 * pair + e] = (
                    powers * jnp.concatenate([share] * (patches // (2 * HD)), axis=1)
                ).astype(LOW)
                found.append(both[:, : 2 * HD] * share)
            att[rows, cols] = jnp.where(value_lanes(0), found[0], found[1]).astype(LOW)

        loop(H // 2, heads, unroll=H // 2)

    def middle(b):
        rows = rows_at(b)
        keep_col = fcol[rows, :][:, 0:1]
        branch = dot(att[rows, :], proj_w[...]) + vector(PROJ_SHIFT)
        mid[rows, :] = xin[rows, :].astype(F32) + keep_col * branch

        def norm_two(here, inside):
            hat, _ = normalise(mid[here, :])
            n2[here, :] = (hat * vector(GAIN_TWO) + vector(SHIFT_TWO)).astype(LOW)

        chunks(b, norm_two)

    def raised(b):
        rows = rows_at(b)
        hidden = dot(n2[rows, :], up_w[...]) + up_b[...]
        value, gradient = gelu_pair(hidden)
        act[rows, :] = value.astype(LOW)
        slope[rows, :] = gradient.astype(LOW)

    def lowered(b):
        rows = rows_at(b)
        keep_col = fcol[rows, :][:, 0:1]
        branch = dot(act[rows, :], down_w[...]) + vector(DOWN_SHIFT)
        shipped[rows, :] = (mid[rows, :] + keep_col * branch).astype(LOW)

    def piece_range(n):
        return [i for i, piece in enumerate(pieces) if piece[0] == n]

    def ready(n):
        for i in piece_range(n):
            gather_wait(i)

    def section_zero(stages):
        @pl.when(at.role == 0)
        def _():
            for stage_now, b in stages:
                stage_now(b)

    slots = {}
    for step, stages in (
        (1, [(tables, 0)]),
        (2, [(tables, 1)]),
        (LAG + piece_range(1)[-1], [1, (attention_inputs, 0)]),
        (LAG + piece_range(1)[-1] + 1, [(attention_inputs, 1)]),
        (LAG + piece_range(1)[-1] + 2, [(attention, 0)]),
        (LAG + piece_range(1)[-1] + 3, [(attention, 1)]),
        (LAG + piece_range(1)[-1] + 4, [2, (middle, 0)]),
        (LAG + piece_range(1)[-1] + 5, [(middle, 1)]),
        (LAG + piece_range(3)[-1], [3, (raised, 0)]),
        (LAG + piece_range(3)[-1] + 2, [(raised, 1)]),
    ):
        slots.setdefault(step, []).extend(stages)
    for i in range(1, count + LAG):
        if i < count:
            gather_step(i)
        if 1 <= i - LAG:
            gather_pass(i - LAG)
        if i == piece_range(1)[-1]:
            swap_wait(1)
        for item in slots.get(i, []):
            if isinstance(item, int):
                ready(item)
            elif item[0] is tables:
                tables(item[1])
            else:
                section_zero([item])
    swap_start(2)
    ready(4)

    def pass_token():
        pl.semaphore_signal(token, inc=1, device_id=at.sibling(), device_id_type=MESH)

    def send_on(b):
        pipe(0, b, xin, at.role + 1).start()

    @pl.when(at.role == 0)
    def _():
        for b in range(images_here):
            lowered(b)

            @pl.when(jnp.logical_and(at.core == 0, b == 0))
            def _():
                send_on(b)

        for b in range(images_here):

            @pl.when(at.core == 0)
            def _():
                if b > 0:
                    pl.semaphore_wait(token, 1)
                    send_on(b)
                pipe(0, b, xin, at.role + 1).wait_send()
                pass_token()

            @pl.when(at.core == 1)
            def _():
                pl.semaphore_wait(token, 1)
                send_on(b)
                pipe(0, b, xin, at.role + 1).wait_send()
                if b < images_here - 1:
                    pass_token()

    @pl.when(at.role > 0)
    def _():
        def forward(b):
            pipe(0, b, xin, at.role - 1).wait_recv()
            for stage_now in (attention_inputs, attention, middle, raised, lowered):
                stage_now(b)

            @pl.when(at.role < last)
            def _():
                send_on(b)

        loop(images_here, forward)
        for b in range(images_here):

            @pl.when(at.role < last)
            def _():
                pipe(0, b, xin, at.role + 1).wait_send()

    for b in range(images_here):
        ship_start(0, b, shipped, result_out)
    swap_wait(2)
    for n in range(3):
        swap_sent(n)
    for i in range(count):
        gather_sent(i)

    def norm_back(values, gain_row, grad):
        hat, scale = normalise(values)
        vec_g[gain_row] += jnp.sum(grad * hat, axis=0, keepdims=True)
        vec_g[gain_row + 1] += jnp.sum(grad, axis=0, keepdims=True)
        inner = grad * vector(gain_row)
        along_hat = jnp.mean(inner * hat, axis=-1, keepdims=True)
        level = jnp.mean(inner, axis=-1, keepdims=True)
        return scale * (inner - level - hat * along_hat), hat

    def add_row(ref, cols, values):
        ref[:, cols] += jnp.sum(values.astype(F32), axis=0, keepdims=True)

    def hidden_back(b):
        rows = rows_at(b)

        def mask_coming(here, inside):
            coming = gin[here, :].astype(F32)
            gcopy[inside, :] = gin[here, :]
            grad_two = (coming * fcol[here, :][:, 0:1]).astype(LOW)
            gin[here, :] = grad_two
            vec_g[DOWN_SHIFT] += jnp.sum(grad_two.astype(F32), axis=0, keepdims=True)

        chunks(b, mask_coming)
        grad = dot_nt(gin[rows, :], down_w[...])
        low = (grad * slope[rows, :].astype(F32)).astype(LOW)
        slope[rows, :] = low
        up_bg[...] += jnp.sum(low.astype(F32), axis=0, keepdims=True)
        wide[...] = dot_nt(slope[rows, :], up_w[...])

    def middle_back(b):
        rows = rows_at(b)

        def norm_two_back(here, inside):
            part, _ = norm_back(mid[here, :], GAIN_TWO, wide[inside, :])
            grad_mid = gcopy[inside, :].astype(F32) + part
            mid[here, :] = grad_mid
            grad_one = (grad_mid * fcol[here, :][:, 0:1]).astype(LOW)
            g1[here, :] = grad_one
            vec_g[PROJ_SHIFT] += jnp.sum(grad_one.astype(F32), axis=0, keepdims=True)

        chunks(b, norm_two_back)
        gat[...] = dot_nt(g1[rows, :], proj_w[...]).astype(LOW)

    def attention_back(b):
        rows = rows_at(b)
        facts = fcol[rows, :]
        row_at, col_at = facts[:, 1:2], facts[:, 2:3]
        lane_from = lax.broadcasted_iota(jnp.int32, (4 * HD, 4 * HD), 0)
        lane_to = lax.broadcasted_iota(jnp.int32, (4 * HD, 4 * HD), 1)
        same = lax.rem(lax.div(lane_from, HD), 2) == lax.div(lane_to, 2 * HD)
        head_sums = jnp.where(same, 1.0, 0.0).astype(LOW)

        def heads(pair):
            cols = span(pair * 2 * HD, 2 * HD)
            key_cols = span(D + pair * 2 * HD, 2 * HD)
            value_cols = span(2 * D + pair * 2 * HD, 2 * HD)
            query, key, value = qkv[rows, cols], qkv[rows, key_cols], qkv[rows, value_cols]
            grad = gat[:, cols]
            product = grad.astype(F32) * att[rows, cols].astype(F32)
            high = product.astype(LOW)
            rest = (product - high.astype(F32)).astype(LOW)
            centres = dot(jnp.concatenate([high, rest], axis=1), head_sums)
            to_q, to_k, to_v = [], [], []
            for e in range(2):
                own_grad = jnp.where(value_lanes(e), grad, jnp.zeros_like(grad))
                soft_low = probs[b * H + 2 * pair + e]
                soft = soft_low.astype(F32)
                grad_soft = dot_nt(own_grad, value)
                centre = centres[:, e * 2 * HD : (e + 1) * 2 * HD]
                centre = jnp.concatenate([centre] * (patches // (2 * HD)), axis=1)
                grad_scores = (soft * (grad_soft - centre)).astype(LOW)
                to_q.append(dot(grad_scores, key))
                to_k.append(dot_tn(grad_scores, query))
                to_v.append(dot_tn(soft_low, grad))
            scale = HD ** (-0.5)
            turned_q = jnp.where(own_lanes(0), to_q[0], to_q[1]) * scale
            turned_k = jnp.where(own_lanes(0), to_k[0], to_k[1]) * scale
            grad_v = jnp.where(value_lanes(0), to_v[0], to_v[1]).astype(LOW)
            cosine, sine = unfold_turn(turns[rows, cols])
            other_q, other_k = partner(turned_q), partner(turned_k)
            sign = jnp.where(first_half((1, 2 * HD)), 1.0, -1.0)
            swing = sign * (other_q * query.astype(F32) + other_k * key.astype(F32))
            for n, place_at in enumerate((row_at, col_at)):
                vec_g[FREQ_ROW + n, :, cols] += jnp.sum(swing * place_at, axis=0, keepdims=True)
            grad_q = (turned_q * cosine - other_q * sine).astype(LOW)
            grad_k = (turned_k * cosine - other_k * sine).astype(LOW)
            for where, low in ((cols, grad_q), (key_cols, grad_k), (value_cols, grad_v)):
                qkv[rows, where] = low
                add_row(qkv_bg, where, low)

        loop(H // 2, heads, unroll=H // 2)

    def source_back(b):
        rows = rows_at(b)
        wide[...] = dot_nt(qkv[rows, :], qkv_w[...])

        def norm_one_back(here, inside):
            part, hat = norm_back(xin[here, :].astype(F32), GAIN_ONE, wide[inside, :])
            xin[here, :] = (hat * vector(GAIN_ONE) + vector(SHIFT_ONE)).astype(LOW)
            back_shipped[here, :] = (mid[here, :] + part).astype(LOW)

        chunks(b, norm_one_back)

        @pl.when(at.role > 0)
        def _():
            pipe(1, b, gin, at.role - 1).start()

        @pl.when(at.role == 0)
        def _():
            ship_start(1, b, back_shipped, grad_out_ref)

    def backward_wait(b):
        @pl.when(at.role < last)
        def _():
            pipe(1, b, gin, at.role + 1).wait_recv()

    parts = reduce_pieces([partial.shape[0] // GROUPS for partial in partials])

    def to_sibling(n, slot):
        k, other = slot % 2, slot < 2
        group = 2 * (1 - at.core + 2 * k) + (1 - at.y if other else at.y)
        return remote(
            block_of(partials[n], group), firsts[n].at[slot],
            near_send.at[n, slot], near_arrive.at[n, slot], at.sibling(),
        )

    def held(slot):
        k, other = slot % 2, slot < 2
        return 2 * (at.core + 2 * k) + (1 - at.y if other else at.y)

    def held_part(p, slot):
        n, start, size = parts[p]
        first = held(slot) * (partials[n].shape[0] // GROUPS) + start
        return partials[n].at[pl.ds(pl.multiple_of(first, 16), size), :]

    def to_across(p, k):
        n, start, size = parts[p]
        return remote(
            held_part(p, k), seconds[n].at[k, pl.ds(start, size), :],
            across_send.at[p, k], across_arrive.at[p, k], at.across(),
        )

    def landing(p, half):
        n, start, size = parts[p]
        return totals[n].at[half, pl.ds(start, size), :]

    def to_owner(p, k):
        return remote(
            held_part(p, 2 + k), landing(p, at.half),
            along_send.at[p, k], along_arrive.at[p, at.half], at.along(k),
        )

    def to_self(p, k):
        return pltpu.make_async_copy(
            held_part(p, 2 + k), landing(p, k), along_arrive.at[p, k]
        )

    def from_other(p, k):
        return remote(
            held_part(p, 2 + k), landing(p, k),
            along_send.at[p, k], along_arrive.at[p, k], at.along(k),
        )

    def add(p, slot, source, index):
        n, start, size = parts[p]
        ref = partials[n]
        base = held(slot) * (ref.shape[0] // GROUPS) + start
        step = 16

        def body(i):
            here = pl.ds(pl.multiple_of(base + i * step, step), step)
            there = pl.ds(pl.multiple_of(start + i * step, step), step)
            total = ref[here, :].astype(F32) + source[index, there, :].astype(F32)
            ref[here, :] = total.astype(ref.dtype)

        loop(size // step, body)

    def reduce_start(n):
        for slot in range(4):
            to_sibling(n, slot).start()

    def reduce_across(p):
        n, start, size = parts[p]
        if start == 0:
            for slot in range(4):
                to_sibling(n, slot).wait_recv()
        for slot in range(2):
            add(p, slot, firsts[n], slot)
        for k in range(2):
            if p >= WINDOW:
                to_across(p - WINDOW, k).wait_send()
            to_across(p, k).start()
        for slot in range(2, 4):
            add(p, slot, firsts[n], slot)

    def reduce_along(p):
        n, start, size = parts[p]
        for k in range(2):
            to_across(p, k).wait_recv()
            add(p, 2 + k, seconds[n], k)

            @pl.when(jnp.logical_not(at.is_self(k)))
            def _():
                to_owner(p, k).start()

            @pl.when(at.is_self(k))
            def _():
                to_self(p, k).start()

    def down_grad():
        def tile(t):
            cols = span(t * GRAD_TILE, GRAD_TILE)
            down_w[cols, :] = dot_tn(act[:, cols], gin[...]).astype(LOW)

        loop(down_w.shape[0] // GRAD_TILE, tile)
        reduce_start(4)

    def up_grad():
        def tile(t):
            cols = span(t * GRAD_TILE, GRAD_TILE)
            up_w[:, cols] = dot_tn(n2[...], slope[:, cols]).astype(LOW)

        loop(up_w.shape[1] // GRAD_TILE, tile)
        reduce_start(3)

    def proj_grad():
        proj_w[...] = dot_tn(att[...], g1[...]).astype(LOW)
        reduce_start(2)

    def qkv_grad():
        for block_no in range(2 * H // 2):
            cols = slice(block_no * 2 * HD, (block_no + 1) * 2 * HD)
            qkv[:, cols] = dot_nt(qkv[:, cols], pairing()).astype(LOW)

        def tile(t):
            cols = span(t * D, D)
            qkv_w[:, cols] = dot_tn(xin[...], qkv[:, cols]).astype(LOW)

        loop(qkv_w.shape[1] // D, tile)
        reduce_start(1)

    def vector_grads():
        small_f[...] = jnp.zeros_like(small_f)

        def give_vector(row):
            small_f[...] += fold(vec_g[row], q, row, plain)

        def give_frequency(t):
            small_f[...] += fold(vec_g[FREQ_ROW + t], q, FREQ_ROW, apart + as_float(t) * (D // 2))

        def give_qkv(t):
            small_f[...] += fold(qkv_bg[:, span(t * D, D)], 3 * q, 7, qkv_positions(t))

        def give_up(t):
            small_f[...] += fold(up_bg[:, span(t * D, D)], 4 * q, 10, plain + as_float(t) * D)

        loop(FREQ_ROW, give_vector)
        loop(2, give_frequency)
        loop(3, give_qkv)
        loop(4, give_up)
        reduce_start(0)

    stages = (hidden_back, middle_back, attention_back, source_back)

    def backward(b):
        backward_wait(b)
        for stage_now in stages:
            stage_now(b)

    loop(images_here - 1, backward)
    final = images_here - 1
    backward_wait(final)
    hidden_back(final)

    def early_grads():
        down_grad()
        reduce_across(0)
        up_grad()
        for p in range(1, WINDOW):
            reduce_across(p)

    @pl.when(at.role == 0)
    def _():
        early_grads()

    middle_back(final)
    attention_back(final)
    source_back(final)

    @pl.when(at.role > 0)
    def _():
        early_grads()

    qkv_grad()
    reduce_across(WINDOW)
    proj_grad()
    vector_grads()
    for b in range(images_here):

        @pl.when(at.role > 0)
        def _():
            pipe(1, b, gin, at.role - 1).wait_send()
            ship_start(1, b, back_shipped, grad_out_ref)

    for p in range(len(parts)):
        if p + WINDOW + 1 < len(parts):
            reduce_across(p + WINDOW + 1)
        reduce_along(p)

    for b in range(images_here):
        ship_wait(0, b, shipped, result_out)
        ship_wait(1, b, back_shipped, grad_out_ref)
    for n in range(5):
        for slot in range(4):
            to_sibling(n, slot).wait_send()
    for p in range(len(parts)):
        for k in range(2):
            if p >= len(parts) - WINDOW:
                to_across(p, k).wait_send()

            @pl.when(jnp.logical_not(at.is_self(k)))
            def _():
                to_owner(p, k).wait_send()
                from_other(p, k).wait_recv()

            @pl.when(at.is_self(k))
            def _():
                to_self(p, k).wait()


def run_block(replicas, sections, matrices, images, cotangent, counts, indices, vectors):
    images_here, patches = images.shape[:2]
    rows = images_here * patches
    hidden = matrices[2].shape[1]
    anywhere = pl.BlockSpec(memory_space=pl.ANY)
    vmem, dma = pltpu.VMEM, pltpu.SemaphoreType.DMA
    inside = pl.BlockSpec(memory_space=vmem)
    flat = [value.reshape(rows, D) for value in (images, cotangent)]
    shapes = [(SMALL_ROWS, LANES)] + [matrix.shape for matrix in matrices]
    kinds = [F32] + [LOW] * 4
    outs = [jax.ShapeDtypeStruct((rows, D), LOW)] * 2
    outs += [jax.ShapeDtypeStruct((2, *shape), kind) for shape, kind in zip(shapes, kinds)]

    reduce_count = sum(parts for _, parts in REDUCE_PARTS)

    def buffers(slots):
        return [vmem((slots, *shape), kind) for shape, kind in zip(shapes, kinds)]

    scratch = [vmem((GROUPS * shape[0], shape[1]), LOW) for shape in shapes]
    scratch += buffers(4) + buffers(2)
    scratch += [
        vmem((rows, D), LOW),
        vmem((rows, D), LOW),
        vmem((patches, D), LOW),
        vmem((rows, LANES), F32),
        vmem((images_here * 8, patches), F32),
        vmem((rows, 3 * D), LOW),
        vmem((images_here * H, patches, patches), LOW),
        vmem((rows, D), LOW),
        vmem((rows, D), F32),
        vmem((rows, D), LOW),
        vmem((rows, hidden), LOW),
        vmem((rows, hidden), LOW),
        vmem((rows, D), LOW),
        vmem((patches, D), F32),
        vmem((rows, D), LOW),
        vmem((rows, D), LOW),
        vmem((patches, D), LOW),
        vmem((rows, D), F32),
        vmem((8, 1, D), F32),
        vmem((1, 3 * D), F32),
        vmem((1, hidden), F32),
        vmem((8, 1, D), F32),
        vmem((1, 3 * D), F32),
        vmem((1, hidden), F32),
        vmem((GROUPS * SMALL_ROWS, LANES), F32),
        vmem(matrices[0].shape, LOW),
        vmem((SMALL_ROWS, LANES), LOW),
        vmem((images_here * 8, patches), F32),
        dma((sum(GATHER_PARTS), 8)),
        dma((sum(GATHER_PARTS), GROUPS)),
        dma((5, 4)),
        dma((5, 4)),
        dma((reduce_count, 2)),
        dma((reduce_count, 2)),
        dma((reduce_count, 2)),
        dma((reduce_count, 2)),
        dma((3,)),
        dma((3,)),
        dma((2, images_here)),
        dma((2, images_here)),
        dma((2, images_here)),
        dma((2, images_here)),
        dma,
        pltpu.SemaphoreType.REGULAR,
    ]
    results = pl.pallas_call(
        functools.partial(block_kernel, replicas, sections, images_here, patches),
        out_shape=outs,
        in_specs=[anywhere] * 6
        + [pl.BlockSpec(memory_space=pltpu.SMEM), inside]
        + [inside] * len(vectors),
        out_specs=[anywhere] * 7,
        scratch_shapes=scratch,
        compiler_params=pltpu.CompilerParams(
            collective_id=0, has_side_effects=True, vmem_limit_bytes=63 * 1024 * 1024
        ),
        name="block",
    )(*matrices, *flat, counts, indices, *vectors)
    finished = finish(results, [vector.shape[1] for vector in vectors])
    outputs, input_grads = (value.reshape(images.shape) for value in finished[:2])
    return outputs, input_grads, finished[2:6], finished[6:]


def finish_kernel(sizes, *refs):
    result, grad, small, *pairs = refs[:7]
    result_out, grad_out, *outs = refs[7:]
    result_out[...] = result[...].astype(F32)
    grad_out[...] = grad[...].astype(F32)
    for pair, out in zip(pairs, outs[:4]):
        out[...] = pair[0].astype(F32) + pair[1].astype(F32)

    @pl.when(pl.program_id(0) == 0)
    def _():
        row = 0
        for size, out in zip(sizes, outs[4:]):
            for start in range(0, size, LANES):
                width = min(LANES, size - start)
                out[:, start : start + width] = (
                    small[0, row : row + 1, 0:width] + small[1, row : row + 1, 0:width]
                )
                row += 1


def finish(values, sizes):
    steps = FINISH_STEPS
    rows = values[0].shape[0]
    whole = pl.BlockSpec((rows // steps, D), lambda i: (i, 0))
    ins, outs, shapes = [whole] * 2, [whole] * 2, [(rows, D)] * 2
    ins.append(pl.BlockSpec(values[2].shape, lambda i: (0, 0, 0)))
    for pair in values[3:]:
        _, size, width = pair.shape
        ins.append(pl.BlockSpec((2, size // steps, width), lambda i: (0, i, 0)))
        outs.append(pl.BlockSpec((size // steps, width), lambda i: (i, 0)))
        shapes.append((size, width))
    for size in sizes:
        outs.append(pl.BlockSpec((1, size), lambda i: (0, 0)))
        shapes.append((1, size))
    return pl.pallas_call(
        functools.partial(finish_kernel, sizes),
        grid=(steps,),
        out_shape=[jax.ShapeDtypeStruct(shape, F32) for shape in shapes],
        in_specs=ins,
        out_specs=outs,
        compiler_params=pltpu.CompilerParams(vmem_limit_bytes=63 * 1024 * 1024),
        name="finish",
    )(*values)


def local(images, cotangent, kept_count, kept_index, *weights):
    sections = lax.axis_size("section")
    replicas = lax.axis_size("dp") // GROUPS
    subgroups = [[g * replicas + r for r in range(replicas)] for g in range(GROUPS)]
    if replicas > 1:
        weights = tuple(
            lax.all_gather(value, "dp", axis=1, tiled=True, axis_index_groups=subgroups)
            for value in weights
        )
    matrices = [weights[n][0] for n in MATRICES]
    vectors = [weights[n] for n in VECTORS]
    outputs, input_grads, sums, vector_sums = run_block(
        replicas, sections, matrices, images, cotangent, kept_count, kept_index, vectors
    )
    grads = [None] * len(weights)
    for n, value in zip(MATRICES, sums):
        grads[n] = value
    for n, vector in zip(VECTORS, vector_sums):
        grads[n] = vector[0]
    if replicas > 1:
        grads = [
            lax.psum_scatter(
                value, "dp", scatter_dimension=0, tiled=True, axis_index_groups=subgroups
            )
            for value in grads
        ]
    return (outputs[None], input_grads[None], *(value[None] for value in grads))


def solution(mesh):
    in_specs = (
        P("dp", None, None),
        P("dp", None, None),
        P("dp"),
        P("dp", None),
        P("section", "dp"),
        P("section", "dp"),
        P("section", "dp", None),
        P("section", "dp"),
        P("section", "dp", None),
        P("section", "dp"),
        P("section", "dp"),
        P("section", "dp"),
        P("section", "dp", None),
        P("section", "dp"),
        P("section", "dp", None),
        P("section", "dp"),
        P("section", "dp"),
    )
    out_specs = (
        P("section", "dp", None, None),
        P("section", "dp", None, None),
        P("section", "dp"),
        P("section", "dp"),
        P("section", "dp", None),
        P("section", "dp"),
        P("section", "dp", None),
        P("section", "dp"),
        P("section", "dp"),
        P("section", "dp"),
        P("section", "dp", None),
        P("section", "dp"),
        P("section", "dp", None),
        P("section", "dp"),
        P("section", "dp"),
    )
    return jax.shard_map(local, mesh=mesh, in_specs=in_specs, out_specs=out_specs, check_vma=False)
```

```python
import functools
import math

import jax
import jax.numpy as jnp
from jax import lax
from jax.experimental import pallas as pl
from jax.experimental.pallas import tpu as pltpu
from jax.sharding import PartitionSpec as P

D = 768
H = 12
HD = 64
GRID = 16
GRID_BITS = 4
EPSILON = 1e-06
MASKED = -1e30
GROUPS = 8
LANES = 128
TILE = 768
CHUNK = 64
GRAD_TILE = 768
GATHER_PARTS = (1, 3, 1, 6, 6)
AHEAD = 3
REDUCE_PARTS = ((4, 3), (3, 3), (1, 3), (2, 1), (0, 1))
WINDOW = 3
FINISH_STEPS = 2
LAG = 3
MESH = pl.DeviceIdType.MESH
F32 = jnp.float32
LOW = jnp.bfloat16


class Place:
    def __init__(self, replicas):
        section = lax.axis_index("section")
        dp = lax.axis_index("dp")
        self.replicas = replicas
        self.x, self.core = lax.div(section, 2), lax.rem(section, 2)
        group, self.m = lax.div(dp, replicas), lax.rem(dp, replicas)
        self.z, self.y = lax.div(group, 2), lax.rem(group, 2)
        self.half, self.odd = lax.div(self.z, 2), lax.rem(self.z, 2)
        self.role = 2 * self.x + self.odd
        self.mine = 2 * self.z + self.y
        self.home = self.core == self.odd
        self.away = self.core != self.odd

    def device(self, x, core, z, y):
        return (2 * x + core, (2 * z + y) * self.replicas + self.m)

    def sibling(self):
        return self.device(self.x, 1 - self.core, self.z, self.y)

    def across(self):
        return self.device(self.x, self.core, self.z, 1 - self.y)

    def along(self, k):
        return self.device(self.x, self.odd, self.core + 2 * k, self.y)

    def twin(self):
        return self.along(self.half)

    def is_self(self, k):
        return jnp.logical_and(self.home, self.half == k)

    def section(self, role):
        return self.device(
            lax.div(role, 2), self.core, 2 * self.half + lax.rem(role, 2), self.y
        )


def remote(source, target, send, arrive, to):
    return pltpu.make_async_remote_copy(
        src_ref=source,
        dst_ref=target,
        send_sem=send,
        recv_sem=arrive,
        device_id=to,
        device_id_type=MESH,
    )


def enter(at, sections):
    barrier = pltpu.get_barrier_semaphore()

    def greet(to):
        pl.semaphore_signal(barrier, inc=1, device_id=to, device_id_type=MESH)

    greet(at.sibling())
    greet(at.across())
    for k in range(2):

        @pl.when(jnp.logical_not(at.is_self(k)))
        def _():
            greet(at.along(k))

    @pl.when(at.role > 0)
    def _():
        greet(at.section(at.role - 1))

    @pl.when(at.role < sections - 1)
    def _():
        greet(at.section(at.role + 1))

    ends = jnp.where(jnp.logical_or(at.role == 0, at.role == sections - 1), 1, 0)
    pl.semaphore_wait(barrier, 6 - jnp.where(at.home, 1, 0) - ends)


def span(start, size):
    return pl.ds(pl.multiple_of(start, size), size)


def dot(a, b):
    return jnp.dot(a, b, preferred_element_type=F32)


def dot_nt(a, b):
    return lax.dot_general(a, b, (((1,), (1,)), ((), ())), preferred_element_type=F32)


def dot_tn(a, b):
    return lax.dot_general(a, b, (((0,), (0,)), ((), ())), preferred_element_type=F32)


def gather_pieces(sizes):
    pieces = []
    for n, (size, parts) in enumerate(zip(sizes, GATHER_PARTS)):
        rows = size // parts
        pieces += [(n, start, rows) for start in range(0, size, rows)]
    return pieces


def reduce_pieces(sizes):
    pieces = []
    for n, parts in REDUCE_PARTS:
        rows = sizes[n] // parts
        pieces += [(n, start, rows) for start in range(0, sizes[n], rows)]
    return pieces


def loop(count, body, unroll=1):
    def step(i, carry):
        body(i)
        return carry

    lax.fori_loop(0, count, step, 0, unroll=unroll)


SMALL_ROWS = 16


def quotient(values, divisor):
    return jnp.floor((values + 0.5) * (1.0 / divisor))


def selectors(size, first_row, index):
    group = quotient(index, size)
    inside = index - group * size
    row_in = quotient(inside, LANES)
    lane = inside - row_in * LANES
    row = group * SMALL_ROWS + as_float(first_row) + row_in
    ids = lax.broadcasted_iota(jnp.int32, (GROUPS * SMALL_ROWS, index.shape[1]), 0).astype(F32)
    return (ids == row).astype(F32), (ids == lane).astype(F32)


def positions(count):
    return lax.broadcasted_iota(jnp.int32, (1, count), 1).astype(F32)


def as_float(value):
    return lax.convert_element_type(value, F32)


def spread_positions():
    at = positions(D)
    pair = quotient(at, 2 * HD)
    return at - quotient(at, HD) * HD + pair * HD


def paired_positions():
    at = positions(D)
    pair = quotient(at, 2 * HD)
    inside = at - pair * (2 * HD)
    half = quotient(inside, HD)
    rest = inside - half * HD
    head = quotient(rest, HD // 2)
    return pair * (2 * HD) + head * HD + half * (HD // 2) + rest - head * (HD // 2)


def expand(block, size, first_row, index):
    rows, lanes = selectors(size, first_row, index)
    values = dot(block, lanes.astype(LOW))
    return jnp.sum(values * rows, axis=0, keepdims=True)


def fold(vector, size, first_row, index):
    rows, lanes = selectors(size, first_row, index)
    return lax.dot_general(
        rows * vector,
        lanes,
        (((1,), (1,)), ((), ())),
        precision=lax.Precision.HIGHEST,
        preferred_element_type=F32,
    )


def normalise(values):
    mean = jnp.mean(values, axis=-1, keepdims=True)
    centred = values - mean
    variance = jnp.mean(centred * centred, axis=-1, keepdims=True)
    scale = lax.rsqrt(variance + EPSILON)
    return centred * scale, scale


def pairing():
    shape = (2 * HD, 2 * HD)
    source = lax.broadcasted_iota(jnp.int32, shape, 0)
    target = lax.broadcasted_iota(jnp.int32, shape, 1)
    half, head = lax.div(target, HD), lax.rem(lax.div(target, HD // 2), 2)
    return jnp.where(
        source == head * HD + half * (HD // 2) + lax.rem(target, HD // 2), 1.0, 0.0
    ).astype(LOW)


def lanes_of(shape):
    return lax.broadcasted_iota(jnp.int32, shape, 1)


def first_half(shape):
    return jnp.bitwise_and(lanes_of(shape), 2 * HD - 1) < HD


def partner(values):
    pieces = [
        pltpu.roll(values[:, start : start + 2 * HD], HD, 1)
        for start in range(0, values.shape[1], 2 * HD)
    ]
    return jnp.concatenate(pieces, axis=1) if len(pieces) > 1 else pieces[0]


def unfold_turn(table):
    first, other = first_half(table.shape), partner(table)
    return jnp.where(first, table, other), jnp.where(first, -other, table)


LOG2_E = 1.0 / math.log(2.0)


def gelu_pair(u):
    phi = 0.5 * (1.0 + lax.erf(u * math.sqrt(0.5)))
    density = jnp.exp2(u * u * (-0.5 * LOG2_E)) * (1.0 / math.sqrt(2.0 * math.pi))
    return u * phi, phi + u * density


MATRICES = (2, 4, 8, 10)
VECTORS = (0, 1, 5, 6, 7, 11, 12, 3, 9)

GAIN_ONE, SHIFT_ONE, PROJ_SHIFT, GAIN_TWO, SHIFT_TWO, DOWN_SHIFT, FREQ_ROW, FREQ_COL = range(8)


def block_kernel(replicas, sections, images_here, patches, *refs):
    ins, refs = refs[:8], refs[8:]
    given, refs = refs[: len(VECTORS)], refs[len(VECTORS) :]
    outs, refs = refs[:7], refs[7:]
    qkv_part, proj_part, up_part, down_part, images, cotangent, counts, indices = ins
    result_out, grad_out_ref = outs[:2]
    totals = outs[2:]
    (
        small_w, qkv_w, proj_w, up_w, down_w,
        first_0, first_1, first_2, first_3, first_4,
        second_0, second_1, second_2, second_3, second_4,
        xin, gin, gcopy, fcol, frow, qkv, probs, att, mid, n2, act, slope, g1, wide,
        shipped, back_shipped, gat, turns, vec, qkv_b, up_b, vec_g, qkv_bg, up_bg, small_f,
        qkv_own, small_own, facts_own,
        gather_send, gather_arrive, near_send, near_arrive,
        across_send, across_arrive, along_send, along_arrive,
        swap_send, swap_arrive, pipe_send, pipe_arrive, ship_send, ship_arrive, load, token,
    ) = refs
    wholes = (small_w, qkv_w, proj_w, up_w, down_w)
    shares = (small_own, qkv_own, proj_part, up_part, down_part)
    firsts = (first_0, first_1, first_2, first_3, first_4)
    seconds = (second_0, second_1, second_2, second_3, second_4)
    partials = (small_f, qkv_w, proj_w, up_w, down_w)
    at = Place(replicas)
    last = sections - 1
    q = D // GROUPS

    own_qkv = pltpu.make_async_copy(qkv_part, qkv_own, load)
    own_qkv.start()
    small_f[...] = jnp.zeros_like(small_f)
    row = 0
    for vector_ref in given:
        size = vector_ref.shape[1]
        for start in range(0, size, LANES):
            width = min(LANES, size - start)
            small_f[row : row + 1, 0:width] = vector_ref[:, start : start + width].astype(F32)
            row += 1
    small_own[...] = small_f[0:SMALL_ROWS, :].astype(LOW)
    facts_own[...] = jnp.zeros_like(facts_own)
    for b in range(images_here):
        slot = lax.broadcasted_iota(jnp.int32, (1, patches), 1)
        index = indices[b : b + 1, :]
        facts_own[8 * b : 8 * b + 1, :] = jnp.where(slot < counts[b], 1.0, 0.0)
        facts_own[8 * b + 1 : 8 * b + 2, :] = as_float(lax.shift_right_logical(index, GRID_BITS))
        facts_own[8 * b + 2 : 8 * b + 3, :] = as_float(jnp.bitwise_and(index, GRID - 1))
    own_qkv.wait()
    for block_no in range(2 * H // 2):
        cols = slice(block_no * 2 * HD, (block_no + 1) * 2 * HD)
        qkv_own[:, cols] = dot(qkv_own[:, cols], pairing()).astype(LOW)

    enter(at, sections)

    def swap_copy(n, source, target):
        return remote(source, target, swap_send.at[n], swap_arrive.at[n], at.twin())

    def swap_local(n, source, target):
        return pltpu.make_async_copy(source, target, swap_arrive.at[n])

    every = at.core >= 0
    moves = (
        (0, facts_own, frow, every, every),
        (
            1, images, xin,
            jnp.logical_and(at.x == 0, at.core == 0),
            at.role == 0,
        ),
        (
            2, cotangent, gin,
            jnp.logical_and(at.x == last // 2, at.core == last % 2),
            at.role == last,
        ),
    )

    def swap_start(n):
        number, source, target, sends, takes = moves[n]

        @pl.when(jnp.logical_and(sends, at.home))
        def _():
            swap_local(number, source, target).start()

        @pl.when(jnp.logical_and(sends, at.away))
        def _():
            swap_copy(number, source, target).start()

    def swap_wait(n):
        number, source, target, sends, takes = moves[n]

        @pl.when(jnp.logical_and(takes, at.home))
        def _():
            swap_local(number, source, target).wait()

        @pl.when(jnp.logical_and(takes, at.away))
        def _():
            swap_copy(number, source, target).wait_recv()

    def swap_sent(n):
        number, source, target, sends, takes = moves[n]

        @pl.when(jnp.logical_and(sends, at.away))
        def _():
            swap_copy(number, source, target).wait_send()

    pieces = gather_pieces([share.shape[0] for share in shares])

    def block_of(ref, group):
        size = ref.shape[0] // GROUPS
        return ref.at[span(group * size, size), :]

    def piece_of(i, group):
        n, start, size = pieces[i]
        first = group * (wholes[n].shape[0] // GROUPS) + start
        return wholes[n].at[pl.ds(pl.multiple_of(first, 16), size), :]

    def share_of(i):
        n, start, size = pieces[i]
        return shares[n].at[pl.ds(start, size), :]

    def along(i, k):
        return remote(
            share_of(i), piece_of(i, at.mine),
            gather_send.at[i, k], gather_arrive.at[i, at.mine], at.along(k),
        )

    def own(i):
        return pltpu.make_async_copy(
            share_of(i), piece_of(i, at.mine), gather_arrive.at[i, at.mine]
        )

    def relay(i, slot, group, to):
        block = piece_of(i, group)
        return remote(block, block, gather_send.at[i, slot], gather_arrive.at[i, group], to)

    def gather_start(i):
        for k in range(2):

            @pl.when(at.is_self(k))
            def _():
                own(i).start()

            @pl.when(jnp.logical_not(at.is_self(k)))
            def _():
                along(i, k).start()

    def gather_started(i):
        for k in range(2):

            @pl.when(jnp.logical_not(at.is_self(k)))
            def _():
                along(i, k).wait_send()

    def gather_relay(i):
        for k in range(2):
            group = 2 * (at.core + 2 * k) + at.y

            @pl.when(at.is_self(k))
            def _():
                own(i).wait()

            @pl.when(jnp.logical_not(at.is_self(k)))
            def _():
                relay(i, 2 + k, group, at.sibling()).wait_recv()

            relay(i, 4 + k, group, at.across()).start()
            relay(i, 2 + k, group, at.sibling()).start()

    def gather_pass(i):
        for k in range(2):
            group = 2 * (at.core + 2 * k) + 1 - at.y
            relay(i, 6 + k, group, at.sibling()).wait_recv()
            relay(i, 6 + k, group, at.sibling()).start()

    def gather_wait(i):
        for k in range(2):
            for row in range(2):
                group = 2 * (1 - at.core + 2 * k) + row
                relay(i, 2 + k, group, at.sibling()).wait_recv()

    def gather_sent(i):
        for k in range(2):
            group = 2 * (at.core + 2 * k) + at.y
            other = 2 * (at.core + 2 * k) + 1 - at.y
            relay(i, 2 + k, group, at.sibling()).wait_send()
            relay(i, 4 + k, group, at.across()).wait_send()
            relay(i, 6 + k, other, at.sibling()).wait_send()

    count = len(pieces)

    def gather_step(i):
        gather_relay(i)
        gather_started(i)
        if i + AHEAD < count:
            gather_start(i + AHEAD)

    swap_start(0)
    gather_start(0)
    swap_start(1)
    for i in range(1, AHEAD):
        gather_start(i)
    gather_step(0)
    swap_wait(0)
    gather_pass(0)
    gather_wait(0)
    for b in range(images_here):
        filled = jnp.concatenate(
            [frow[8 * b : 8 * b + 8, :], jnp.zeros((LANES - 8, patches), F32)], axis=0
        )
        fcol[b * patches : (b + 1) * patches, :] = jnp.transpose(filled)

    block = small_w[...]
    plain = positions(D)
    apart = spread_positions()
    paired = paired_positions()

    def qkv_positions(t):
        return jnp.where(t < 2, paired, plain) + as_float(t) * D

    def take_vector(row):
        vec[row] = expand(block, q, row, plain)

    def take_frequency(t):
        vec[FREQ_ROW + t] = expand(block, q, FREQ_ROW, apart + as_float(t) * (D // 2))

    def take_qkv(t):
        qkv_b[:, span(t * D, D)] = expand(block, 3 * q, 7, qkv_positions(t))

    def take_up(t):
        up_b[:, span(t * D, D)] = expand(block, 4 * q, 10, plain + as_float(t) * D)

    loop(FREQ_ROW, take_vector)
    loop(2, take_frequency)
    loop(3, take_qkv)
    loop(4, take_up)
    vec_g[...] = jnp.zeros_like(vec_g)
    qkv_bg[...] = jnp.zeros_like(qkv_bg)
    up_bg[...] = jnp.zeros_like(up_bg)

    def vector(row):
        return vec[row]

    def vector_at(row, cols):
        return vec[row, :, cols]

    def tables(b):
        rows = span(b * patches, patches)
        facts = fcol[rows, :]
        row_at, col_at = facts[:, 1:2], facts[:, 2:3]
        first = first_half((patches, TILE))

        def piece(t):
            cols = span(t * TILE, TILE)
            angle = row_at * vector_at(FREQ_ROW, cols) + col_at * vector_at(FREQ_COL, cols)
            turns[rows, cols] = jnp.where(first, jnp.cos(angle), jnp.sin(angle))

        loop(D // TILE, piece)

    def ship_start(n, b, source, target):
        rows = span(b * patches, patches)

        @pl.when(at.home)
        def _():
            ship_here(n, b, source, target).start()

        @pl.when(at.away)
        def _():
            ship_away(n, b, source, target).start()

    def ship_here(n, b, source, target):
        rows = span(b * patches, patches)
        return pltpu.make_async_copy(
            source.at[rows, :], target.at[rows, :], ship_arrive.at[n, b]
        )

    def ship_away(n, b, source, target):
        rows = span(b * patches, patches)
        return remote(
            source.at[rows, :], target.at[rows, :],
            ship_send.at[n, b], ship_arrive.at[n, b], at.twin(),
        )

    def ship_wait(n, b, source, target):
        @pl.when(at.home)
        def _():
            ship_here(n, b, source, target).wait()

        @pl.when(at.away)
        def _():
            ship_away(n, b, source, target).wait_recv()
            ship_away(n, b, source, target).wait_send()

    def pipe(n, b, target, role):
        rows = span(b * patches, patches)
        source = shipped if n == 0 else back_shipped
        return remote(
            source.at[rows, :], target.at[rows, :],
            pipe_send.at[n, b], pipe_arrive.at[n, b], at.section(role),
        )

    def chunks(b, body):
        loop(
            patches // CHUNK,
            lambda i: body(span(b * patches + i * CHUNK, CHUNK), span(i * CHUNK, CHUNK)),
            unroll=patches // CHUNK,
        )

    def own_lanes(e):
        inside = jnp.bitwise_and(lanes_of((patches, 2 * HD)), HD - 1) < HD // 2
        return inside if e == 0 else jnp.logical_not(inside)

    def value_lanes(e):
        inside = lanes_of((patches, 2 * HD)) < HD
        return inside if e == 0 else jnp.logical_not(inside)

    def rows_at(b):
        return span(b * patches, patches)

    def attention_inputs(b):
        rows = rows_at(b)

        def norm_one(here, inside):
            hat, _ = normalise(xin[here, :].astype(F32))
            shipped[here, :] = (hat * vector(GAIN_ONE) + vector(SHIFT_ONE)).astype(LOW)

        chunks(b, norm_one)

        def turn(t):
            cols = span(t * D, D)
            raw = dot(shipped[rows, :], qkv_w[:, cols]) + qkv_b[:, cols]
            cosine, sine = unfold_turn(turns[rows, :])
            turned = raw * cosine + partner(raw) * sine
            qkv[rows, cols] = turned.astype(LOW)

        loop(2, turn, unroll=2)
        cols = pl.ds(2 * D, D)
        qkv[rows, cols] = (dot(shipped[rows, :], qkv_w[:, cols]) + qkv_b[:, cols]).astype(LOW)

    def attention(b, unroll=H // 2):
        rows = rows_at(b)
        barred = jnp.where(frow[span(b * 8, 8), :][0:1, :] > 0, 0.0, MASKED)

        def heads(pair):
            cols = span(pair * 2 * HD, 2 * HD)
            query = qkv[rows, cols]
            key = qkv[rows, span(D + pair * 2 * HD, 2 * HD)]
            value = qkv[rows, span(2 * D + pair * 2 * HD, 2 * HD)]
            value = jnp.concatenate([value, jnp.ones_like(value)], axis=1)
            found = []
            for e in range(2):
                own_query = jnp.where(own_lanes(e), query, jnp.zeros_like(query))
                scores = dot_nt(own_query, key) * (HD ** (-0.5) * LOG2_E) + barred
                powers = jnp.exp2(scores - jnp.max(scores, axis=1, keepdims=True))
                both = dot(powers.astype(LOW), value)
                share = 1.0 / both[:, 2 * HD :]
                probs[b * H + 2 * pair + e] = (
                    powers * jnp.concatenate([share] * (patches // (2 * HD)), axis=1)
                ).astype(LOW)
                found.append(both[:, : 2 * HD] * share)
            att[rows, cols] = jnp.where(value_lanes(0), found[0], found[1]).astype(LOW)

        loop(H // 2, heads, unroll=unroll)

    def middle(b):
        rows = rows_at(b)
        keep_col = fcol[rows, :][:, 0:1]
        branch = dot(att[rows, :], proj_w[...]) + vector(PROJ_SHIFT)
        mid[rows, :] = xin[rows, :].astype(F32) + keep_col * branch

        def norm_two(here, inside):
            hat, _ = normalise(mid[here, :])
            n2[here, :] = (hat * vector(GAIN_TWO) + vector(SHIFT_TWO)).astype(LOW)

        chunks(b, norm_two)

    def raised(b, pieces_now=1):
        rows = rows_at(b)
        tile = up_w.shape[1] // pieces_now

        def part(t):
            cols = span(t * tile, tile)
            hidden = dot(n2[rows, :], up_w[:, cols]) + up_b[:, cols]
            value, gradient = gelu_pair(hidden)
            act[rows, cols] = value.astype(LOW)
            slope[rows, cols] = gradient.astype(LOW)

        if pieces_now == 1:
            part(0)
        else:
            loop(pieces_now, part)

    def lowered(b):
        rows = rows_at(b)
        keep_col = fcol[rows, :][:, 0:1]
        branch = dot(act[rows, :], down_w[...]) + vector(DOWN_SHIFT)
        shipped[rows, :] = (mid[rows, :] + keep_col * branch).astype(LOW)

    def piece_range(n):
        return [i for i, piece in enumerate(pieces) if piece[0] == n]

    def ready(n):
        for i in piece_range(n):
            gather_wait(i)

    def section_zero(stage_now):
        @pl.when(at.role == 0)
        def _():
            loop(images_here, stage_now)

    ready_qkv = LAG + piece_range(1)[-1]
    slots = {
        1: (None, tables),
        ready_qkv: (1, attention_inputs),
        ready_qkv + 2: (None, lambda b: attention(b, 3)),
        ready_qkv + 4: (2, middle),
        LAG + piece_range(3)[-1]: (3, lambda b: raised(b, 4)),
    }
    for i in range(1, count + LAG):
        if i < count:
            gather_step(i)
        if 1 <= i - LAG:
            gather_pass(i - LAG)
        if i == piece_range(1)[-1]:
            swap_wait(1)
        if i in slots:
            matrix, stage_now = slots[i]
            if matrix is not None:
                ready(matrix)
            if stage_now is tables:
                loop(images_here, tables)
            else:
                section_zero(stage_now)
    swap_start(2)
    ready(4)

    def pass_token():
        pl.semaphore_signal(token, inc=1, device_id=at.sibling(), device_id_type=MESH)

    def send_on(b):
        pipe(0, b, xin, at.role + 1).start()

    @pl.when(at.role == 0)
    def _():
        def lower_and_send(b):
            lowered(b)

            @pl.when(jnp.logical_and(at.core == 0, b == 0))
            def _():
                send_on(b)

        loop(images_here, lower_and_send)
        for b in range(images_here):

            @pl.when(at.core == 0)
            def _():
                if b > 0:
                    pl.semaphore_wait(token, 1)
                    send_on(b)
                pipe(0, b, xin, at.role + 1).wait_send()
                pass_token()

            @pl.when(at.core == 1)
            def _():
                pl.semaphore_wait(token, 1)
                send_on(b)
                pipe(0, b, xin, at.role + 1).wait_send()
                if b < images_here - 1:
                    pass_token()

    @pl.when(at.role > 0)
    def _():
        def forward(b):
            pipe(0, b, xin, at.role - 1).wait_recv()
            for stage_now in (attention_inputs, attention, middle, raised, lowered):
                stage_now(b)

            @pl.when(at.role < last)
            def _():
                send_on(b)

        loop(images_here, forward)
        for b in range(images_here):

            @pl.when(at.role < last)
            def _():
                pipe(0, b, xin, at.role + 1).wait_send()

    for b in range(images_here):
        ship_start(0, b, shipped, result_out)
    swap_wait(2)
    for n in range(3):
        swap_sent(n)
    for i in range(count):
        gather_sent(i)

    def norm_back(values, gain_row, grad):
        hat, scale = normalise(values)
        vec_g[gain_row] += jnp.sum(grad * hat, axis=0, keepdims=True)
        vec_g[gain_row + 1] += jnp.sum(grad, axis=0, keepdims=True)
        inner = grad * vector(gain_row)
        along_hat = jnp.mean(inner * hat, axis=-1, keepdims=True)
        level = jnp.mean(inner, axis=-1, keepdims=True)
        return scale * (inner - level - hat * along_hat), hat

    def add_row(ref, cols, values):
        ref[:, cols] += jnp.sum(values.astype(F32), axis=0, keepdims=True)

    def hidden_back(b):
        rows = rows_at(b)

        def mask_coming(here, inside):
            coming = gin[here, :].astype(F32)
            gcopy[inside, :] = gin[here, :]
            grad_two = (coming * fcol[here, :][:, 0:1]).astype(LOW)
            gin[here, :] = grad_two
            vec_g[DOWN_SHIFT] += jnp.sum(grad_two.astype(F32), axis=0, keepdims=True)

        chunks(b, mask_coming)
        grad = dot_nt(gin[rows, :], down_w[...])
        low = (grad * slope[rows, :].astype(F32)).astype(LOW)
        slope[rows, :] = low
        up_bg[...] += jnp.sum(low.astype(F32), axis=0, keepdims=True)
        wide[...] = dot_nt(slope[rows, :], up_w[...])

    def middle_back(b):
        rows = rows_at(b)

        def norm_two_back(here, inside):
            part, _ = norm_back(mid[here, :], GAIN_TWO, wide[inside, :])
            grad_mid = gcopy[inside, :].astype(F32) + part
            mid[here, :] = grad_mid
            grad_one = (grad_mid * fcol[here, :][:, 0:1]).astype(LOW)
            g1[here, :] = grad_one
            vec_g[PROJ_SHIFT] += jnp.sum(grad_one.astype(F32), axis=0, keepdims=True)

        chunks(b, norm_two_back)
        gat[...] = dot_nt(g1[rows, :], proj_w[...]).astype(LOW)

    def attention_back(b):
        rows = rows_at(b)
        facts = fcol[rows, :]
        row_at, col_at = facts[:, 1:2], facts[:, 2:3]
        lane_from = lax.broadcasted_iota(jnp.int32, (4 * HD, 4 * HD), 0)
        lane_to = lax.broadcasted_iota(jnp.int32, (4 * HD, 4 * HD), 1)
        same = lax.rem(lax.div(lane_from, HD), 2) == lax.div(lane_to, 2 * HD)
        head_sums = jnp.where(same, 1.0, 0.0).astype(LOW)

        def heads(pair):
            cols = span(pair * 2 * HD, 2 * HD)
            key_cols = span(D + pair * 2 * HD, 2 * HD)
            value_cols = span(2 * D + pair * 2 * HD, 2 * HD)
            query, key, value = qkv[rows, cols], qkv[rows, key_cols], qkv[rows, value_cols]
            grad = gat[:, cols]
            product = grad.astype(F32) * att[rows, cols].astype(F32)
            high = product.astype(LOW)
            rest = (product - high.astype(F32)).astype(LOW)
            centres = dot(jnp.concatenate([high, rest], axis=1), head_sums)
            to_q, to_k, to_v = [], [], []
            for e in range(2):
                own_grad = jnp.where(value_lanes(e), grad, jnp.zeros_like(grad))
                soft_low = probs[b * H + 2 * pair + e]
                soft = soft_low.astype(F32)
                grad_soft = dot_nt(own_grad, value)
                centre = centres[:, e * 2 * HD : (e + 1) * 2 * HD]
                centre = jnp.concatenate([centre] * (patches // (2 * HD)), axis=1)
                grad_scores = (soft * (grad_soft - centre)).astype(LOW)
                to_q.append(dot(grad_scores, key))
                to_k.append(dot_tn(grad_scores, query))
                to_v.append(dot_tn(soft_low, grad))
            scale = HD ** (-0.5)
            turned_q = jnp.where(own_lanes(0), to_q[0], to_q[1]) * scale
            turned_k = jnp.where(own_lanes(0), to_k[0], to_k[1]) * scale
            grad_v = jnp.where(value_lanes(0), to_v[0], to_v[1]).astype(LOW)
            cosine, sine = unfold_turn(turns[rows, cols])
            other_q, other_k = partner(turned_q), partner(turned_k)
            sign = jnp.where(first_half((1, 2 * HD)), 1.0, -1.0)
            swing = sign * (other_q * query.astype(F32) + other_k * key.astype(F32))
            for n, place_at in enumerate((row_at, col_at)):
                vec_g[FREQ_ROW + n, :, cols] += jnp.sum(swing * place_at, axis=0, keepdims=True)
            grad_q = (turned_q * cosine - other_q * sine).astype(LOW)
            grad_k = (turned_k * cosine - other_k * sine).astype(LOW)
            for where, low in ((cols, grad_q), (key_cols, grad_k), (value_cols, grad_v)):
                qkv[rows, where] = low
                add_row(qkv_bg, where, low)

        loop(H // 2, heads, unroll=H // 2)

    def source_back(b):
        rows = rows_at(b)
        wide[...] = dot_nt(qkv[rows, :], qkv_w[...])

        def norm_one_back(here, inside):
            part, hat = norm_back(xin[here, :].astype(F32), GAIN_ONE, wide[inside, :])
            xin[here, :] = (hat * vector(GAIN_ONE) + vector(SHIFT_ONE)).astype(LOW)
            back_shipped[here, :] = (mid[here, :] + part).astype(LOW)

        chunks(b, norm_one_back)

        @pl.when(at.role > 0)
        def _():
            pipe(1, b, gin, at.role - 1).start()

        @pl.when(at.role == 0)
        def _():
            ship_start(1, b, back_shipped, grad_out_ref)

    def backward_wait(b):
        @pl.when(at.role < last)
        def _():
            pipe(1, b, gin, at.role + 1).wait_recv()

    parts = reduce_pieces([partial.shape[0] // GROUPS for partial in partials])

    def to_sibling(n, slot):
        k, other = slot % 2, slot < 2
        group = 2 * (1 - at.core + 2 * k) + (1 - at.y if other else at.y)
        return remote(
            block_of(partials[n], group), firsts[n].at[slot],
            near_send.at[n, slot], near_arrive.at[n, slot], at.sibling(),
        )

    def held(slot):
        k, other = slot % 2, slot < 2
        return 2 * (at.core + 2 * k) + (1 - at.y if other else at.y)

    def held_part(p, slot):
        n, start, size = parts[p]
        first = held(slot) * (partials[n].shape[0] // GROUPS) + start
        return partials[n].at[pl.ds(pl.multiple_of(first, 16), size), :]

    def to_across(p, k):
        n, start, size = parts[p]
        return remote(
            held_part(p, k), seconds[n].at[k, pl.ds(start, size), :],
            across_send.at[p, k], across_arrive.at[p, k], at.across(),
        )

    def landing(p, half):
        n, start, size = parts[p]
        return totals[n].at[half, pl.ds(start, size), :]

    def to_owner(p, k):
        return remote(
            held_part(p, 2 + k), landing(p, at.half),
            along_send.at[p, k], along_arrive.at[p, at.half], at.along(k),
        )

    def to_self(p, k):
        return pltpu.make_async_copy(
            held_part(p, 2 + k), landing(p, k), along_arrive.at[p, k]
        )

    def from_other(p, k):
        return remote(
            held_part(p, 2 + k), landing(p, k),
            along_send.at[p, k], along_arrive.at[p, k], at.along(k),
        )

    def add(p, slot, source, index):
        n, start, size = parts[p]
        ref = partials[n]
        base = held(slot) * (ref.shape[0] // GROUPS) + start
        step = 16

        def body(i):
            here = pl.ds(pl.multiple_of(base + i * step, step), step)
            there = pl.ds(pl.multiple_of(start + i * step, step), step)
            total = ref[here, :].astype(F32) + source[index, there, :].astype(F32)
            ref[here, :] = total.astype(ref.dtype)

        loop(size // step, body)

    def reduce_start(n):
        for slot in range(4):
            to_sibling(n, slot).start()

    def reduce_across(p):
        n, start, size = parts[p]
        if start == 0:
            for slot in range(4):
                to_sibling(n, slot).wait_recv()
        for slot in range(2):
            add(p, slot, firsts[n], slot)
        for k in range(2):
            if p >= WINDOW:
                to_across(p - WINDOW, k).wait_send()
            to_across(p, k).start()
        for slot in range(2, 4):
            add(p, slot, firsts[n], slot)

    def reduce_along(p):
        n, start, size = parts[p]
        for k in range(2):
            to_across(p, k).wait_recv()
            add(p, 2 + k, seconds[n], k)

            @pl.when(jnp.logical_not(at.is_self(k)))
            def _():
                to_owner(p, k).start()

            @pl.when(at.is_self(k))
            def _():
                to_self(p, k).start()

    def down_grad(width):
        def tile(t):
            cols = span(t * width, width)
            down_w[cols, :] = dot_tn(act[:, cols], gin[...]).astype(LOW)

        loop(down_w.shape[0] // width, tile)
        reduce_start(4)

    def up_grad(width):
        def tile(t):
            cols = span(t * width, width)
            up_w[:, cols] = dot_tn(n2[...], slope[:, cols]).astype(LOW)

        loop(up_w.shape[1] // width, tile)
        reduce_start(3)

    def proj_grad():
        proj_w[...] = dot_tn(att[...], g1[...]).astype(LOW)
        reduce_start(2)

    def qkv_grad():
        for block_no in range(2 * H // 2):
            cols = slice(block_no * 2 * HD, (block_no + 1) * 2 * HD)
            qkv[:, cols] = dot_nt(qkv[:, cols], pairing()).astype(LOW)

        def tile(t):
            cols = span(t * D, D)
            qkv_w[:, cols] = dot_tn(xin[...], qkv[:, cols]).astype(LOW)

        loop(qkv_w.shape[1] // D, tile)
        reduce_start(1)

    def vector_grads():
        small_f[...] = jnp.zeros_like(small_f)

        def give_vector(row):
            small_f[...] += fold(vec_g[row], q, row, plain)

        def give_frequency(t):
            small_f[...] += fold(vec_g[FREQ_ROW + t], q, FREQ_ROW, apart + as_float(t) * (D // 2))

        def give_qkv(t):
            small_f[...] += fold(qkv_bg[:, span(t * D, D)], 3 * q, 7, qkv_positions(t))

        def give_up(t):
            small_f[...] += fold(up_bg[:, span(t * D, D)], 4 * q, 10, plain + as_float(t) * D)

        loop(FREQ_ROW, give_vector)
        loop(2, give_frequency)
        loop(3, give_qkv)
        loop(4, give_up)
        reduce_start(0)

    def early_grads(width):
        down_grad(width)
        reduce_across(0)
        up_grad(width)
        for p in range(1, WINDOW):
            reduce_across(p)

    def backward(b):
        backward_wait(b)
        hidden_back(b)

        @pl.when(jnp.logical_and(at.role == 0, b == images_here - 1))
        def _():
            early_grads(GRAD_TILE)

        middle_back(b)
        attention_back(b)
        source_back(b)

    loop(images_here, backward)

    @pl.when(at.role > 0)
    def _():
        early_grads(GRAD_TILE // 2)

    qkv_grad()
    reduce_across(WINDOW)
    proj_grad()
    vector_grads()
    for b in range(images_here):

        @pl.when(at.role > 0)
        def _():
            pipe(1, b, gin, at.role - 1).wait_send()
            ship_start(1, b, back_shipped, grad_out_ref)

    for p in range(len(parts)):
        if p + WINDOW + 1 < len(parts):
            reduce_across(p + WINDOW + 1)
        reduce_along(p)

    for b in range(images_here):
        ship_wait(0, b, shipped, result_out)
        ship_wait(1, b, back_shipped, grad_out_ref)
    for n in range(5):
        for slot in range(4):
            to_sibling(n, slot).wait_send()
    for p in range(len(parts)):
        for k in range(2):
            if p >= len(parts) - WINDOW:
                to_across(p, k).wait_send()

            @pl.when(jnp.logical_not(at.is_self(k)))
            def _():
                to_owner(p, k).wait_send()
                from_other(p, k).wait_recv()

            @pl.when(at.is_self(k))
            def _():
                to_self(p, k).wait()


def run_block(replicas, sections, matrices, images, cotangent, counts, indices, vectors):
    images_here, patches = images.shape[:2]
    rows = images_here * patches
    hidden = matrices[2].shape[1]
    anywhere = pl.BlockSpec(memory_space=pl.ANY)
    vmem, dma = pltpu.VMEM, pltpu.SemaphoreType.DMA
    inside = pl.BlockSpec(memory_space=vmem)
    flat = [value.reshape(rows, D) for value in (images, cotangent)]
    shapes = [(SMALL_ROWS, LANES)] + [matrix.shape for matrix in matrices]
    kinds = [F32] + [LOW] * 4
    outs = [jax.ShapeDtypeStruct((rows, D), LOW)] * 2
    outs += [jax.ShapeDtypeStruct((2, *shape), kind) for shape, kind in zip(shapes, kinds)]

    reduce_count = sum(parts for _, parts in REDUCE_PARTS)

    def buffers(slots):
        return [vmem((slots, *shape), kind) for shape, kind in zip(shapes, kinds)]

    scratch = [vmem((GROUPS * shape[0], shape[1]), LOW) for shape in shapes]
    scratch += buffers(4) + buffers(2)
    scratch += [
        vmem((rows, D), LOW),
        vmem((rows, D), LOW),
        vmem((patches, D), LOW),
        vmem((rows, LANES), F32),
        vmem((images_here * 8, patches), F32),
        vmem((rows, 3 * D), LOW),
        vmem((images_here * H, patches, patches), LOW),
        vmem((rows, D), LOW),
        vmem((rows, D), F32),
        vmem((rows, D), LOW),
        vmem((rows, hidden), LOW),
        vmem((rows, hidden), LOW),
        vmem((rows, D), LOW),
        vmem((patches, D), F32),
        vmem((rows, D), LOW),
        vmem((rows, D), LOW),
        vmem((patches, D), LOW),
        vmem((rows, D), F32),
        vmem((8, 1, D), F32),
        vmem((1, 3 * D), F32),
        vmem((1, hidden), F32),
        vmem((8, 1, D), F32),
        vmem((1, 3 * D), F32),
        vmem((1, hidden), F32),
        vmem((GROUPS * SMALL_ROWS, LANES), F32),
        vmem(matrices[0].shape, LOW),
        vmem((SMALL_ROWS, LANES), LOW),
        vmem((images_here * 8, patches), F32),
        dma((sum(GATHER_PARTS), 8)),
        dma((sum(GATHER_PARTS), GROUPS)),
        dma((5, 4)),
        dma((5, 4)),
        dma((reduce_count, 2)),
        dma((reduce_count, 2)),
        dma((reduce_count, 2)),
        dma((reduce_count, 2)),
        dma((3,)),
        dma((3,)),
        dma((2, images_here)),
        dma((2, images_here)),
        dma((2, images_here)),
        dma((2, images_here)),
        dma,
        pltpu.SemaphoreType.REGULAR,
    ]
    results = pl.pallas_call(
        functools.partial(block_kernel, replicas, sections, images_here, patches),
        out_shape=outs,
        in_specs=[anywhere] * 6
        + [pl.BlockSpec(memory_space=pltpu.SMEM), inside]
        + [inside] * len(vectors),
        out_specs=[anywhere] * 7,
        scratch_shapes=scratch,
        compiler_params=pltpu.CompilerParams(
            collective_id=0, has_side_effects=True, vmem_limit_bytes=63 * 1024 * 1024
        ),
        name="block",
    )(*matrices, *flat, counts, indices, *vectors)
    finished = finish(results, [vector.shape[1] for vector in vectors])
    outputs, input_grads = (value.reshape(images.shape) for value in finished[:2])
    return outputs, input_grads, finished[2:6], finished[6:]


def finish_kernel(sizes, *refs):
    result, grad, small, *pairs = refs[:7]
    result_out, grad_out, *outs = refs[7:]
    result_out[...] = result[...].astype(F32)
    grad_out[...] = grad[...].astype(F32)
    for pair, out in zip(pairs, outs[:4]):
        out[...] = pair[0].astype(F32) + pair[1].astype(F32)

    @pl.when(pl.program_id(0) == 0)
    def _():
        row = 0
        for size, out in zip(sizes, outs[4:]):
            for start in range(0, size, LANES):
                width = min(LANES, size - start)
                out[:, start : start + width] = (
                    small[0, row : row + 1, 0:width] + small[1, row : row + 1, 0:width]
                )
                row += 1


def finish(values, sizes):
    steps = FINISH_STEPS
    rows = values[0].shape[0]
    whole = pl.BlockSpec((rows // steps, D), lambda i: (i, 0))
    ins, outs, shapes = [whole] * 2, [whole] * 2, [(rows, D)] * 2
    ins.append(pl.BlockSpec(values[2].shape, lambda i: (0, 0, 0)))
    for pair in values[3:]:
        _, size, width = pair.shape
        ins.append(pl.BlockSpec((2, size // steps, width), lambda i: (0, i, 0)))
        outs.append(pl.BlockSpec((size // steps, width), lambda i: (i, 0)))
        shapes.append((size, width))
    for size in sizes:
        outs.append(pl.BlockSpec((1, size), lambda i: (0, 0)))
        shapes.append((1, size))
    return pl.pallas_call(
        functools.partial(finish_kernel, sizes),
        grid=(steps,),
        out_shape=[jax.ShapeDtypeStruct(shape, F32) for shape in shapes],
        in_specs=ins,
        out_specs=outs,
        compiler_params=pltpu.CompilerParams(vmem_limit_bytes=63 * 1024 * 1024),
        name="finish",
    )(*values)


def local(images, cotangent, kept_count, kept_index, *weights):
    sections = lax.axis_size("section")
    replicas = lax.axis_size("dp") // GROUPS
    subgroups = [[g * replicas + r for r in range(replicas)] for g in range(GROUPS)]
    if replicas > 1:
        weights = tuple(
            lax.all_gather(value, "dp", axis=1, tiled=True, axis_index_groups=subgroups)
            for value in weights
        )
    matrices = [weights[n][0] for n in MATRICES]
    vectors = [weights[n] for n in VECTORS]
    outputs, input_grads, sums, vector_sums = run_block(
        replicas, sections, matrices, images, cotangent, kept_count, kept_index, vectors
    )
    grads = [None] * len(weights)
    for n, value in zip(MATRICES, sums):
        grads[n] = value
    for n, vector in zip(VECTORS, vector_sums):
        grads[n] = vector[0]
    if replicas > 1:
        grads = [
            lax.psum_scatter(
                value, "dp", scatter_dimension=0, tiled=True, axis_index_groups=subgroups
            )
            for value in grads
        ]
    return (outputs[None], input_grads[None], *(value[None] for value in grads))


def solution(mesh):
    in_specs = (
        P("dp", None, None),
        P("dp", None, None),
        P("dp"),
        P("dp", None),
        P("section", "dp"),
        P("section", "dp"),
        P("section", "dp", None),
        P("section", "dp"),
        P("section", "dp", None),
        P("section", "dp"),
        P("section", "dp"),
        P("section", "dp"),
        P("section", "dp", None),
        P("section", "dp"),
        P("section", "dp", None),
        P("section", "dp"),
        P("section", "dp"),
    )
    out_specs = (
        P("section", "dp", None, None),
        P("section", "dp", None, None),
        P("section", "dp"),
        P("section", "dp"),
        P("section", "dp", None),
        P("section", "dp"),
        P("section", "dp", None),
        P("section", "dp"),
        P("section", "dp"),
        P("section", "dp"),
        P("section", "dp", None),
        P("section", "dp"),
        P("section", "dp", None),
        P("section", "dp"),
        P("section", "dp"),
    )
    return jax.shard_map(local, mesh=mesh, in_specs=in_specs, out_specs=out_specs, check_vma=False)
```

```python
import functools
import math

import jax
import jax.numpy as jnp
from jax import lax
from jax.experimental import pallas as pl
from jax.experimental.pallas import tpu as pltpu
from jax.sharding import PartitionSpec as P

D = 768
H = 12
HD = 64
GRID = 16
GRID_BITS = 4
EPSILON = 1e-06
MASKED = -1e30
GROUPS = 8
LANES = 128
TILE = 768
CHUNK = 64
GRAD_TILE = 768
GATHER_PARTS = (1, 3, 1, 6, 6)
AHEAD = 3
REDUCE_PARTS = ((4, 3), (3, 3), (1, 3), (2, 1), (0, 1))
WINDOW = 3
FINISH_STEPS = 2
LAG = 3
MESH = pl.DeviceIdType.MESH
F32 = jnp.float32
LOW = jnp.bfloat16


class Place:
    def __init__(self, replicas):
        section = lax.axis_index("section")
        dp = lax.axis_index("dp")
        self.replicas = replicas
        self.x, self.core = lax.div(section, 2), lax.rem(section, 2)
        group, self.m = lax.div(dp, replicas), lax.rem(dp, replicas)
        self.z, self.y = lax.div(group, 2), lax.rem(group, 2)
        self.half, self.odd = lax.div(self.z, 2), lax.rem(self.z, 2)
        self.role = 2 * self.x + self.odd
        self.mine = 2 * self.z + self.y
        self.home = self.core == self.odd
        self.away = self.core != self.odd

    def device(self, x, core, z, y):
        return (2 * x + core, (2 * z + y) * self.replicas + self.m)

    def sibling(self):
        return self.device(self.x, 1 - self.core, self.z, self.y)

    def across(self):
        return self.device(self.x, self.core, self.z, 1 - self.y)

    def along(self, k):
        return self.device(self.x, self.odd, self.core + 2 * k, self.y)

    def twin(self):
        return self.along(self.half)

    def is_self(self, k):
        return jnp.logical_and(self.home, self.half == k)

    def section(self, role):
        return self.device(
            lax.div(role, 2), self.core, 2 * self.half + lax.rem(role, 2), self.y
        )


def remote(source, target, send, arrive, to):
    return pltpu.make_async_remote_copy(
        src_ref=source,
        dst_ref=target,
        send_sem=send,
        recv_sem=arrive,
        device_id=to,
        device_id_type=MESH,
    )


def enter(at, sections):
    barrier = pltpu.get_barrier_semaphore()

    def greet(to):
        pl.semaphore_signal(barrier, inc=1, device_id=to, device_id_type=MESH)

    greet(at.sibling())
    greet(at.across())
    for k in range(2):

        @pl.when(jnp.logical_not(at.is_self(k)))
        def _():
            greet(at.along(k))

    @pl.when(at.role > 0)
    def _():
        greet(at.section(at.role - 1))

    @pl.when(at.role < sections - 1)
    def _():
        greet(at.section(at.role + 1))

    ends = jnp.where(jnp.logical_or(at.role == 0, at.role == sections - 1), 1, 0)
    pl.semaphore_wait(barrier, 6 - jnp.where(at.home, 1, 0) - ends)


def span(start, size):
    return pl.ds(pl.multiple_of(start, size), size)


def dot(a, b):
    return jnp.dot(a, b, preferred_element_type=F32)


def dot_nt(a, b):
    return lax.dot_general(a, b, (((1,), (1,)), ((), ())), preferred_element_type=F32)


def dot_tn(a, b):
    return lax.dot_general(a, b, (((0,), (0,)), ((), ())), preferred_element_type=F32)


def gather_pieces(sizes):
    pieces = []
    for n, (size, parts) in enumerate(zip(sizes, GATHER_PARTS)):
        rows = size // parts
        pieces += [(n, start, rows) for start in range(0, size, rows)]
    return pieces


def reduce_pieces(sizes):
    pieces = []
    for n, parts in REDUCE_PARTS:
        rows = sizes[n] // parts
        pieces += [(n, start, rows) for start in range(0, sizes[n], rows)]
    return pieces


def loop(count, body, unroll=1):
    def step(i, carry):
        body(i)
        return carry

    lax.fori_loop(0, count, step, 0, unroll=unroll)


SMALL_ROWS = 16


def quotient(values, divisor):
    return jnp.floor((values + 0.5) * (1.0 / divisor))


def selectors(size, first_row, index):
    group = quotient(index, size)
    inside = index - group * size
    row_in = quotient(inside, LANES)
    lane = inside - row_in * LANES
    row = group * SMALL_ROWS + as_float(first_row) + row_in
    ids = lax.broadcasted_iota(jnp.int32, (GROUPS * SMALL_ROWS, index.shape[1]), 0).astype(F32)
    return (ids == row).astype(F32), (ids == lane).astype(F32)


def positions(count):
    return lax.broadcasted_iota(jnp.int32, (1, count), 1).astype(F32)


def as_float(value):
    return lax.convert_element_type(value, F32)


def spread_positions():
    at = positions(D)
    pair = quotient(at, 2 * HD)
    return at - quotient(at, HD) * HD + pair * HD


def paired_positions():
    at = positions(D)
    pair = quotient(at, 2 * HD)
    inside = at - pair * (2 * HD)
    half = quotient(inside, HD)
    rest = inside - half * HD
    head = quotient(rest, HD // 2)
    return pair * (2 * HD) + head * HD + half * (HD // 2) + rest - head * (HD // 2)


def expand(block, size, first_row, index):
    rows, lanes = selectors(size, first_row, index)
    values = dot(block, lanes.astype(LOW))
    return jnp.sum(values * rows, axis=0, keepdims=True)


def fold(vector, size, first_row, index):
    rows, lanes = selectors(size, first_row, index)
    return lax.dot_general(
        rows * vector,
        lanes,
        (((1,), (1,)), ((), ())),
        precision=lax.Precision.HIGHEST,
        preferred_element_type=F32,
    )


def normalise(values):
    mean = jnp.mean(values, axis=-1, keepdims=True)
    centred = values - mean
    variance = jnp.mean(centred * centred, axis=-1, keepdims=True)
    scale = lax.rsqrt(variance + EPSILON)
    return centred * scale, scale


def pairing():
    shape = (2 * HD, 2 * HD)
    source = lax.broadcasted_iota(jnp.int32, shape, 0)
    target = lax.broadcasted_iota(jnp.int32, shape, 1)
    half, head = lax.div(target, HD), lax.rem(lax.div(target, HD // 2), 2)
    return jnp.where(
        source == head * HD + half * (HD // 2) + lax.rem(target, HD // 2), 1.0, 0.0
    ).astype(LOW)


def lanes_of(shape):
    return lax.broadcasted_iota(jnp.int32, shape, 1)


def first_half(shape):
    return jnp.bitwise_and(lanes_of(shape), 2 * HD - 1) < HD


def partner(values):
    pieces = [
        pltpu.roll(values[:, start : start + 2 * HD], HD, 1)
        for start in range(0, values.shape[1], 2 * HD)
    ]
    return jnp.concatenate(pieces, axis=1) if len(pieces) > 1 else pieces[0]


def unfold_turn(table):
    first, other = first_half(table.shape), partner(table)
    return jnp.where(first, table, other), jnp.where(first, -other, table)


LOG2_E = 1.0 / math.log(2.0)


def gelu_pair(u):
    phi = 0.5 * (1.0 + lax.erf(u * math.sqrt(0.5)))
    density = jnp.exp2(u * u * (-0.5 * LOG2_E)) * (1.0 / math.sqrt(2.0 * math.pi))
    return u * phi, phi + u * density


MATRICES = (2, 4, 8, 10)
VECTORS = (0, 1, 5, 6, 7, 11, 12, 3, 9)

GAIN_ONE, SHIFT_ONE, PROJ_SHIFT, GAIN_TWO, SHIFT_TWO, DOWN_SHIFT, FREQ_ROW, FREQ_COL = range(8)


def block_kernel(replicas, sections, images_here, patches, *refs):
    ins, refs = refs[:8], refs[8:]
    given, refs = refs[: len(VECTORS)], refs[len(VECTORS) :]
    outs, refs = refs[:7], refs[7:]
    qkv_part, proj_part, up_part, down_part, images, cotangent, counts, indices = ins
    result_out, grad_out_ref = outs[:2]
    totals = outs[2:]
    (
        small_w, qkv_w, proj_w, up_w, down_w,
        first_0, first_1, first_2, first_3, first_4,
        second_0, second_1, second_2, second_3, second_4,
        xin, gin, gcopy, fcol, frow, qkv, probs, att, mid, n2, act, slope, g1, wide,
        shipped, back_shipped, gat, turns, vec, qkv_b, up_b, vec_g, qkv_bg, up_bg, small_f,
        qkv_own, small_own, facts_own,
        gather_send, gather_arrive, near_send, near_arrive,
        across_send, across_arrive, along_send, along_arrive,
        swap_send, swap_arrive, pipe_send, pipe_arrive, ship_send, ship_arrive, load, token,
    ) = refs
    wholes = (small_w, qkv_w, proj_w, up_w, down_w)
    shares = (small_own, qkv_own, proj_part, up_part, down_part)
    firsts = (first_0, first_1, first_2, first_3, first_4)
    seconds = (second_0, second_1, second_2, second_3, second_4)
    partials = (small_f, qkv_w, proj_w, up_w, down_w)
    at = Place(replicas)
    last = sections - 1
    q = D // GROUPS

    own_qkv = pltpu.make_async_copy(qkv_part, qkv_own, load)
    own_qkv.start()
    small_f[...] = jnp.zeros_like(small_f)
    row = 0
    for vector_ref in given:
        size = vector_ref.shape[1]
        for start in range(0, size, LANES):
            width = min(LANES, size - start)
            small_f[row : row + 1, 0:width] = vector_ref[:, start : start + width].astype(F32)
            row += 1
    small_own[...] = small_f[0:SMALL_ROWS, :].astype(LOW)
    facts_own[...] = jnp.zeros_like(facts_own)
    for b in range(images_here):
        slot = lax.broadcasted_iota(jnp.int32, (1, patches), 1)
        index = indices[b : b + 1, :]
        facts_own[8 * b : 8 * b + 1, :] = jnp.where(slot < counts[b], 1.0, 0.0)
        facts_own[8 * b + 1 : 8 * b + 2, :] = as_float(lax.shift_right_logical(index, GRID_BITS))
        facts_own[8 * b + 2 : 8 * b + 3, :] = as_float(jnp.bitwise_and(index, GRID - 1))
    own_qkv.wait()
    for block_no in range(2 * H // 2):
        cols = slice(block_no * 2 * HD, (block_no + 1) * 2 * HD)
        qkv_own[:, cols] = dot(qkv_own[:, cols], pairing()).astype(LOW)

    enter(at, sections)

    def swap_copy(n, source, target):
        return remote(source, target, swap_send.at[n], swap_arrive.at[n], at.twin())

    def swap_local(n, source, target):
        return pltpu.make_async_copy(source, target, swap_arrive.at[n])

    every = at.core >= 0
    moves = (
        (0, facts_own, frow, every, every),
        (
            1, images, xin,
            jnp.logical_and(at.x == 0, at.core == 0),
            at.role == 0,
        ),
        (
            2, cotangent, gin,
            jnp.logical_and(at.x == last // 2, at.core == last % 2),
            at.role == last,
        ),
    )

    def swap_start(n):
        number, source, target, sends, takes = moves[n]

        @pl.when(jnp.logical_and(sends, at.home))
        def _():
            swap_local(number, source, target).start()

        @pl.when(jnp.logical_and(sends, at.away))
        def _():
            swap_copy(number, source, target).start()

    def swap_wait(n):
        number, source, target, sends, takes = moves[n]

        @pl.when(jnp.logical_and(takes, at.home))
        def _():
            swap_local(number, source, target).wait()

        @pl.when(jnp.logical_and(takes, at.away))
        def _():
            swap_copy(number, source, target).wait_recv()

    def swap_sent(n):
        number, source, target, sends, takes = moves[n]

        @pl.when(jnp.logical_and(sends, at.away))
        def _():
            swap_copy(number, source, target).wait_send()

    pieces = gather_pieces([share.shape[0] for share in shares])

    def block_of(ref, group):
        size = ref.shape[0] // GROUPS
        return ref.at[span(group * size, size), :]

    def piece_of(i, group):
        n, start, size = pieces[i]
        first = group * (wholes[n].shape[0] // GROUPS) + start
        return wholes[n].at[pl.ds(pl.multiple_of(first, 16), size), :]

    def share_of(i):
        n, start, size = pieces[i]
        return shares[n].at[pl.ds(start, size), :]

    def along(i, k):
        return remote(
            share_of(i), piece_of(i, at.mine),
            gather_send.at[i, k], gather_arrive.at[i, at.mine], at.along(k),
        )

    def own(i):
        return pltpu.make_async_copy(
            share_of(i), piece_of(i, at.mine), gather_arrive.at[i, at.mine]
        )

    def relay(i, slot, group, to):
        block = piece_of(i, group)
        return remote(block, block, gather_send.at[i, slot], gather_arrive.at[i, group], to)

    def gather_start(i):
        for k in range(2):

            @pl.when(at.is_self(k))
            def _():
                own(i).start()

            @pl.when(jnp.logical_not(at.is_self(k)))
            def _():
                along(i, k).start()

    def gather_started(i):
        for k in range(2):

            @pl.when(jnp.logical_not(at.is_self(k)))
            def _():
                along(i, k).wait_send()

    def gather_relay(i):
        for k in range(2):
            group = 2 * (at.core + 2 * k) + at.y

            @pl.when(at.is_self(k))
            def _():
                own(i).wait()

            @pl.when(jnp.logical_not(at.is_self(k)))
            def _():
                relay(i, 2 + k, group, at.sibling()).wait_recv()

            relay(i, 4 + k, group, at.across()).start()
            relay(i, 2 + k, group, at.sibling()).start()

    def gather_pass(i):
        for k in range(2):
            group = 2 * (at.core + 2 * k) + 1 - at.y
            relay(i, 6 + k, group, at.sibling()).wait_recv()
            relay(i, 6 + k, group, at.sibling()).start()

    def gather_wait(i):
        for k in range(2):
            for row in range(2):
                group = 2 * (1 - at.core + 2 * k) + row
                relay(i, 2 + k, group, at.sibling()).wait_recv()

    def gather_sent(i):
        for k in range(2):
            group = 2 * (at.core + 2 * k) + at.y
            other = 2 * (at.core + 2 * k) + 1 - at.y
            relay(i, 2 + k, group, at.sibling()).wait_send()
            relay(i, 4 + k, group, at.across()).wait_send()
            relay(i, 6 + k, other, at.sibling()).wait_send()

    count = len(pieces)

    def gather_step(i):
        gather_relay(i)
        gather_started(i)
        if i + AHEAD < count:
            gather_start(i + AHEAD)

    swap_start(0)
    gather_start(0)
    swap_start(1)
    for i in range(1, AHEAD):
        gather_start(i)
    gather_step(0)
    swap_wait(0)
    gather_pass(0)
    gather_wait(0)
    for b in range(images_here):
        filled = jnp.concatenate(
            [frow[8 * b : 8 * b + 8, :], jnp.zeros((LANES - 8, patches), F32)], axis=0
        )
        fcol[b * patches : (b + 1) * patches, :] = jnp.transpose(filled)

    block = small_w[...]
    plain = positions(D)
    apart = spread_positions()
    paired = paired_positions()

    def qkv_positions(t):
        return jnp.where(t < 2, paired, plain) + as_float(t) * D

    def take_vector(row):
        vec[row] = expand(block, q, row, plain)

    def take_frequency(t):
        vec[FREQ_ROW + t] = expand(block, q, FREQ_ROW, apart + as_float(t) * (D // 2))

    def take_qkv(t):
        qkv_b[:, span(t * D, D)] = expand(block, 3 * q, 7, qkv_positions(t))

    def take_up(t):
        up_b[:, span(t * D, D)] = expand(block, 4 * q, 10, plain + as_float(t) * D)

    loop(FREQ_ROW, take_vector)
    loop(2, take_frequency)
    loop(3, take_qkv)
    loop(4, take_up)
    vec_g[...] = jnp.zeros_like(vec_g)
    qkv_bg[...] = jnp.zeros_like(qkv_bg)
    up_bg[...] = jnp.zeros_like(up_bg)

    def vector(row):
        return vec[row]

    def vector_at(row, cols):
        return vec[row, :, cols]

    def tables(b):
        rows = span(b * patches, patches)
        facts = fcol[rows, :]
        row_at, col_at = facts[:, 1:2], facts[:, 2:3]
        first = first_half((patches, TILE))

        def piece(t):
            cols = span(t * TILE, TILE)
            angle = row_at * vector_at(FREQ_ROW, cols) + col_at * vector_at(FREQ_COL, cols)
            turns[rows, cols] = jnp.where(first, jnp.cos(angle), jnp.sin(angle))

        loop(D // TILE, piece)

    def ship_start(n, b, source, target):
        rows = span(b * patches, patches)

        @pl.when(at.home)
        def _():
            ship_here(n, b, source, target).start()

        @pl.when(at.away)
        def _():
            ship_away(n, b, source, target).start()

    def ship_here(n, b, source, target):
        rows = span(b * patches, patches)
        return pltpu.make_async_copy(
            source.at[rows, :], target.at[rows, :], ship_arrive.at[n, b]
        )

    def ship_away(n, b, source, target):
        rows = span(b * patches, patches)
        return remote(
            source.at[rows, :], target.at[rows, :],
            ship_send.at[n, b], ship_arrive.at[n, b], at.twin(),
        )

    def ship_wait(n, b, source, target):
        @pl.when(at.home)
        def _():
            ship_here(n, b, source, target).wait()

        @pl.when(at.away)
        def _():
            ship_away(n, b, source, target).wait_recv()
            ship_away(n, b, source, target).wait_send()

    def pipe(n, b, target, role):
        rows = span(b * patches, patches)
        source = shipped if n == 0 else back_shipped
        return remote(
            source.at[rows, :], target.at[rows, :],
            pipe_send.at[n, b], pipe_arrive.at[n, b], at.section(role),
        )

    def chunks(b, body):
        loop(
            patches // CHUNK,
            lambda i: body(span(b * patches + i * CHUNK, CHUNK), span(i * CHUNK, CHUNK)),
            unroll=patches // CHUNK,
        )

    def own_lanes(e):
        inside = jnp.bitwise_and(lanes_of((patches, 2 * HD)), HD - 1) < HD // 2
        return inside if e == 0 else jnp.logical_not(inside)

    def value_lanes(e):
        inside = lanes_of((patches, 2 * HD)) < HD
        return inside if e == 0 else jnp.logical_not(inside)

    def rows_at(b):
        return span(b * patches, patches)

    def attention_inputs(b):
        rows = rows_at(b)

        def norm_one(here, inside):
            hat, _ = normalise(xin[here, :].astype(F32))
            shipped[here, :] = (hat * vector(GAIN_ONE) + vector(SHIFT_ONE)).astype(LOW)

        chunks(b, norm_one)

        def turn(t):
            cols = span(t * D, D)
            raw = dot(shipped[rows, :], qkv_w[:, cols]) + qkv_b[:, cols]
            cosine, sine = unfold_turn(turns[rows, :])
            turned = raw * cosine + partner(raw) * sine
            qkv[rows, cols] = turned.astype(LOW)

        loop(2, turn, unroll=2)
        cols = pl.ds(2 * D, D)
        qkv[rows, cols] = (dot(shipped[rows, :], qkv_w[:, cols]) + qkv_b[:, cols]).astype(LOW)

    def attention(b, unroll=H // 2):
        rows = rows_at(b)
        barred = jnp.where(frow[span(b * 8, 8), :][0:1, :] > 0, 0.0, MASKED)

        def heads(pair):
            cols = span(pair * 2 * HD, 2 * HD)
            query = qkv[rows, cols]
            key = qkv[rows, span(D + pair * 2 * HD, 2 * HD)]
            value = qkv[rows, span(2 * D + pair * 2 * HD, 2 * HD)]
            value = jnp.concatenate([value, jnp.ones_like(value)], axis=1)
            found = []
            for e in range(2):
                own_query = jnp.where(own_lanes(e), query, jnp.zeros_like(query))
                scores = dot_nt(own_query, key) * (HD ** (-0.5) * LOG2_E) + barred
                powers = jnp.exp2(scores - jnp.max(scores, axis=1, keepdims=True))
                both = dot(powers.astype(LOW), value)
                share = 1.0 / both[:, 2 * HD :]
                probs[b * H + 2 * pair + e] = (
                    powers * jnp.concatenate([share] * (patches // (2 * HD)), axis=1)
                ).astype(LOW)
                found.append(both[:, : 2 * HD] * share)
            att[rows, cols] = jnp.where(value_lanes(0), found[0], found[1]).astype(LOW)

        loop(H // 2, heads, unroll=unroll)

    def middle(b):
        rows = rows_at(b)
        keep_col = fcol[rows, :][:, 0:1]
        branch = dot(att[rows, :], proj_w[...]) + vector(PROJ_SHIFT)
        mid[rows, :] = xin[rows, :].astype(F32) + keep_col * branch

        def norm_two(here, inside):
            hat, _ = normalise(mid[here, :])
            n2[here, :] = (hat * vector(GAIN_TWO) + vector(SHIFT_TWO)).astype(LOW)

        chunks(b, norm_two)

    def raised(b, pieces_now=1):
        rows = rows_at(b)
        tile = up_w.shape[1] // pieces_now

        def part(t):
            cols = span(t * tile, tile)
            hidden = dot(n2[rows, :], up_w[:, cols]) + up_b[:, cols]
            value, gradient = gelu_pair(hidden)
            act[rows, cols] = value.astype(LOW)
            slope[rows, cols] = gradient.astype(LOW)

        if pieces_now == 1:
            part(0)
        else:
            loop(pieces_now, part)

    def lowered(b):
        rows = rows_at(b)
        keep_col = fcol[rows, :][:, 0:1]
        branch = dot(act[rows, :], down_w[...]) + vector(DOWN_SHIFT)
        shipped[rows, :] = (mid[rows, :] + keep_col * branch).astype(LOW)

    def piece_range(n):
        return [i for i, piece in enumerate(pieces) if piece[0] == n]

    def ready(n):
        for i in piece_range(n):
            gather_wait(i)

    def section_zero(stage_now):
        @pl.when(at.role == 0)
        def _():
            loop(images_here, stage_now)

    ready_qkv = LAG + piece_range(1)[-1]
    slots = {
        1: (None, tables),
        ready_qkv: (1, attention_inputs),
        ready_qkv + 2: (None, lambda b: attention(b, 2)),
        ready_qkv + 4: (2, middle),
        LAG + piece_range(3)[-1]: (3, lambda b: raised(b, 4)),
    }
    for i in range(1, count + LAG):
        if i < count:
            gather_step(i)
        if 1 <= i - LAG:
            gather_pass(i - LAG)
        if i == piece_range(1)[-1]:
            swap_wait(1)
        if i in slots:
            matrix, stage_now = slots[i]
            if matrix is not None:
                ready(matrix)
            if stage_now is tables:
                loop(images_here, tables)
            else:
                section_zero(stage_now)
    swap_start(2)
    ready(4)

    def pass_token():
        pl.semaphore_signal(token, inc=1, device_id=at.sibling(), device_id_type=MESH)

    def send_on(b):
        pipe(0, b, xin, at.role + 1).start()

    @pl.when(at.role == 0)
    def _():
        def lower_and_send(b):
            lowered(b)

            @pl.when(jnp.logical_and(at.core == 0, b == 0))
            def _():
                send_on(b)

        loop(images_here, lower_and_send)
        for b in range(images_here):

            @pl.when(at.core == 0)
            def _():
                if b > 0:
                    pl.semaphore_wait(token, 1)
                    send_on(b)
                pipe(0, b, xin, at.role + 1).wait_send()
                pass_token()

            @pl.when(at.core == 1)
            def _():
                pl.semaphore_wait(token, 1)
                send_on(b)
                pipe(0, b, xin, at.role + 1).wait_send()
                if b < images_here - 1:
                    pass_token()

    @pl.when(at.role > 0)
    def _():
        def forward(b):
            pipe(0, b, xin, at.role - 1).wait_recv()
            for stage_now in (attention_inputs, attention, middle, raised, lowered):
                stage_now(b)

            @pl.when(at.role < last)
            def _():
                send_on(b)

        loop(images_here, forward)
        for b in range(images_here):

            @pl.when(at.role < last)
            def _():
                pipe(0, b, xin, at.role + 1).wait_send()

    for b in range(images_here):
        ship_start(0, b, shipped, result_out)
    swap_wait(2)
    for n in range(3):
        swap_sent(n)
    for i in range(count):
        gather_sent(i)

    def norm_back(values, gain_row, grad):
        hat, scale = normalise(values)
        vec_g[gain_row] += jnp.sum(grad * hat, axis=0, keepdims=True)
        vec_g[gain_row + 1] += jnp.sum(grad, axis=0, keepdims=True)
        inner = grad * vector(gain_row)
        along_hat = jnp.mean(inner * hat, axis=-1, keepdims=True)
        level = jnp.mean(inner, axis=-1, keepdims=True)
        return scale * (inner - level - hat * along_hat), hat

    def add_row(ref, cols, values):
        ref[:, cols] += jnp.sum(values.astype(F32), axis=0, keepdims=True)

    def hidden_back(b):
        rows = rows_at(b)

        def mask_coming(here, inside):
            coming = gin[here, :].astype(F32)
            gcopy[inside, :] = gin[here, :]
            grad_two = (coming * fcol[here, :][:, 0:1]).astype(LOW)
            gin[here, :] = grad_two
            vec_g[DOWN_SHIFT] += jnp.sum(grad_two.astype(F32), axis=0, keepdims=True)

        chunks(b, mask_coming)
        grad = dot_nt(gin[rows, :], down_w[...])
        low = (grad * slope[rows, :].astype(F32)).astype(LOW)
        slope[rows, :] = low
        up_bg[...] += jnp.sum(low.astype(F32), axis=0, keepdims=True)
        wide[...] = dot_nt(slope[rows, :], up_w[...])

    def middle_back(b):
        rows = rows_at(b)

        def norm_two_back(here, inside):
            part, _ = norm_back(mid[here, :], GAIN_TWO, wide[inside, :])
            grad_mid = gcopy[inside, :].astype(F32) + part
            mid[here, :] = grad_mid
            grad_one = (grad_mid * fcol[here, :][:, 0:1]).astype(LOW)
            g1[here, :] = grad_one
            vec_g[PROJ_SHIFT] += jnp.sum(grad_one.astype(F32), axis=0, keepdims=True)

        chunks(b, norm_two_back)
        gat[...] = dot_nt(g1[rows, :], proj_w[...]).astype(LOW)

    def attention_back(b):
        rows = rows_at(b)
        facts = fcol[rows, :]
        row_at, col_at = facts[:, 1:2], facts[:, 2:3]
        lane_from = lax.broadcasted_iota(jnp.int32, (4 * HD, 4 * HD), 0)
        lane_to = lax.broadcasted_iota(jnp.int32, (4 * HD, 4 * HD), 1)
        same = lax.rem(lax.div(lane_from, HD), 2) == lax.div(lane_to, 2 * HD)
        head_sums = jnp.where(same, 1.0, 0.0).astype(LOW)

        def heads(pair):
            cols = span(pair * 2 * HD, 2 * HD)
            key_cols = span(D + pair * 2 * HD, 2 * HD)
            value_cols = span(2 * D + pair * 2 * HD, 2 * HD)
            query, key, value = qkv[rows, cols], qkv[rows, key_cols], qkv[rows, value_cols]
            grad = gat[:, cols]
            product = grad.astype(F32) * att[rows, cols].astype(F32)
            high = product.astype(LOW)
            rest = (product - high.astype(F32)).astype(LOW)
            centres = dot(jnp.concatenate([high, rest], axis=1), head_sums)
            to_q, to_k, to_v = [], [], []
            for e in range(2):
                own_grad = jnp.where(value_lanes(e), grad, jnp.zeros_like(grad))
                soft_low = probs[b * H + 2 * pair + e]
                soft = soft_low.astype(F32)
                grad_soft = dot_nt(own_grad, value)
                centre = centres[:, e * 2 * HD : (e + 1) * 2 * HD]
                centre = jnp.concatenate([centre] * (patches // (2 * HD)), axis=1)
                grad_scores = (soft * (grad_soft - centre)).astype(LOW)
                to_q.append(dot(grad_scores, key))
                to_k.append(dot_tn(grad_scores, query))
                to_v.append(dot_tn(soft_low, grad))
            scale = HD ** (-0.5)
            turned_q = jnp.where(own_lanes(0), to_q[0], to_q[1]) * scale
            turned_k = jnp.where(own_lanes(0), to_k[0], to_k[1]) * scale
            grad_v = jnp.where(value_lanes(0), to_v[0], to_v[1]).astype(LOW)
            cosine, sine = unfold_turn(turns[rows, cols])
            other_q, other_k = partner(turned_q), partner(turned_k)
            sign = jnp.where(first_half((1, 2 * HD)), 1.0, -1.0)
            swing = sign * (other_q * query.astype(F32) + other_k * key.astype(F32))
            for n, place_at in enumerate((row_at, col_at)):
                vec_g[FREQ_ROW + n, :, cols] += jnp.sum(swing * place_at, axis=0, keepdims=True)
            grad_q = (turned_q * cosine - other_q * sine).astype(LOW)
            grad_k = (turned_k * cosine - other_k * sine).astype(LOW)
            for where, low in ((cols, grad_q), (key_cols, grad_k), (value_cols, grad_v)):
                qkv[rows, where] = low
                add_row(qkv_bg, where, low)

        loop(H // 2, heads, unroll=H // 2)

    def source_back(b):
        rows = rows_at(b)
        wide[...] = dot_nt(qkv[rows, :], qkv_w[...])

        def norm_one_back(here, inside):
            part, hat = norm_back(xin[here, :].astype(F32), GAIN_ONE, wide[inside, :])
            xin[here, :] = (hat * vector(GAIN_ONE) + vector(SHIFT_ONE)).astype(LOW)
            back_shipped[here, :] = (mid[here, :] + part).astype(LOW)

        chunks(b, norm_one_back)

        @pl.when(at.role > 0)
        def _():
            pipe(1, b, gin, at.role - 1).start()

        @pl.when(at.role == 0)
        def _():
            ship_start(1, b, back_shipped, grad_out_ref)

    def backward_wait(b):
        @pl.when(at.role < last)
        def _():
            pipe(1, b, gin, at.role + 1).wait_recv()

    parts = reduce_pieces([partial.shape[0] // GROUPS for partial in partials])

    def to_sibling(n, slot):
        k, other = slot % 2, slot < 2
        group = 2 * (1 - at.core + 2 * k) + (1 - at.y if other else at.y)
        return remote(
            block_of(partials[n], group), firsts[n].at[slot],
            near_send.at[n, slot], near_arrive.at[n, slot], at.sibling(),
        )

    def held(slot):
        k, other = slot % 2, slot < 2
        return 2 * (at.core + 2 * k) + (1 - at.y if other else at.y)

    def held_part(p, slot):
        n, start, size = parts[p]
        first = held(slot) * (partials[n].shape[0] // GROUPS) + start
        return partials[n].at[pl.ds(pl.multiple_of(first, 16), size), :]

    def to_across(p, k):
        n, start, size = parts[p]
        return remote(
            held_part(p, k), seconds[n].at[k, pl.ds(start, size), :],
            across_send.at[p, k], across_arrive.at[p, k], at.across(),
        )

    def landing(p, half):
        n, start, size = parts[p]
        return totals[n].at[half, pl.ds(start, size), :]

    def to_owner(p, k):
        return remote(
            held_part(p, 2 + k), landing(p, at.half),
            along_send.at[p, k], along_arrive.at[p, at.half], at.along(k),
        )

    def to_self(p, k):
        return pltpu.make_async_copy(
            held_part(p, 2 + k), landing(p, k), along_arrive.at[p, k]
        )

    def from_other(p, k):
        return remote(
            held_part(p, 2 + k), landing(p, k),
            along_send.at[p, k], along_arrive.at[p, k], at.along(k),
        )

    def add(p, slot, source, index):
        n, start, size = parts[p]
        ref = partials[n]
        base = held(slot) * (ref.shape[0] // GROUPS) + start
        step = 16

        def body(i):
            here = pl.ds(pl.multiple_of(base + i * step, step), step)
            there = pl.ds(pl.multiple_of(start + i * step, step), step)
            total = ref[here, :].astype(F32) + source[index, there, :].astype(F32)
            ref[here, :] = total.astype(ref.dtype)

        loop(size // step, body)

    def reduce_start(n):
        for slot in range(4):
            to_sibling(n, slot).start()

    def reduce_across(p):
        n, start, size = parts[p]
        if start == 0:
            for slot in range(4):
                to_sibling(n, slot).wait_recv()
        for slot in range(2):
            add(p, slot, firsts[n], slot)
        for k in range(2):
            if p >= WINDOW:
                to_across(p - WINDOW, k).wait_send()
            to_across(p, k).start()
        for slot in range(2, 4):
            add(p, slot, firsts[n], slot)

    def reduce_along(p):
        n, start, size = parts[p]
        for k in range(2):
            to_across(p, k).wait_recv()
            add(p, 2 + k, seconds[n], k)

            @pl.when(jnp.logical_not(at.is_self(k)))
            def _():
                to_owner(p, k).start()

            @pl.when(at.is_self(k))
            def _():
                to_self(p, k).start()

    def down_grad(width):
        def tile(t):
            cols = span(t * width, width)
            down_w[cols, :] = dot_tn(act[:, cols], gin[...]).astype(LOW)

        loop(down_w.shape[0] // width, tile)
        reduce_start(4)

    def up_grad(width):
        def tile(t):
            cols = span(t * width, width)
            up_w[:, cols] = dot_tn(n2[...], slope[:, cols]).astype(LOW)

        loop(up_w.shape[1] // width, tile)
        reduce_start(3)

    def proj_grad():
        proj_w[...] = dot_tn(att[...], g1[...]).astype(LOW)
        reduce_start(2)

    def qkv_grad():
        for block_no in range(2 * H // 2):
            cols = slice(block_no * 2 * HD, (block_no + 1) * 2 * HD)
            qkv[:, cols] = dot_nt(qkv[:, cols], pairing()).astype(LOW)

        def tile(t):
            cols = span(t * D, D)
            qkv_w[:, cols] = dot_tn(xin[...], qkv[:, cols]).astype(LOW)

        loop(qkv_w.shape[1] // D, tile)
        reduce_start(1)

    def vector_grads():
        small_f[...] = jnp.zeros_like(small_f)

        def give_vector(row):
            small_f[...] += fold(vec_g[row], q, row, plain)

        def give_frequency(t):
            small_f[...] += fold(vec_g[FREQ_ROW + t], q, FREQ_ROW, apart + as_float(t) * (D // 2))

        def give_qkv(t):
            small_f[...] += fold(qkv_bg[:, span(t * D, D)], 3 * q, 7, qkv_positions(t))

        def give_up(t):
            small_f[...] += fold(up_bg[:, span(t * D, D)], 4 * q, 10, plain + as_float(t) * D)

        loop(FREQ_ROW, give_vector)
        loop(2, give_frequency)
        loop(3, give_qkv)
        loop(4, give_up)
        reduce_start(0)

    def early_grads(width):
        down_grad(width)
        reduce_across(0)
        up_grad(width)
        for p in range(1, WINDOW):
            reduce_across(p)

    def backward(b):
        backward_wait(b)
        hidden_back(b)

        @pl.when(jnp.logical_and(at.role == 0, b == images_here - 1))
        def _():
            early_grads(GRAD_TILE)

        middle_back(b)
        attention_back(b)
        source_back(b)

    loop(images_here, backward)

    @pl.when(at.role > 0)
    def _():
        early_grads(GRAD_TILE)

    qkv_grad()
    reduce_across(WINDOW)
    proj_grad()
    vector_grads()
    for b in range(images_here):

        @pl.when(at.role > 0)
        def _():
            pipe(1, b, gin, at.role - 1).wait_send()
            ship_start(1, b, back_shipped, grad_out_ref)

    for p in range(len(parts)):
        if p + WINDOW + 1 < len(parts):
            reduce_across(p + WINDOW + 1)
        reduce_along(p)

    for b in range(images_here):
        ship_wait(0, b, shipped, result_out)
        ship_wait(1, b, back_shipped, grad_out_ref)
    for n in range(5):
        for slot in range(4):
            to_sibling(n, slot).wait_send()
    for p in range(len(parts)):
        for k in range(2):
            if p >= len(parts) - WINDOW:
                to_across(p, k).wait_send()

            @pl.when(jnp.logical_not(at.is_self(k)))
            def _():
                to_owner(p, k).wait_send()
                from_other(p, k).wait_recv()

            @pl.when(at.is_self(k))
            def _():
                to_self(p, k).wait()


def run_block(replicas, sections, matrices, images, cotangent, counts, indices, vectors):
    images_here, patches = images.shape[:2]
    rows = images_here * patches
    hidden = matrices[2].shape[1]
    anywhere = pl.BlockSpec(memory_space=pl.ANY)
    vmem, dma = pltpu.VMEM, pltpu.SemaphoreType.DMA
    inside = pl.BlockSpec(memory_space=vmem)
    flat = [value.reshape(rows, D) for value in (images, cotangent)]
    shapes = [(SMALL_ROWS, LANES)] + [matrix.shape for matrix in matrices]
    kinds = [F32] + [LOW] * 4
    outs = [jax.ShapeDtypeStruct((rows, D), LOW)] * 2
    outs += [jax.ShapeDtypeStruct((2, *shape), kind) for shape, kind in zip(shapes, kinds)]

    reduce_count = sum(parts for _, parts in REDUCE_PARTS)

    def buffers(slots):
        return [vmem((slots, *shape), kind) for shape, kind in zip(shapes, kinds)]

    scratch = [vmem((GROUPS * shape[0], shape[1]), LOW) for shape in shapes]
    scratch += buffers(4) + buffers(2)
    scratch += [
        vmem((rows, D), LOW),
        vmem((rows, D), LOW),
        vmem((patches, D), LOW),
        vmem((rows, LANES), F32),
        vmem((images_here * 8, patches), F32),
        vmem((rows, 3 * D), LOW),
        vmem((images_here * H, patches, patches), LOW),
        vmem((rows, D), LOW),
        vmem((rows, D), F32),
        vmem((rows, D), LOW),
        vmem((rows, hidden), LOW),
        vmem((rows, hidden), LOW),
        vmem((rows, D), LOW),
        vmem((patches, D), F32),
        vmem((rows, D), LOW),
        vmem((rows, D), LOW),
        vmem((patches, D), LOW),
        vmem((rows, D), F32),
        vmem((8, 1, D), F32),
        vmem((1, 3 * D), F32),
        vmem((1, hidden), F32),
        vmem((8, 1, D), F32),
        vmem((1, 3 * D), F32),
        vmem((1, hidden), F32),
        vmem((GROUPS * SMALL_ROWS, LANES), F32),
        vmem(matrices[0].shape, LOW),
        vmem((SMALL_ROWS, LANES), LOW),
        vmem((images_here * 8, patches), F32),
        dma((sum(GATHER_PARTS), 8)),
        dma((sum(GATHER_PARTS), GROUPS)),
        dma((5, 4)),
        dma((5, 4)),
        dma((reduce_count, 2)),
        dma((reduce_count, 2)),
        dma((reduce_count, 2)),
        dma((reduce_count, 2)),
        dma((3,)),
        dma((3,)),
        dma((2, images_here)),
        dma((2, images_here)),
        dma((2, images_here)),
        dma((2, images_here)),
        dma,
        pltpu.SemaphoreType.REGULAR,
    ]
    results = pl.pallas_call(
        functools.partial(block_kernel, replicas, sections, images_here, patches),
        out_shape=outs,
        in_specs=[anywhere] * 6
        + [pl.BlockSpec(memory_space=pltpu.SMEM), inside]
        + [inside] * len(vectors),
        out_specs=[anywhere] * 7,
        scratch_shapes=scratch,
        compiler_params=pltpu.CompilerParams(
            collective_id=0, has_side_effects=True, vmem_limit_bytes=63 * 1024 * 1024
        ),
        name="block",
    )(*matrices, *flat, counts, indices, *vectors)
    finished = finish(results, [vector.shape[1] for vector in vectors])
    outputs, input_grads = (value.reshape(images.shape) for value in finished[:2])
    return outputs, input_grads, finished[2:6], finished[6:]


def finish_kernel(sizes, *refs):
    result, grad, small, *pairs = refs[:7]
    result_out, grad_out, *outs = refs[7:]
    result_out[...] = result[...].astype(F32)
    grad_out[...] = grad[...].astype(F32)
    for pair, out in zip(pairs, outs[:4]):
        out[...] = pair[0].astype(F32) + pair[1].astype(F32)

    @pl.when(pl.program_id(0) == 0)
    def _():
        row = 0
        for size, out in zip(sizes, outs[4:]):
            for start in range(0, size, LANES):
                width = min(LANES, size - start)
                out[:, start : start + width] = (
                    small[0, row : row + 1, 0:width] + small[1, row : row + 1, 0:width]
                )
                row += 1


def finish(values, sizes):
    steps = FINISH_STEPS
    rows = values[0].shape[0]
    whole = pl.BlockSpec((rows // steps, D), lambda i: (i, 0))
    ins, outs, shapes = [whole] * 2, [whole] * 2, [(rows, D)] * 2
    ins.append(pl.BlockSpec(values[2].shape, lambda i: (0, 0, 0)))
    for pair in values[3:]:
        _, size, width = pair.shape
        ins.append(pl.BlockSpec((2, size // steps, width), lambda i: (0, i, 0)))
        outs.append(pl.BlockSpec((size // steps, width), lambda i: (i, 0)))
        shapes.append((size, width))
    for size in sizes:
        outs.append(pl.BlockSpec((1, size), lambda i: (0, 0)))
        shapes.append((1, size))
    return pl.pallas_call(
        functools.partial(finish_kernel, sizes),
        grid=(steps,),
        out_shape=[jax.ShapeDtypeStruct(shape, F32) for shape in shapes],
        in_specs=ins,
        out_specs=outs,
        compiler_params=pltpu.CompilerParams(vmem_limit_bytes=63 * 1024 * 1024),
        name="finish",
    )(*values)


def local(images, cotangent, kept_count, kept_index, *weights):
    sections = lax.axis_size("section")
    replicas = lax.axis_size("dp") // GROUPS
    subgroups = [[g * replicas + r for r in range(replicas)] for g in range(GROUPS)]
    if replicas > 1:
        weights = tuple(
            lax.all_gather(value, "dp", axis=1, tiled=True, axis_index_groups=subgroups)
            for value in weights
        )
    matrices = [weights[n][0] for n in MATRICES]
    vectors = [weights[n] for n in VECTORS]
    outputs, input_grads, sums, vector_sums = run_block(
        replicas, sections, matrices, images, cotangent, kept_count, kept_index, vectors
    )
    grads = [None] * len(weights)
    for n, value in zip(MATRICES, sums):
        grads[n] = value
    for n, vector in zip(VECTORS, vector_sums):
        grads[n] = vector[0]
    if replicas > 1:
        grads = [
            lax.psum_scatter(
                value, "dp", scatter_dimension=0, tiled=True, axis_index_groups=subgroups
            )
            for value in grads
        ]
    return (outputs[None], input_grads[None], *(value[None] for value in grads))


def solution(mesh):
    in_specs = (
        P("dp", None, None),
        P("dp", None, None),
        P("dp"),
        P("dp", None),
        P("section", "dp"),
        P("section", "dp"),
        P("section", "dp", None),
        P("section", "dp"),
        P("section", "dp", None),
        P("section", "dp"),
        P("section", "dp"),
        P("section", "dp"),
        P("section", "dp", None),
        P("section", "dp"),
        P("section", "dp", None),
        P("section", "dp"),
        P("section", "dp"),
    )
    out_specs = (
        P("section", "dp", None, None),
        P("section", "dp", None, None),
        P("section", "dp"),
        P("section", "dp"),
        P("section", "dp", None),
        P("section", "dp"),
        P("section", "dp", None),
        P("section", "dp"),
        P("section", "dp"),
        P("section", "dp"),
        P("section", "dp", None),
        P("section", "dp"),
        P("section", "dp", None),
        P("section", "dp"),
        P("section", "dp"),
    )
    return jax.shard_map(local, mesh=mesh, in_specs=in_specs, out_specs=out_specs, check_vma=False)
```
